32 devices in a mesh: wide: 8 (over z, y), narrow: 4 (over x, core).
Axes of the slice: x: 2, y: 2, z: 4, core: 2. Of those that a mesh axis runs over, the one named last changes fastest.
Arguments:
- token_ids: int32 [32, 512], P(('wide', 'narrow')), may hold values from 0 to 30719
- live_lengths: int32 [32], P(('wide', 'narrow')), may hold values from 0 to 512, as said below
- key_keep: int32 [32, 512], P(('wide', 'narrow')), may hold values 0 or 1
- buckets: int32 [32, 512], P(('wide', 'narrow')), may hold values from 0 to 3
- mask_pos: int32 [32, 80], P(('wide', 'narrow')), may hold values from 0 to 511, as said below
- mask_labels: int32 [32, 80], P(('wide', 'narrow')), may hold values from 0 to 30719
- mask_counts: int32 [32], P(('wide', 'narrow')), may hold values from 0 to 80, as said below
- source_logits: bfloat16 [32, 80, 30720], P(('wide', 'narrow')), may hold values from -12 to 12
- embed_table: float32 [31744, 1024], P(('wide', 'narrow')), may hold values from -0.6 to 0.6
- embed_first: float32 [31744, 1024], P(('wide', 'narrow')), may hold values from -6e-05 to 6e-05
- embed_second: float32 [31744, 1024], P(('wide', 'narrow')), may hold values from 1e-12 to 1e-10
- attn_mats: float32 [4, 1024, 1024], P('narrow', None, 'wide')
- attn_moment: float32 [4, 1024, 1024], P('narrow', None, 'wide'), may hold values from -0.0006 to 0.0006
- ffn_mats: float32 [2, 1024, 4096], P(None, None, ('wide', 'narrow')), may hold values from -0.1875 to 0.1875
- ffn_moment: float32 [2, 1024, 4096], P(None, None, ('wide', 'narrow')), may hold values from -0.0006 to 0.0006
- other_params: float32 [1096704], P(('wide', 'narrow'))
- other_first: float32 [1096704], P(('wide', 'narrow')), may hold values from -6e-05 to 6e-05
- other_second: float32 [1096704], P(('wide', 'narrow')), may hold values from 1e-12 to 1e-10
Outputs:
- loss_value: float32 [], replicated
- grad_norm: float32 [], replicated
- embed_new: float32 [31744, 1024], P(('wide', 'narrow'))
- embed_first_new: float32 [31744, 1024], P(('wide', 'narrow'))
- embed_second_new: float32 [31744, 1024], P(('wide', 'narrow'))
- attn_new: float32 [4, 1024, 1024], P('narrow', None, 'wide')
- attn_moment_new: float32 [4, 1024, 1024], P('narrow', None, 'wide')
- ffn_new: float32 [2, 1024, 4096], P(None, None, ('wide', 'narrow'))
- ffn_moment_new: float32 [2, 1024, 4096], P(None, None, ('wide', 'narrow'))
- other_new: float32 [1096704], P(('wide', 'narrow'))
- other_first_new: float32 [1096704], P(('wide', 'narrow'))
- other_second_new: float32 [1096704], P(('wide', 'narrow'))
The draws below stay inside these ranges and needn't reach their ends.
Inputs may be any that keep to these rules, and one draw needn't show every extreme that they name: `live_lengths`: A window's live slots come first. Even rows (first windows of sequences) have 512 live slots; window 3 has none. mask_counts = live_lengths * 5 // 32 for each window. `mask_pos`: in each window the first mask_counts entries are distinct live positions of the window; the others hold 0.
All inputs are finite; a program needn't handle non-finite values. No bound on the sum of `key_keep` on one device may be relied on, other than what follows from the above.
Results may differ from the reference program's by a relative error of at most 0.0025.
The reference program's roundings to bfloat16 on the way count: a program that leaves them out, or rounds other values in their place, can miss the bound.
Values may be sent and summed in bfloat16 or wider, within the bound.
No kernel may reach another device: no remote copies, remote signals or barrier semaphores. Data moves between devices by JAX's collectives and lax.ppermute only.
A program may use at most 576 MiB of HBM per device.

```python
import math
import jax
import jax.numpy as jnp
import numpy as np
from jax import lax

D = 1024
FF = 4096
HEADS = 16
L = 1
V = 30720
SEQ = 1024
WINDOW = 512
NBUCKET = 4
NS_ITERS = 3
ADAM_STEP = 5
NWIN = 32
MPW = 80
NV = 13
P_SIZE = 1096704


def draw_layout(key):
    base = jax.random.fold_in(key, 11)
    first_key, second_key = jax.random.split(base)
    seq_count = NWIN // 2
    seq_len = jax.random.randint(first_key, (seq_count,), SEQ // 2, SEQ + 1).astype(jnp.int32)
    seq_len = seq_len.at[0].set(SEQ)
    seq_len = seq_len.at[1].set(SEQ // 2)
    first_live = jnp.clip(seq_len, 0, WINDOW)
    second_live = jnp.clip(seq_len - WINDOW, 0, WINDOW)
    lives = jnp.stack([first_live, second_live], axis=1).reshape(NWIN).astype(jnp.int32)
    counts = lives * 5 // 32
    noise = jax.random.randint(second_key, (NWIN, WINDOW), 1, 2 ** 19).astype(jnp.int32)
    places = jnp.arange(WINDOW, dtype=jnp.int32)
    scores = noise * WINDOW + places[None, :]
    scores = jnp.where(places[None, :] < lives[:, None], scores, scores + 2 ** 30)
    scores = scores.at[0, WINDOW - 1].set(0)
    order = jnp.argsort(scores, axis=1, stable=True)[:, :MPW].astype(jnp.int32)
    slots = jnp.arange(MPW, dtype=jnp.int32)
    chosen = jnp.where(slots[None, :] < counts[:, None], order, 0)
    return (lives, counts, chosen)


def draw_live_lengths(key, part):
    return draw_layout(key)[0]


def draw_mask_counts(key, part):
    return draw_layout(key)[1]


def draw_mask_pos(key, part):
    return draw_layout(key)[2]


def draw_attn_mats(key, part):
    noise = jax.random.normal(jax.random.fold_in(key, 3), (4 * L, D, D), jnp.float32)
    boost = jnp.where(jnp.arange(4 * L) >= 3 * L, 6.0, 1.0)
    return noise * D ** (-0.5) * boost[:, None, None]


def draw_other_params(key, part):
    noise = jnp.clip(jax.random.normal(jax.random.fold_in(key, 5), (P_SIZE,), jnp.float32), -4.0, 4.0)
    index = jnp.arange(P_SIZE, dtype=jnp.int32)
    offset = V + L * FF
    row_id = (index - offset) // D
    in_vectors = (index >= offset) & (index < offset + NV * D)
    inner = (row_id - 2) % 8
    is_gain = in_vectors & ((row_id == 0) | (row_id == NV - 2) | (row_id >= 2) & (row_id < NV - 3) & ((inner == 0) | (inner == 2)))
    scale = jnp.where(index < V, 0.5, 0.3)
    scale = jnp.where(is_gain, 0.1, scale)
    scale = jnp.where(index >= offset + NV * D, D ** (-0.5), scale)
    shift = jnp.where(is_gain, 1.0, 0.0)
    return noise * scale + shift


def set_ends(values, own_key, smallest, high):
    dims = values.shape
    place = [jax.random.randint(jax.random.fold_in(own_key, axis), (), 0, dims[axis]) for axis in range(len(dims))]
    values = values.at[tuple(place)].set(smallest)
    longest = dims.index(max(dims))
    place[longest] = (place[longest] + 1) % dims[longest]
    return values.at[tuple(place)].set(high)


def block_levels(own_key, shape, cuts, smallest, high):
    def one(position, blocks):
        draws = jax.random.uniform(jax.random.fold_in(jax.random.fold_in(own_key, 6), position), (blocks,), jnp.float32, smallest / len(cuts), high / len(cuts))
        return jnp.repeat(jnp.exp(draws), shape[position] // blocks).reshape((-1,) + (1,) * (len(shape) - position - 1))

    level = one(*cuts[0])
    for cut in cuts[1:]:
        level = level * one(*cut)
    return level


def cumulative_ranks(count, slope):
    weights = [(1 << 20) // math.isqrt(grade ** slope) + 1 for grade in range(1, count + 1)]
    deviation = 1 + sum(weights) // (1 << 30)
    return np.cumsum(np.array([max(1, weight // deviation) for weight in weights]))


def skewed_ids(stream_key, shape, count, skew):
    table = cumulative_ranks(count, skew)
    pick = jax.random.randint(jax.random.fold_in(stream_key, 1), shape, 0, int(table[count - 1]))
    standing = jnp.searchsorted(jnp.asarray(table, jnp.int32), pick, side="right")
    return jax.random.permutation(jax.random.fold_in(stream_key, 2), count)[standing].astype(jnp.int32)


def centred(own_key, dims, scale, reach, cuts=(), kind=jnp.bfloat16):
    drawn = scale * jax.random.normal(own_key, dims, jnp.float32)
    if cuts:
        drawn = drawn * block_levels(own_key, dims, cuts, -0.22, 0.18)
    return jnp.clip(drawn, -reach, reach).astype(kind)


def setup_inputs(seed: int = 0) -> dict:
    seeds = jax.random.split(jax.random.key(seed), 19)
    token_ids = set_ends(skewed_ids(seeds[0], (NWIN, WINDOW), V, 2), jax.random.fold_in(seeds[0], 3), 0, V - 1).astype(jnp.int32)
    live_lengths = draw_live_lengths(jax.random.fold_in(seeds[18], 71), 0)
    key_keep = set_ends((jax.random.randint(seeds[2], (NWIN, WINDOW), 0, 8) < 7).astype(jnp.int32), jax.random.fold_in(seeds[2], 1), 0, 1)
    buckets = set_ends(jax.random.randint(seeds[3], (NWIN, WINDOW), 0, NBUCKET), jax.random.fold_in(seeds[3], 1), 0, NBUCKET - 1).astype(jnp.int32)
    mask_pos = draw_mask_pos(jax.random.fold_in(seeds[18], 71), 0)
    mask_labels = set_ends(jax.random.randint(seeds[5], (NWIN, MPW), 0, V), jax.random.fold_in(seeds[5], 1), 0, V - 1).astype(jnp.int32)
    mask_counts = draw_mask_counts(jax.random.fold_in(seeds[18], 71), 0)
    source_logits = centred(seeds[7], (NWIN, MPW, V), 2.0, 12.0, ((0, 32),))
    embed_table = centred(seeds[8], (V + SEQ, D), 0.1, 0.6, ((0, 32),), jnp.float32)
    embed_first = centred(seeds[9], (V + SEQ, D), 0.00001, 5.999999848427251e-05, ((0, 32),), jnp.float32)
    embed_second = jnp.clip(jnp.exp(math.log(1.000000013351432e-10) - 4.6051702 * jax.random.uniform(seeds[10], (V + SEQ, D), jnp.float32) ** block_levels(seeds[10], (V + SEQ, D), ((0, 32),), -0.2, 0.2)), 9.999999960041972e-13, 1.000000013351432e-10)
    attn_mats = draw_attn_mats(jax.random.fold_in(seeds[18], 71), 0)
    attn_moment = centred(seeds[12], (4 * L, D, D), 0.0001, 0.0006, ((0, 4), (2, 8)), jnp.float32)
    ffn_mats = centred(seeds[13], (2 * L, D, FF), D ** -0.5, 0.1875, ((2, 32),), jnp.float32)
    ffn_moment = centred(seeds[14], (2 * L, D, FF), 0.0001, 0.0006, ((2, 32),), jnp.float32)
    other_params = draw_other_params(jax.random.fold_in(seeds[18], 71), 0)
    other_first = centred(seeds[16], (P_SIZE,), 0.00001, 5.999999848427251e-05, ((0, 32),), jnp.float32)
    other_second = jnp.clip(jnp.exp(math.log(1.000000013351432e-10) - 4.6051702 * jax.random.uniform(seeds[17], (P_SIZE,), jnp.float32) ** block_levels(seeds[17], (P_SIZE,), ((0, 32),), -0.2, 0.2)), 9.999999960041972e-13, 1.000000013351432e-10)
    return {"token_ids": token_ids, "live_lengths": live_lengths, "key_keep": key_keep, "buckets": buckets, "mask_pos": mask_pos, "mask_labels": mask_labels, "mask_counts": mask_counts, "source_logits": source_logits, "embed_table": embed_table, "embed_first": embed_first, "embed_second": embed_second, "attn_mats": attn_mats, "attn_moment": attn_moment, "ffn_mats": ffn_mats, "ffn_moment": ffn_moment, "other_params": other_params, "other_first": other_first, "other_second": other_second}


@jax.custom_vjp
def low(v):
    return lax.optimization_barrier(v.astype(jnp.bfloat16)).astype(jnp.float32)

@jax.custom_vjp
def low_back(v):
    return v

def low_keep(v):
    return (low(v), None)

def low_pass(kept, grad):
    return (grad,)

def back_keep(v):
    return (v, None)

def back_low(kept, grad):
    return (low(grad),)
low.defvjp(low_keep, low_pass)
low_back.defvjp(back_keep, back_low)
highest = lax.Precision.HIGHEST
ln_eps = 1e-05
masked_fill = -1e+30
clip_limit = 0.3
ns_a = 3.4445
ns_b = -4.775
ns_c = 2.0315
mu_muon = 0.95
lr_muon = 0.1
muon_shape = 0.2
lr_adam = 0.01
beta_one = 0.9
beta_two = 0.999
adam_eps = 1e-08
group_size = 4

def both_round(inputs):
    return low(low_back(inputs))

def layer_norm(inputs, gain_vec, shift_vec):
    center = inputs - lax.optimization_barrier(jnp.mean(inputs, -1, keepdims=True))
    spread = lax.optimization_barrier(jnp.mean(center * center, -1, keepdims=True))
    return center * lax.rsqrt(spread + ln_eps) * gain_vec + shift_vec

def exact_gelu(inputs):
    return jax.nn.gelu(inputs, approximate=False)

def dense(inputs, weight):
    return jnp.einsum('bsd,df->bsf', inputs, weight, precision=highest)

def to_heads(inputs):
    return inputs.reshape(inputs.shape[0], inputs.shape[1] // WINDOW, WINDOW, HEADS, inputs.shape[2] // HEADS)

def split_other(other_flat):
    offset = V + L * FF
    up_biases = other_flat[V:offset].reshape(L, FF)
    vectors = other_flat[offset:offset + NV * D].reshape(NV, D)
    head_weight = other_flat[offset + NV * D:].reshape(D, D)
    return (other_flat[:V], up_biases, vectors, head_weight)

def attention_mask(lengths, keep_mask, bucket_ids):
    count, length = keep_mask.shape
    places = jnp.arange(length, dtype=jnp.int32)
    is_valid = (places[None, :] < lengths[:, None]) & (keep_mask == 1)
    windows = length // WINDOW
    key_ok = is_valid.reshape(count, windows, 1, 1, WINDOW)
    grouped = bucket_ids.reshape(count, windows, WINDOW)
    same_bucket = grouped[:, :, None, :, None] == grouped[:, :, None, None, :]
    return same_bucket & key_ok | jnp.eye(WINDOW, dtype=bool)

def encode_layer(hidden, params, allowed):
    w_query, w_key, w_value, w_out, w_up, w_down, up_bias, vectors = params
    count, length, model_width = hidden.shape
    inputs = low(hidden)
    queries = both_round(dense(inputs, w_query) + vectors[4])
    key_proj = both_round(dense(inputs, w_key))
    values = both_round(dense(inputs, w_value) + vectors[5])
    raw_scores = low_back(jnp.einsum('bnqhe,bnkhe->bnhqk', to_heads(queries), to_heads(key_proj), precision=highest))
    scores = jnp.where(allowed, raw_scores * (model_width // HEADS) ** (-0.5), masked_fill)
    attn_prob = low(jax.nn.softmax(scores, axis=-1))
    context = jnp.einsum('bnhqk,bnkhe->bnqhe', attn_prob, to_heads(values), precision=highest)
    context = both_round(context.reshape(count, length, model_width))
    middle = layer_norm(hidden + low_back(dense(context, w_out) + vectors[6]), vectors[0], vectors[1])
    up_proj = low_back(dense(low(middle), w_up) + up_bias)
    activated = low(exact_gelu(up_proj))
    down_proj = low_back(jnp.einsum('bsf,df->bsd', activated, w_down, precision=highest) + vectors[7])
    return layer_norm(middle + down_proj, vectors[2], vectors[3])

def group_loss(lowered, group_data):
    embed_rows, attn_stack, ffn_stack, other_flat = lowered
    tokens, lengths, keep_mask, bucket_ids, positions, labels, counts, source, offsets = group_data
    dec_bias, up_biases, vectors, head_weight = split_other(other_flat)
    count, length = tokens.shape
    pos_rows = V + offsets[:, None] + jnp.arange(length, dtype=jnp.int32)[None, :]
    embedded = embed_rows[tokens] + embed_rows[pos_rows]
    hidden = layer_norm(embedded, vectors[0], vectors[1])
    allowed = attention_mask(lengths, keep_mask, bucket_ids)
    for layer_idx in range(L):
        params = (attn_stack[layer_idx], attn_stack[L + layer_idx], attn_stack[2 * L + layer_idx], attn_stack[3 * L + layer_idx], ffn_stack[layer_idx], ffn_stack[L + layer_idx], up_biases[layer_idx], vectors[2 + 8 * layer_idx:10 + 8 * layer_idx])
        hidden = encode_layer(hidden, params, allowed)
    flat_hidden = hidden.reshape(count * length, D)
    row_index = (jnp.arange(count, dtype=jnp.int32)[:, None] * length + positions).reshape(-1)
    head_in = low(flat_hidden[row_index])
    head_pre = low_back(jnp.dot(head_in, head_weight, precision=highest) + vectors[NV - 3])
    head_out = low(layer_norm(exact_gelu(head_pre), vectors[NV - 2], vectors[NV - 1]))
    logits = low_back(jnp.einsum('rd,vd->rv', head_out, embed_rows[:V], precision=highest) + dec_bias)
    log_prob = jax.nn.log_softmax(logits, axis=-1)
    source_log = jax.nn.log_softmax(source.reshape(-1, V).astype(jnp.float32), axis=-1)
    picked = jnp.take_along_axis(log_prob, labels.reshape(-1, 1), axis=1)[:, 0]
    diverge = lax.optimization_barrier(jnp.sum(jnp.exp(source_log) * (source_log - log_prob), -1))
    is_live = (jnp.arange(MPW, dtype=jnp.int32)[None, :] < counts[:, None]).reshape(-1).astype(jnp.float32)
    return jnp.sum((diverge - picked) * is_live)

def orthogonal(matrix):
    current = matrix / (jnp.sqrt(jnp.sum(matrix * matrix)) + 1e-07)
    for _ in range(NS_ITERS):
        gram_mat = jnp.dot(current, current.T, precision=highest)
        poly_term = ns_b * gram_mat + ns_c * jnp.dot(gram_mat, gram_mat, precision=highest)
        current = ns_a * current + jnp.dot(poly_term, current, precision=highest)
    return current

def muon_step(master, moment, gradient):
    new_moment = mu_muon * moment + gradient
    row_count, col_count = master.shape[-2:]
    change = lr_muon * muon_shape * math.sqrt(max(row_count, col_count)) * jax.vmap(orthogonal)(new_moment)
    return (master - change, new_moment)

def adam_step(master, first_moment, second, gradient):
    new_first = beta_one * first_moment + (1.0 - beta_one) * gradient
    new_second = beta_two * second + (1.0 - beta_two) * gradient * gradient
    first_hat = new_first / (1.0 - beta_one ** ADAM_STEP)
    second_hat = new_second / (1.0 - beta_two ** ADAM_STEP)
    return (master - lr_adam * first_hat / (jnp.sqrt(second_hat) + adam_eps), new_first, new_second)

def reference(token_ids, live_lengths, key_keep, buckets, mask_pos, mask_labels, mask_counts, source_logits, embed_table, embed_first, embed_second, attn_mats, attn_moment, ffn_mats, ffn_moment, other_params, other_first, other_second):
    masked_total = jnp.sum(mask_counts).astype(jnp.float32)
    offsets = jnp.arange(NWIN, dtype=jnp.int32) % (SEQ // WINDOW) * WINDOW
    grouped = tuple((a.reshape((-1, group_size) + a.shape[1:]) for a in (token_ids, live_lengths, key_keep, buckets, mask_pos, mask_labels, mask_counts, source_logits, offsets)))

    def raw_loss(weights):
        lowered = tuple((low(w) for w in weights))

        def scan_step(running, group_data):
            return (running + jax.checkpoint(group_loss)(lowered, group_data), None)
        running, _ = lax.scan(scan_step, jnp.zeros((), jnp.float32), grouped)
        return running
    weights = (embed_table, attn_mats, ffn_mats, other_params)
    raw_value, pullback = jax.vjp(raw_loss, weights)
    raw_grads, = pullback(jnp.ones((), jnp.float32))
    gradients = [gradient / masked_total for gradient in raw_grads]
    loss_value = raw_value / masked_total
    squares = jnp.zeros((), jnp.float32)
    for gradient in gradients:
        squares = squares + jnp.sum(gradient * gradient)
    grad_norm = jnp.sqrt(squares)
    factor = jnp.minimum(1.0, clip_limit / grad_norm)
    table_grad, attn_grad, ffn_grad, other_grad = [gradient * factor for gradient in gradients]
    embed_new, embed_first_new, embed_second_new = adam_step(embed_table, embed_first, embed_second, table_grad)
    attn_new, attn_moment_new = muon_step(attn_mats, attn_moment, attn_grad)
    ffn_new, ffn_moment_new = muon_step(ffn_mats, ffn_moment, ffn_grad)
    other_new, other_first_new, other_second_new = adam_step(other_params, other_first, other_second, other_grad)
    return (loss_value, grad_norm, embed_new, embed_first_new, embed_second_new, attn_new, attn_moment_new, ffn_new, ffn_moment_new, other_new, other_first_new, other_second_new)
```

```python
import functools
import math

import jax
import jax.numpy as jnp
import numpy as np
from jax import lax
from jax.experimental import pallas as pl
from jax.experimental.pallas import tpu as pltpu
from jax.sharding import Mesh
from jax.sharding import PartitionSpec as P

D = 1024
FF = 4096
HEADS = 16
L = 1
V = 30720
SEQ = 1024
WINDOW = 512
NS_ITERS = 3
ADAM_STEP = 5
MPW = 80
NV = 13


high = lax.Precision.HIGH
lanes = 128
tile = 16
slots = 32
ln_eps = 1e-05
masked_fill = -1e30
clip_limit = 0.3
ns_a = 3.4445
ns_b = -4.775
ns_c = 2.0315
mu_muon = 0.95
lr_muon = 0.1
muon_shape = 0.2
lr_adam = 0.01
beta_one = 0.9
beta_two = 0.999
adam_eps = 1e-08


def layer_norm(inputs, gain_vec, shift_vec):
    center = inputs - jnp.mean(inputs, -1, keepdims=True)
    spread = jnp.mean(center * center, -1, keepdims=True)
    return center * lax.rsqrt(spread + ln_eps) * gain_vec + shift_vec


def exact_gelu(inputs):
    return jax.nn.gelu(inputs, approximate=False)


def head_tail(head_pre, gain_vec, shift_vec):
    return layer_norm(exact_gelu(head_pre), gain_vec, shift_vec)


def project(inputs, weight):
    return jnp.einsum("bsd,df->bsf", inputs, weight, preferred_element_type=jnp.float32)


def project_back(gradients, weight):
    return jnp.einsum("bsf,df->bsd", gradients, weight, preferred_element_type=jnp.float32)


def col_sum(inputs):
    return jnp.sum(inputs.astype(jnp.float32), axis=(0, 1))


def to_heads(inputs):
    return inputs.reshape(
        inputs.shape[0], inputs.shape[1] // WINDOW, WINDOW, HEADS, inputs.shape[2] // HEADS
    )


def attn_scores(queries, key_proj, allowed):
    raw_scores = jnp.einsum(
        "bnqhe,bnkhe->bnhqk",
        to_heads(queries),
        to_heads(key_proj),
        preferred_element_type=jnp.float32,
    )
    return jnp.where(allowed, raw_scores * (queries.shape[2] // HEADS) ** (-0.5), masked_fill)


def share(values, axis):
    return jnp.concatenate([values, exchange(values, side_bit)], axis=axis)


def swap_pick(for_first, for_second, axis):
    first = lax.axis_index("side") == 0
    keep = jnp.where(first, for_first, for_second)
    got = exchange(jnp.where(first, for_second, for_first), side_bit)
    return jnp.concatenate([keep, got], axis=axis)


def share_half(values):
    side = lax.axis_index("side")
    half = values.shape[1] // 2
    keep = lax.dynamic_slice_in_dim(values, side * half, half, axis=1)
    got = exchange(lax.dynamic_slice_in_dim(values, (1 - side) * half, half, axis=1), side_bit)
    return jnp.concatenate([keep, got])


def layer_forward(hidden, params, allowed):
    w_query, w_key, w_value, w_out, w_up, w_down, up_bias, vectors = params
    count, length, model_width = hidden.shape
    inputs = hidden.astype(jnp.bfloat16)
    queries = (project(inputs, w_query) + vectors[4]).astype(jnp.bfloat16)
    key_proj = project(inputs, w_key).astype(jnp.bfloat16)
    values = (project(inputs, w_value) + vectors[5]).astype(jnp.bfloat16)
    scores = attn_scores(queries, key_proj, allowed)
    log_total = jax.nn.logsumexp(scores, axis=-1, keepdims=True)
    prob_low = jnp.exp(scores - log_total).astype(jnp.bfloat16)
    context = jnp.einsum(
        "bnhqk,bnkhe->bnqhe", prob_low, to_heads(values), preferred_element_type=jnp.float32
    )
    context = context.reshape(count, length, model_width).astype(jnp.bfloat16)
    attn_sum = hidden + (project(context, w_out) + vectors[6])
    middle, first_pull = jax.vjp(layer_norm, attn_sum, vectors[0], vectors[1])
    middle_low = middle.astype(jnp.bfloat16)
    up_proj = project(middle_low, w_up) + up_bias
    activated, gelu_pull = jax.vjp(exact_gelu, up_proj)
    act_low = activated.astype(jnp.bfloat16)
    ffn_sum = middle + (project_back(act_low, w_down) + vectors[7])
    output, second_pull = jax.vjp(layer_norm, ffn_sum, vectors[2], vectors[3])
    stored = (
        inputs,
        queries,
        key_proj,
        values,
        log_total,
        context,
        first_pull,
        middle_low,
        gelu_pull,
        act_low,
        second_pull,
    )
    return (output, stored)


def layer_backward(grad_out, stored, params, allowed):
    w_query, w_key, w_value, w_out, w_up, w_down, _, _ = params
    (
        inputs,
        queries,
        key_proj,
        values,
        log_total,
        context,
        first_pull,
        middle_low,
        gelu_pull,
        act_low,
        second_pull,
    ) = stored
    count, length, model_width = grad_out.shape
    grad_ffn, grad_gain_two, grad_shift_two = second_pull(grad_out)
    down_low = grad_ffn.astype(jnp.bfloat16)
    (grad_up,) = gelu_pull(project(down_low, w_down))
    up_low = grad_up.astype(jnp.bfloat16)
    wide_count = lax.axis_size("wide")
    operands = (
        share(middle_low[0].T, 1),
        share(down_low[0].T, 1),
        share_half(up_low[0]),
        share_half(act_low[0]),
    )
    if FF // (4 * wide_count) == lanes:
        grad_mats_ffn = ffn_weight_grads(*operands, wide_count)
    else:
        blocks = jnp.stack([jnp.dot(*operands[::2], preferred_element_type=jnp.float32),
                            jnp.dot(*operands[1::2], preferred_element_type=jnp.float32)])
        blocks = blocks.reshape(2, D, wide_count, 2, -1).transpose(2, 3, 0, 1, 4)
        grad_mats_ffn = in_routes(blocks, wide_count)
    grad_ffn, *grad_mats_ffn = lax.optimization_barrier((grad_ffn, *grad_mats_ffn))
    grad_middle = grad_ffn + project_back(up_low, w_up)
    grad_attn, grad_gain_one, grad_shift_one = first_pull(grad_middle)
    attn_low = grad_attn.astype(jnp.bfloat16)
    grad_context = to_heads(project_back(attn_low, w_out).astype(jnp.bfloat16))
    attn_prob = jnp.exp(attn_scores(queries, key_proj, allowed) - log_total)
    prob_low = attn_prob.astype(jnp.bfloat16)
    grad_prob = jnp.einsum(
        "bnqhe,bnkhe->bnhqk", grad_context, to_heads(values), preferred_element_type=jnp.float32
    )
    grad_value = jnp.einsum(
        "bnhqk,bnqhe->bnkhe", prob_low, grad_context, preferred_element_type=jnp.float32
    )
    grad_value = grad_value.reshape(count, length, model_width).astype(jnp.bfloat16)
    grad_scores = attn_prob * (grad_prob - jnp.sum(grad_prob * attn_prob, -1, keepdims=True))
    grad_raw = (grad_scores * (model_width // HEADS) ** (-0.5)).astype(jnp.bfloat16)
    grad_query = jnp.einsum(
        "bnhqk,bnkhe->bnqhe", grad_raw, to_heads(key_proj), preferred_element_type=jnp.float32
    )
    grad_query = grad_query.reshape(count, length, model_width).astype(jnp.bfloat16)
    grad_key = jnp.einsum(
        "bnhqk,bnqhe->bnkhe", grad_raw, to_heads(queries), preferred_element_type=jnp.float32
    )
    grad_key = grad_key.reshape(count, length, model_width).astype(jnp.bfloat16)
    grad_hidden = (
        grad_attn
        + project_back(grad_query, w_query)
        + project_back(grad_key, w_key)
        + project_back(grad_value, w_value)
    )
    operands = (
        share(inputs[0].T, 1),
        swap_pick(inputs[0].T, context[0].T, 1),
        swap_pick(grad_query[0], grad_key[0], 0),
        swap_pick(grad_value[0], attn_low[0], 0),
    )
    if D // wide_count == lanes:
        grad_mats_attn = attn_weight_grads(*operands, wide_count)
    else:
        blocks = jnp.stack([jnp.dot(*operands[::2], preferred_element_type=jnp.float32),
                            jnp.dot(*operands[1::2], preferred_element_type=jnp.float32)])
        blocks = blocks.reshape(2, 1, D, wide_count, -1).transpose(3, 0, 1, 2, 4)
        grad_mats_attn = in_routes(blocks, wide_count)
    matrices = (grad_mats_attn, grad_mats_ffn)
    vector_grads = jnp.stack(
        [
            grad_gain_one,
            grad_shift_one,
            grad_gain_two,
            grad_shift_two,
            col_sum(grad_query),
            col_sum(grad_value),
            col_sum(attn_low),
            col_sum(down_low),
        ]
    )
    return (grad_hidden, matrices, col_sum(up_low), vector_grads)


def slab_product(matrix, columns):
    return jnp.einsum(
        "kde,kec->kdc", matrix, columns, precision=high, preferred_element_type=jnp.float32
    )


def newton_cols(moment, gram):
    norms = jnp.sqrt(jnp.trace(gram, axis1=1, axis2=2))
    scaling = 1.0 / (norms + 1e-07)
    current = moment * scaling[:, None, None]
    gram = gram * (scaling * scaling)[:, None, None]
    for step_idx in range(NS_ITERS):
        if step_idx + 1 < NS_ITERS:
            poly = ns_b * gram + ns_c * jnp.einsum("kde,kef->kdf", gram, gram)
            current = ns_a * current + slab_product(poly, current)
            half = ns_a * gram + jnp.einsum("kde,kef->kdf", poly, gram)
            gram = ns_a * half + jnp.einsum("kde,kef->kdf", half, poly)
        else:
            once = slab_product(gram, current)
            current = ns_a * current + ns_b * once + ns_c * slab_product(gram, once)
    return current


def gather_columns(columns, with_pair):
    wide_count = lax.axis_size("wide")
    return gather_relative(columns[0].astype(jnp.bfloat16), wide_count, 0, tile, with_pair)


def gram_of(found):
    return jnp.einsum("wdc,wec->de", found, found, preferred_element_type=jnp.float32)[None]


def relative_order(part, taken):
    names = [bit for bit in wide_bits(lax.axis_size("wide"))[::-1] + [("pair", 1)] if bit in taken]
    dims = [names.index(bit) for bit in taken[::-1]]
    split = part.reshape((2,) * len(taken) + part.shape[1:])
    turn = [dims.index(place) for place in range(len(taken))]
    split = split.transpose(turn + list(range(len(taken), split.ndim)))
    return split.reshape(part.shape)


def muon_cols(master, new_moment, gram, long_side):
    change = lr_muon * muon_shape * math.sqrt(long_side) * newton_cols(new_moment, gram)
    return master - change


def adam_step(master, first_moment, second, gradient):
    new_first = beta_one * first_moment + (1.0 - beta_one) * gradient
    new_second = beta_two * second + (1.0 - beta_two) * gradient * gradient
    first_hat = new_first / (1.0 - beta_one**ADAM_STEP)
    second_hat = new_second / (1.0 - beta_two**ADAM_STEP)
    return (master - lr_adam * first_hat / (jnp.sqrt(second_hat) + adam_eps), new_first, new_second)


def square_sum(arrays):
    running = jnp.zeros((), jnp.float32)
    for member in arrays:
        running = running + jnp.sum(member * member)
    return running


everyone = ("wide", "pair", "side")
side_bit = ("side", 1)


def swap_all(blocks, axes=everyone):
    return lax.all_to_all(blocks, axes, 0, 0, tiled=True)


def spread(values, devices):
    size = values.shape[0]
    row = jnp.pad(values, (0, -size % lanes))
    return swap_all(jnp.broadcast_to(row[None], (devices, row.shape[0])))[:, :size]


def wide_bits(wide_count):
    return [("wide", 1 << k) for k in range(wide_count.bit_length() - 1)]


def routes(wide_count, with_pair=True):
    bits = wide_bits(wide_count)
    near, far, across = bits[:1], bits[1:], [("pair", 1)] if with_pair else []
    return [across + near + far, near + far + across, far + across + near]


def my_bit(bit):
    axis, mask = bit
    return lax.axis_index(axis) // mask % 2


def exchange(values, bit):
    axis, mask = bit
    steps = [(here, here ^ mask) for here in range(lax.axis_size(axis))]
    return lax.ppermute(values, axis, steps)


def halve(values, bit, dim):
    mine = lax.dynamic_index_in_dim(values, my_bit(bit), dim, keepdims=False)
    theirs = lax.dynamic_index_in_dim(values, 1 - my_bit(bit), dim, keepdims=False)
    return mine + exchange(theirs, bit)


def double(values, bit, dim):
    theirs = exchange(values, bit)
    first = my_bit(bit) == 0
    pair = [jnp.where(first, values, theirs), jnp.where(first, theirs, values)]
    return jnp.stack(pair, axis=dim)


def cuts(length, unit):
    whole = length // unit
    sizes = [(whole + 2) // 3 * unit, (whole + 1) // 3 * unit]
    sizes.append(length - sum(sizes))
    starts = [0, sizes[0], sizes[0] + sizes[1]]
    return [(start, start + size) for start, size in zip(starts, sizes) if size]


def reduce_blocks(values, wide_count, axis, unit):
    bits = wide_bits(wide_count)[::-1] + [("pair", 1)]
    parts = []
    for route, (start, stop) in zip(routes(wide_count), cuts(values.shape[2 + axis], unit)):
        part = lax.slice_in_dim(values, start, stop, axis=2 + axis)
        part = part.reshape((2,) * len(bits) + part.shape[2:])
        left = list(bits)
        for bit in route:
            part = halve(part, bit, left.index(bit))
            left.remove(bit)
        parts.append(part)
    return jnp.concatenate(parts, axis=axis)


def here16():
    return lax.axis_index("wide") * 2 + lax.axis_index("pair")


def reduce_relative(parts, wide_count):
    done = []
    for part, route in zip(parts, routes(wide_count)):
        for bit in route:
            part = part[0] + exchange(part[1], bit)
        done.append(part)
    return done


def reduce_rows(values, wide_count):
    bits = wide_bits(wide_count)[::-1] + [("pair", 1)]
    parts = []
    for route, (start, stop) in zip(routes(wide_count), cuts(values.shape[-1], lanes)):
        part = values[..., start:stop].reshape((2,) * len(bits) + (values.shape[1], stop - start))
        left = list(bits)
        for bit in route:
            dim = left.index(bit)
            left.remove(bit)
            keep = lax.index_in_dim(part, 0, dim, keepdims=False)
            part = keep + exchange(lax.index_in_dim(part, 1, dim, keepdims=False), bit)
        parts.append(part)
    return jnp.concatenate(parts, axis=-1)


def gather_relative(block, wide_count, axis, unit, with_pair=True):
    parts = []
    for route, (start, stop) in zip(routes(wide_count, with_pair), cuts(block.shape[axis], unit)):
        part = lax.slice_in_dim(block, start, stop, axis=axis)[None]
        for bit in route[::-1]:
            part = jnp.concatenate([part, exchange(part, bit)])
        parts.append(relative_order(part, route[::-1]))
    return jnp.concatenate(parts, axis=1 + axis)


def route_shape(route, covered):
    wide = [bit for bit in route if bit not in covered]
    shape = tuple(2 if bit in covered else 1 for bit in route)

    def index(step):
        low = 1 << len(covered) - 1
        return tuple(
            0 if bit in covered else step * low // bit[1] % 2 for bit in route
        )

    assert wide
    return shape, index


def weight_grads(kernel, operands, column_specs, covered, steps, members, wide_count):
    here = jnp.stack([lax.axis_index("wide"), lax.axis_index("pair")]).astype(jnp.int32)
    shapes, specs = [], []
    for route, (start, stop) in zip(routes(wide_count), cuts(D, tile)):
        block, index = route_shape(route, covered)
        tail = (members, stop - start, lanes)
        shapes.append(jax.ShapeDtypeStruct((2,) * len(route) + tail, jnp.float32))
        specs.append(
            pl.BlockSpec(block + tail, lambda step, _, index=index: index(step) + (0, 0, 0))
        )
    return pl.pallas_call(
        kernel,
        grid_spec=pltpu.PrefetchScalarGridSpec(
            num_scalar_prefetch=1, grid=(steps,), in_specs=column_specs, out_specs=specs
        ),
        out_shape=shapes,
    )(here, *operands)


def put(refs, wide_count, covered, where, member, values):
    for ref, route, (start, stop) in zip(refs, routes(wide_count), cuts(D, tile)):
        place = tuple(where[bit] if bit in covered else 0 for bit in route)
        ref[place + (member,)] = values[start:stop]


def ffn_grads_kernel(here, up_rows, down_rows, up_cols, down_cols, *refs, wide_count):
    flip = here[1] == 0
    pair = ("pair", 1)
    for member, (rows, cols) in enumerate(((up_rows, up_cols), (down_rows, down_cols))):
        both = jnp.dot(rows[...], cols[...], preferred_element_type=jnp.float32)
        low, top = both[:, :lanes], both[:, lanes:]
        put(refs, wide_count, [pair], {pair: 0}, member, jnp.where(flip, low, top))
        put(refs, wide_count, [pair], {pair: 1}, member, jnp.where(flip, top, low))


def ffn_weight_grads(up_rows, down_rows, up_cols, down_cols, wide_count):
    whole = pl.BlockSpec(up_rows.shape, lambda step, here: (0, 0))
    cols = pl.BlockSpec((up_cols.shape[0], 2 * lanes), lambda step, here: (0, step ^ here[0]))
    kernel = functools.partial(ffn_grads_kernel, wide_count=wide_count)
    operands = (up_rows, down_rows, up_cols, down_cols)
    specs = [whole, whole, cols, cols]
    return weight_grads(kernel, operands, specs, [("pair", 1)], wide_count, 2, wide_count)


def attn_grads_kernel(here, one_rows, two_rows, one_cols, two_cols, *refs, wide_count):
    swap = here[0] % 2 == 0
    flip = here[1] == 0
    pair, near = ("pair", 1), ("wide", 1)
    blocks = []
    for rows, cols in ((one_rows, one_cols), (two_rows, two_cols)):
        both = jnp.dot(rows[...], cols[...], preferred_element_type=jnp.float32)
        low, top = both[:, :lanes], both[:, lanes:]
        blocks.append((jnp.where(swap, low, top), jnp.where(swap, top, low)))
    for step in range(2):
        one, two = blocks[0][step], blocks[1][step]
        first, second = jnp.where(flip, one, two), jnp.where(flip, two, one)
        put(refs, wide_count, [pair, near], {pair: 0, near: step}, 0, first)
        put(refs, wide_count, [pair, near], {pair: 1, near: step}, 0, second)


def attn_weight_grads(one_rows, two_rows, one_cols, two_cols, wide_count):
    whole = pl.BlockSpec(one_rows.shape, lambda step, here: (0, 0))
    cols = pl.BlockSpec((one_cols.shape[0], 2 * lanes), lambda step, here: (0, step ^ here[0] // 2))
    kernel = functools.partial(attn_grads_kernel, wide_count=wide_count)
    operands = (one_rows, two_rows, one_cols, two_cols)
    specs = [whole, whole, cols, cols]
    covered = [("pair", 1), ("wide", 1)]
    return weight_grads(kernel, operands, specs, covered, wide_count // 2, 1, wide_count)


def in_routes(blocks, wide_count):
    count = wide_count * 2
    order = jnp.arange(count) ^ here16()
    blocks = jnp.take(blocks.reshape((count,) + blocks.shape[2:]), order, axis=0)
    bits = wide_bits(wide_count)[::-1] + [("pair", 1)]
    parts = []
    for route, (start, stop) in zip(routes(wide_count), cuts(D, tile)):
        part = blocks[:, :, start:stop].reshape((2,) * len(bits) + blocks[:, :, start:stop].shape[1:])
        dims = [bits.index(bit) for bit in route]
        parts.append(part.transpose(dims + list(range(len(bits), part.ndim))))
    return parts


def gather_blocks(block, wide_count, axis, unit):
    bits = wide_bits(wide_count)[::-1] + [("pair", 1)]
    parts = []
    for route, (start, stop) in zip(routes(wide_count), cuts(block.shape[axis], unit)):
        part = lax.slice_in_dim(block, start, stop, axis=axis)
        have = []
        for bit in route[::-1]:
            have = sorted(have + [bit], key=bits.index)
            part = double(part, bit, have.index(bit))
        parts.append(part.reshape((wide_count, 2) + part.shape[len(bits) :]))
    return jnp.concatenate(parts, axis=2 + axis)


def select_rows(index, rows, precision=None):
    hits = index[:, None] == jnp.arange(rows.shape[0], dtype=jnp.int32)[None, :]
    return jnp.dot(
        hits.astype(rows.dtype), rows, precision=precision, preferred_element_type=jnp.float32
    )


def logit_grads_kernel(facts, logits_ref, source_ref, rows_ref, grad_ref, loss_ref, dec_ref):
    step = pl.program_id(0)

    @pl.when(step == 0)
    def _():
        loss_ref[...] = jnp.zeros_like(loss_ref)
        dec_ref[...] = jnp.zeros_like(dec_ref)

    columns = lax.broadcasted_iota(jnp.int32, logits_ref.shape, 1) + facts[0]
    is_word = columns < V
    rows = rows_ref[...]
    log_prob = logits_ref[...] - rows[:, 0:1]
    source_log = source_ref[0].astype(jnp.float32) - rows[:, 1:2]
    source_prob = jnp.where(is_word, jnp.exp(source_log), 0.0)
    hits = columns == rows[:, 3:4].astype(jnp.int32)
    keep = is_word & (rows[:, 2:3] > 0.5)
    losses = source_prob * (source_log - log_prob) - jnp.where(hits, log_prob, 0.0)
    loss_ref[...] += jnp.sum(jnp.where(keep, losses, 0.0), axis=0, keepdims=True)
    grads = 2.0 * jnp.exp(log_prob) - jnp.where(hits, 1.0, 0.0) - source_prob
    grads = jnp.where(keep, grads, 0.0).astype(jnp.bfloat16)
    grad_ref[...] = grads
    dec_ref[...] += jnp.sum(grads.astype(jnp.float32), axis=0, keepdims=True)


def logit_grads(facts, logits, source, row_facts, devices):
    owned = logits.shape[1]
    group = devices // 2

    def source_block(step, facts):
        return ((step % group ^ facts[1]) * 2 + (step // group ^ facts[2]), 0, 0)

    line = pl.BlockSpec((1, owned), lambda step, facts: (0, 0))
    grads, losses, dec = pl.pallas_call(
        logit_grads_kernel,
        grid_spec=pltpu.PrefetchScalarGridSpec(
            num_scalar_prefetch=1,
            grid=(devices,),
            in_specs=[
                pl.BlockSpec((MPW, owned), lambda step, facts: (step, 0)),
                pl.BlockSpec((1, MPW, owned), source_block),
                pl.BlockSpec((MPW, 4), lambda step, facts: (step, 0)),
            ],
            out_specs=[pl.BlockSpec((MPW, owned), lambda step, facts: (step, 0)), line, line],
        ),
        out_shape=[
            jax.ShapeDtypeStruct(logits.shape, jnp.bfloat16),
            jax.ShapeDtypeStruct((1, owned), jnp.float32),
            jax.ShapeDtypeStruct((1, owned), jnp.float32),
        ],
    )(facts, logits, source, row_facts)
    return grads, losses, dec[0]


def pick_rows(values, index):
    hits = index[:, None] == jnp.arange(values.shape[0], dtype=jnp.int32)[None, :]
    return jnp.sum(jnp.where(hits[:, :, None], values[None], 0), axis=1)


def add_rows(index, rows, count):
    hits = jnp.arange(count, dtype=jnp.int32)[:, None] == index[None, :]
    return jnp.dot(
        hits.astype(rows.dtype), rows, precision=high, preferred_element_type=jnp.float32
    )


def position_plan(devices, owned):
    group = devices // 2
    place = np.arange(SEQ)
    owner = (V + place) // owned
    target = 2 * (place % WINDOW % group) + place // WINDOW
    rank = np.zeros(SEQ, np.int64)
    seen = {}
    for p in range(SEQ):
        pair = (owner[p], target[p])
        rank[p] = seen.get(pair, 0)
        seen[pair] = rank[p] + 1
    assert rank.max() < slots
    return owner, target, rank


def flat_blocks(size, devices):
    total = size * devices
    starts = [dev * size // (tile * lanes) * tile for dev in range(devices)] + [total // lanes]
    ends = [-(-(dev + 1) * size // (tile * lanes)) * tile for dev in range(devices)]
    rows = max(end - start for start, end in zip(starts, ends))
    return starts, rows


def place_flat(share, device, devices):
    size = share.shape[0]
    _, rows = flat_blocks(size, devices)
    offset = device * size % (tile * lanes)
    block = lax.dynamic_update_slice(jnp.zeros((rows * lanes,), share.dtype), share, (offset,))
    return block.reshape(rows, lanes)


def join_flat(blocks, size):
    devices, rows = blocks.shape[:2]
    starts, _ = flat_blocks(size, devices)
    pieces, carry = [], None
    for dev in range(devices):
        length = starts[dev + 1] - starts[dev]
        first = blocks[dev, :tile] if carry is None else blocks[dev, :tile] + carry
        pieces += [first, blocks[dev, tile:length]]
        carry = blocks[dev, length : length + tile] if length < rows else None
    return jnp.concatenate(pieces)


def scatter_flat(flat_rows, size, device, devices):
    wide_count = lax.axis_size("wide")
    starts, rows = flat_blocks(size, devices)
    padded = jnp.pad(flat_rows, ((0, rows), (0, 0)))
    blocks = jnp.stack([padded[starts[dev] : starts[dev] + rows] for dev in range(devices)])
    bits = wide_bits(wide_count)[::-1] + [("pair", 1), side_bit]
    part = blocks.reshape((2,) * len(bits) + blocks.shape[1:])
    for bit in [side_bit] + routes(wide_count)[0]:
        part = halve(part, bit, bits.index(bit))
        bits.remove(bit)
    return lax.dynamic_slice(part.reshape(-1), (device * size % (tile * lanes),), (size,))


def shards(
    token_ids,
    live_lengths,
    key_keep,
    buckets,
    mask_pos,
    mask_labels,
    mask_counts,
    source_logits,
    embed_table,
    embed_first,
    embed_second,
    attn_mats,
    attn_moment,
    ffn_mats,
    ffn_moment,
    other_params,
    other_first,
    other_second,
):
    wide_count = lax.axis_size("wide")
    narrow_count = lax.axis_size("pair") * 2
    devices = wide_count * narrow_count
    device = lax.axis_index(everyone).astype(jnp.int32)
    owned = embed_table.shape[0]
    size = other_params.shape[0]
    col_width = attn_mats.shape[2]
    ffn_width = ffn_mats.shape[2]
    kinds = attn_mats.shape[0]
    table_low = embed_table.astype(jnp.bfloat16)

    attn_own = attn_mats.astype(jnp.bfloat16)
    other_own = place_flat(other_params.astype(jnp.bfloat16), device, devices)
    if col_width == lanes:
        merged = jnp.concatenate([attn_own.reshape(-1, lanes), other_own])
        merged = lax.all_gather(merged, everyone)
        attn_all, other_all = merged[:, : kinds * D], merged[:, kinds * D :]
    else:
        attn_all = lax.all_gather(attn_own, everyone)
        other_all = lax.all_gather(other_own, everyone)
    other_flat = join_flat(other_all, size)
    attn_all = attn_all.reshape(wide_count, narrow_count * kinds, D, col_width)
    attn_low = attn_all.transpose(1, 2, 0, 3).reshape(narrow_count * kinds, D, D)
    ffn_all = lax.all_gather(ffn_mats.astype(jnp.bfloat16), everyone)
    bias_rows = V // lanes
    up_rows = bias_rows + L * FF // lanes
    vec_rows = up_rows + NV * D // lanes
    dec_bias = lax.dynamic_slice(other_flat.reshape(-1), (device * owned,), (owned,))
    dec_bias = dec_bias.astype(jnp.float32)
    up_biases = other_flat[bias_rows:up_rows].reshape(devices // 2, 2, ffn_width)
    up_biases = up_biases.transpose(1, 0, 2).reshape(L, FF).astype(jnp.float32)
    vectors = other_flat[up_rows:vec_rows].reshape(NV, D).astype(jnp.float32)
    head_weight = other_flat[vec_rows:].reshape(D, D)

    win_count = token_ids.shape[0]
    assert win_count == 1 and SEQ == 2 * WINDOW
    group = devices // 2
    per_place = WINDOW // group
    half = device % 2
    owner_of, target_of, rank_of = position_plan(devices, owned)
    tokens = token_ids.reshape(-1)
    token_owner = tokens // owned
    token_local = tokens - token_owner * owned
    order = jnp.arange(WINDOW, dtype=jnp.int32)
    earlier = order[None, :] < order[:, None]
    same = tokens[:, None] == tokens[None, :]
    is_first = ~jnp.any(same & earlier, axis=1)
    same_owner = token_owner[:, None] == token_owner[None, :]
    rank = jnp.sum((same_owner & earlier & is_first[None, :]).astype(jnp.int32), axis=1)
    taken = np.zeros((devices, devices), np.int32)
    np.add.at(taken, (target_of, owner_of), 1)
    taken_here = lax.dynamic_index_in_dim(jnp.asarray(taken), device, 0, keepdims=False)
    owners = jnp.arange(devices, dtype=jnp.int32)
    offset = jnp.sum(jnp.where(token_owner[:, None] == owners[None, :], taken_here[None], 0), 1)
    first_slot = jnp.where(is_first, offset + rank, 0)
    slot = jnp.sum(jnp.where(same & is_first[None, :], first_slot[None, :], 0), axis=1)

    def address(round_idx):
        there = slot - round_idx * slots
        return jnp.where((there >= 0) & (there < slots), token_owner * slots + there, -1)

    def requests(addresses):
        cells = jnp.arange(devices * slots, dtype=jnp.int32)
        hits = (cells[:, None] == addresses[None, :]) & is_first[None, :]
        return jnp.sum(jnp.where(hits, token_local[None, :] + 1, 0), axis=1)

    now = address(0)
    labels_at = slots + 2
    message = jnp.concatenate(
        [
            requests(now).reshape(devices, slots),
            jnp.broadcast_to(jnp.max(slot)[None, None], (devices, 1)),
            jnp.broadcast_to(mask_counts.reshape(1, 1), (devices, 1)),
            jnp.broadcast_to(mask_labels.reshape(1, MPW), (devices, MPW)),
            jnp.zeros((devices, lanes - labels_at - MPW), jnp.int32),
        ],
        axis=1,
    )
    message = swap_all(message)
    rounds = jnp.max(message[:, slots]) // slots + 1
    counts_all = message[:, slots + 1]
    labels_all = message[:, labels_at : labels_at + MPW].reshape(-1)
    masked_total = jnp.sum(counts_all).astype(jnp.float32)
    place = np.arange(SEQ)
    cell_of = jnp.asarray(target_of * slots + rank_of, jnp.int32)
    local_of = jnp.asarray(V + place - owner_of * owned + 1, jnp.int32)
    mine = jnp.asarray(owner_of, jnp.int32) == device
    cells = jnp.arange(devices * slots, dtype=jnp.int32)
    place_hits = (cells[:, None] == cell_of[None, :]) & mine[None, :]
    place_rows = jnp.sum(jnp.where(place_hits, local_of[None, :], 0), axis=1)
    asked = message[:, :slots].reshape(-1) + place_rows - 1
    held = (owner_of * slots + rank_of).reshape(2, per_place, group).transpose(0, 2, 1)
    held = jnp.asarray(held.reshape(devices, per_place), jnp.int32)
    held = lax.dynamic_index_in_dim(held, half * group + device // 2, 0, keepdims=False)

    def fetch(asked_rows):
        rows = select_rows(asked_rows, table_low).astype(jnp.bfloat16)
        return swap_all(rows.reshape(devices, slots, D)).reshape(-1, D)

    def ask_again(addresses):
        return swap_all(requests(addresses).reshape(devices, slots)).reshape(-1) - 1

    fetched = fetch(asked)
    source_own = source_logits.reshape(MPW, V)
    source_max = jnp.max(source_own, axis=1).astype(jnp.float32)
    source_sum = jnp.sum(jnp.exp(source_own.astype(jnp.float32) - source_max[:, None]), axis=1)
    source_total = source_max + jnp.log(source_sum)
    source_cut = jnp.pad(source_own, ((0, 0), (0, devices * owned - V)))
    source_cut = source_cut.reshape(MPW, devices, owned).transpose(1, 0, 2)
    fetched, source_cut, source_total = lax.optimization_barrier(
        (fetched, source_cut, source_total)
    )
    ffn_all, source_cut = lax.optimization_barrier((ffn_all, source_cut))
    ffn_low = ffn_all.reshape(devices // 2, 2, 2 * L, D, ffn_width)
    ffn_low = ffn_low.transpose(2, 3, 1, 0, 4).reshape(2 * L, D, FF)
    source_here = swap_all(source_cut)
    token_rows = select_rows(now, fetched)
    place_part = select_rows(held, fetched).astype(jnp.bfloat16)
    place_all = gather_blocks(place_part, wide_count, 1, 128).reshape(group, per_place, D)
    place_all = place_all.transpose(1, 0, 2).reshape(WINDOW, D).astype(jnp.float32)

    def more_rows(state):
        round_idx, rows = state
        addresses = address(round_idx)
        return (round_idx + 1, rows + select_rows(addresses, fetch(ask_again(addresses))))

    _, token_rows = lax.while_loop(
        lambda state: state[0] < rounds, more_rows, (jnp.int32(1), token_rows)
    )

    is_valid = (order[None, :] < live_lengths[:, None]) & (key_keep == 1)
    key_ok = is_valid.reshape(win_count, 1, 1, 1, WINDOW)
    bucket_ids = buckets.reshape(win_count, 1, WINDOW)
    same_bucket = bucket_ids[:, :, None, :, None] == bucket_ids[:, :, None, None, :]
    allowed = same_bucket & key_ok | jnp.eye(WINDOW, dtype=bool)
    embedded = (token_rows + place_all).reshape(win_count, WINDOW, D)
    hidden, embed_pull = jax.vjp(layer_norm, embedded, vectors[0], vectors[1])
    params = (
        attn_low[0],
        attn_low[1],
        attn_low[2],
        attn_low[3],
        ffn_low[0],
        ffn_low[1],
        up_biases[0],
        vectors[2:10],
    )
    hidden, stored = layer_forward(hidden, params, allowed)
    picks = mask_pos.reshape(-1)
    head_in = select_rows(picks, hidden.reshape(WINDOW, D).astype(jnp.bfloat16))
    head_in = head_in.astype(jnp.bfloat16)
    head_pre = jnp.dot(head_in, head_weight, preferred_element_type=jnp.float32) + vectors[NV - 3]
    head_out, head_pull = jax.vjp(head_tail, head_pre, vectors[NV - 2], vectors[NV - 1])
    head_low = head_out.astype(jnp.bfloat16)

    rows_all = devices * MPW
    side = lax.axis_index("side").astype(jnp.int32)
    here = here16().astype(jnp.int32)
    order_rows = jnp.arange(devices, dtype=jnp.int32)
    rank_of_dev = (order_rows % 2 ^ side) * group + (order_rows // 2 ^ here)
    dev_of_rank = (order_rows % group ^ here) * 2 + (order_rows // group ^ side)
    head_all = gather_relative(head_low, wide_count, 1, lanes)
    head_all = jnp.concatenate([head_all, exchange(head_all, side_bit)]).reshape(rows_all, D)
    labels_all = pick_rows(labels_all.reshape(devices, MPW), dev_of_rank).reshape(rows_all, 1)
    is_live = jnp.arange(MPW, dtype=jnp.int32)[None, :] < pick_rows(counts_all[:, None], dev_of_rank)
    word_ids = device * owned + jnp.arange(owned, dtype=jnp.int32)
    is_word = (word_ids < V)[None, :]
    logits = jnp.einsum("rd,vd->rv", head_all, table_low, preferred_element_type=jnp.float32)
    logits = jnp.where(is_word, logits + dec_bias[None, :], masked_fill)
    top_here = jnp.max(logits, axis=1)
    sum_here = jnp.sum(jnp.exp(logits - top_here[:, None]), axis=1)
    stats = jnp.concatenate(
        [
            top_here.reshape(devices, MPW),
            sum_here.reshape(devices, MPW),
            jnp.zeros((devices, 2 * lanes - 2 * MPW), jnp.float32),
        ],
        axis=1,
    )
    stats, source_here = lax.optimization_barrier((stats, source_here))
    stats = swap_all(pick_rows(stats, rank_of_dev))
    tops = stats[:, :MPW]
    top = jnp.max(tops, axis=0)
    total = top + jnp.log(jnp.sum(stats[:, MPW : 2 * MPW] * jnp.exp(tops - top[None]), axis=0))
    totals = spread(jnp.concatenate([total, source_total]), devices)
    totals = pick_rows(totals, dev_of_rank)
    row_facts = jnp.concatenate(
        [
            totals[:, :MPW].reshape(rows_all, 1),
            totals[:, MPW:].reshape(rows_all, 1),
            is_live.reshape(rows_all, 1).astype(jnp.float32),
            labels_all.astype(jnp.float32),
        ],
        axis=1,
    )
    place_facts = jnp.stack([device * owned, here, side]).astype(jnp.int32)
    grad_logits, losses, grad_dec = logit_grads(
        place_facts, logits, source_here, row_facts, devices
    )
    loss_part = jnp.sum(losses)
    give = jnp.dot(grad_logits[rows_all // 2 :], table_low, preferred_element_type=jnp.float32)
    got = exchange(give, side_bit)
    keep = jnp.dot(grad_logits[: rows_all // 2], table_low, preferred_element_type=jnp.float32)
    grad_head_out = reduce_rows((keep + got).reshape(group, MPW, D), wide_count)
    grad_words = jnp.einsum("rv,rd->vd", grad_logits, head_all, preferred_element_type=jnp.float32)

    grad_pre, grad_head_gain, grad_head_shift = head_pull(grad_head_out)
    pre_low = grad_pre.astype(jnp.bfloat16)
    grad_head_w = jnp.einsum("rd,rf->df", head_in, pre_low, preferred_element_type=jnp.float32)
    grad_head_in = jnp.einsum("rf,df->rd", pre_low, head_weight, preferred_element_type=jnp.float32)
    grad_hidden = add_rows(picks, grad_head_in, WINDOW).reshape(win_count, WINDOW, D)
    grad_hidden, layer_mats, up_grad, vec_grads = layer_backward(
        grad_hidden, stored, params, allowed
    )
    grad_embed, grad_emb_gain, grad_emb_shift = embed_pull(grad_hidden)
    flat_embed = grad_embed.reshape(WINDOW, D)

    ffn_grad = jnp.concatenate(reduce_relative(layer_mats[1], wide_count), axis=1)
    attn_grad = jnp.concatenate(reduce_relative(layer_mats[0], wide_count), axis=1)
    dec_block = jnp.zeros((devices * owned,), jnp.float32)
    dec_block = lax.dynamic_update_slice(dec_block, grad_dec, (device * owned,))[:V]
    vector_block = jnp.concatenate(
        [jnp.stack([grad_emb_gain, grad_emb_shift])]
        + [vec_grads]
        + [jnp.stack([jnp.sum(pre_low.astype(jnp.float32), 0), grad_head_gain, grad_head_shift])],
        axis=0,
    )
    grad_other = jnp.concatenate(
        [
            dec_block.reshape(-1, lanes),
            up_grad.reshape(2, devices // 2, ffn_width).transpose(1, 0, 2).reshape(-1, lanes),
            vector_block.reshape(-1, lanes),
            grad_head_w.reshape(-1, lanes),
        ]
    )
    other_grad = scatter_flat(grad_other, size, device, devices)

    place_grad = flat_embed.reshape(per_place, group, D).transpose(1, 0, 2)
    place_grad = place_grad.reshape(wide_count, narrow_count // 2, per_place, D)
    place_grad = reduce_blocks(place_grad, wide_count, 1, 128)
    sent = add_rows(now, flat_embed, devices * slots) + add_rows(held, place_grad, devices * slots)
    arrived = swap_all(sent.reshape(devices, slots, D)).reshape(-1, D)
    table_grad = grad_words + add_rows(asked, arrived, owned)

    def more_grads(state):
        round_idx, grads = state
        addresses = address(round_idx)
        asked_rows = ask_again(addresses)
        sent = add_rows(addresses, flat_embed, devices * slots)
        arrived = swap_all(sent.reshape(devices, slots, D)).reshape(-1, D)
        return (round_idx + 1, grads + add_rows(asked_rows, arrived, owned))

    _, table_grad = lax.while_loop(
        lambda state: state[0] < rounds, more_grads, (jnp.int32(1), table_grad)
    )

    squares = square_sum((table_grad, attn_grad, ffn_grad, other_grad))
    sums = jnp.sum(spread(jnp.stack([squares, loss_part]), devices), axis=0)
    grad_norm = jnp.sqrt(sums[0]) / masked_total
    loss_value = sums[1] / masked_total
    factor = jnp.minimum(1.0, clip_limit / grad_norm)
    scaling = factor / masked_total

    attn_moment_new = mu_muon * attn_moment + attn_grad * scaling
    ffn_moment_new = mu_muon * ffn_moment + ffn_grad * scaling
    second = lax.axis_index("side") == 1
    keep = jnp.where(second, ffn_moment_new[1], ffn_moment_new[0])
    got = exchange(jnp.where(second, ffn_moment_new[0], ffn_moment_new[1]), side_bit)
    ffn_pair = jnp.concatenate([keep, got], axis=1)[None]
    ffn_found = gather_columns(ffn_pair, True)
    attn_found = gather_columns(attn_moment_new, False)
    ffn_found, attn_found = lax.optimization_barrier((ffn_found, attn_found))
    attn_new = muon_cols(attn_mats, attn_moment_new, gram_of(attn_found), D)
    ffn_turn = newton_cols(ffn_pair, gram_of(ffn_found))[0]
    keep, give = ffn_turn[:, :ffn_width], ffn_turn[:, ffn_width:]
    got = exchange(give, side_bit)
    ffn_turn = jnp.stack([jnp.where(second, got, keep), jnp.where(second, keep, got)])
    ffn_new = ffn_mats - lr_muon * muon_shape * math.sqrt(max(D, FF)) * ffn_turn
    embed_new, embed_first_new, embed_second_new = adam_step(
        embed_table, embed_first, embed_second, table_grad * scaling
    )
    other_new, other_first_new, other_second_new = adam_step(
        other_params, other_first, other_second, other_grad * scaling
    )
    return (
        loss_value,
        grad_norm,
        embed_new,
        embed_first_new,
        embed_second_new,
        attn_new,
        attn_moment_new,
        ffn_new,
        ffn_moment_new,
        other_new,
        other_first_new,
        other_second_new,
    )


def solution(mesh):
    wide_count, narrow_count = mesh.shape["wide"], mesh.shape["narrow"]
    assert narrow_count % 2 == 0
    split = Mesh(
        np.asarray(mesh.devices).reshape(wide_count, narrow_count // 2, 2), everyone
    )
    rows, narrow = P(everyone), ("pair", "side")
    attn_spec, ffn_spec = P(narrow, None, "wide"), P(None, None, everyone)
    in_specs = (rows,) * 11 + (attn_spec,) * 2 + (ffn_spec,) * 2 + (rows,) * 3
    out_specs = (P(), P()) + (rows,) * 3 + (attn_spec,) * 2 + (ffn_spec,) * 2 + (rows,) * 3

    return jax.shard_map(
        shards, mesh=split, in_specs=in_specs, out_specs=out_specs, check_vma=False
    )
```

```python
import functools
import math

import jax
import jax.numpy as jnp
import numpy as np
from jax import lax
from jax.experimental import pallas as pl
from jax.experimental.pallas import tpu as pltpu
from jax.sharding import Mesh
from jax.sharding import PartitionSpec as P

D = 1024
FF = 4096
HEADS = 16
L = 1
V = 30720
SEQ = 1024
WINDOW = 512
NS_ITERS = 3
ADAM_STEP = 5
MPW = 80
NV = 13


high = lax.Precision.HIGH
lanes = 128
tile = 16
slots = 32
ln_eps = 1e-05
masked_fill = -1e30
clip_limit = 0.3
ns_a = 3.4445
ns_b = -4.775
ns_c = 2.0315
mu_muon = 0.95
lr_muon = 0.1
muon_shape = 0.2
lr_adam = 0.01
beta_one = 0.9
beta_two = 0.999
adam_eps = 1e-08


def layer_norm(inputs, gain_vec, shift_vec):
    center = inputs - jnp.mean(inputs, -1, keepdims=True)
    spread = jnp.mean(center * center, -1, keepdims=True)
    return center * lax.rsqrt(spread + ln_eps) * gain_vec + shift_vec


def exact_gelu(inputs):
    return jax.nn.gelu(inputs, approximate=False)


def head_tail(head_pre, gain_vec, shift_vec):
    return layer_norm(exact_gelu(head_pre), gain_vec, shift_vec)


def project(inputs, weight):
    return jnp.einsum("bsd,df->bsf", inputs, weight, preferred_element_type=jnp.float32)


def project_back(gradients, weight):
    return jnp.einsum("bsf,df->bsd", gradients, weight, preferred_element_type=jnp.float32)


def col_sum(inputs):
    return jnp.sum(inputs.astype(jnp.float32), axis=(0, 1))


def to_heads(inputs):
    return inputs.reshape(
        inputs.shape[0], inputs.shape[1] // WINDOW, WINDOW, HEADS, inputs.shape[2] // HEADS
    )


def attn_scores(queries, key_proj, allowed):
    raw_scores = jnp.einsum(
        "bnqhe,bnkhe->bnhqk",
        to_heads(queries),
        to_heads(key_proj),
        preferred_element_type=jnp.float32,
    )
    return jnp.where(allowed, raw_scores * (queries.shape[2] // HEADS) ** (-0.5), masked_fill)


def share(values, axis):
    return jnp.concatenate([values, exchange(values, side_bit)], axis=axis)


def swap_pick(for_first, for_second, axis):
    first = lax.axis_index("side") == 0
    keep = jnp.where(first, for_first, for_second)
    got = exchange(jnp.where(first, for_second, for_first), side_bit)
    return jnp.concatenate([keep, got], axis=axis)


def share_half(values):
    side = lax.axis_index("side")
    half = values.shape[1] // 2
    keep = lax.dynamic_slice_in_dim(values, side * half, half, axis=1)
    got = exchange(lax.dynamic_slice_in_dim(values, (1 - side) * half, half, axis=1), side_bit)
    return jnp.concatenate([keep, got])


def layer_forward(hidden, params, allowed):
    w_query, w_key, w_value, w_out, w_up, w_down, up_bias, vectors = params
    count, length, model_width = hidden.shape
    inputs = hidden.astype(jnp.bfloat16)
    queries = (project(inputs, w_query) + vectors[4]).astype(jnp.bfloat16)
    key_proj = project(inputs, w_key).astype(jnp.bfloat16)
    values = (project(inputs, w_value) + vectors[5]).astype(jnp.bfloat16)
    scores = attn_scores(queries, key_proj, allowed)
    log_total = jax.nn.logsumexp(scores, axis=-1, keepdims=True)
    prob_low = jnp.exp(scores - log_total).astype(jnp.bfloat16)
    context = jnp.einsum(
        "bnhqk,bnkhe->bnqhe", prob_low, to_heads(values), preferred_element_type=jnp.float32
    )
    context = context.reshape(count, length, model_width).astype(jnp.bfloat16)
    attn_sum = hidden + (project(context, w_out) + vectors[6])
    middle, first_pull = jax.vjp(layer_norm, attn_sum, vectors[0], vectors[1])
    middle_low = middle.astype(jnp.bfloat16)
    up_proj = project(middle_low, w_up) + up_bias
    activated, gelu_pull = jax.vjp(exact_gelu, up_proj)
    act_low = activated.astype(jnp.bfloat16)
    ffn_sum = middle + (project_back(act_low, w_down) + vectors[7])
    output, second_pull = jax.vjp(layer_norm, ffn_sum, vectors[2], vectors[3])
    stored = (
        inputs,
        queries,
        key_proj,
        values,
        log_total,
        context,
        first_pull,
        middle_low,
        gelu_pull,
        act_low,
        second_pull,
    )
    return (output, stored)


def layer_backward(grad_out, stored, params, allowed):
    w_query, w_key, w_value, w_out, w_up, w_down, _, _ = params
    (
        inputs,
        queries,
        key_proj,
        values,
        log_total,
        context,
        first_pull,
        middle_low,
        gelu_pull,
        act_low,
        second_pull,
    ) = stored
    count, length, model_width = grad_out.shape
    grad_ffn, grad_gain_two, grad_shift_two = second_pull(grad_out)
    down_low = grad_ffn.astype(jnp.bfloat16)
    (grad_up,) = gelu_pull(project(down_low, w_down))
    up_low = grad_up.astype(jnp.bfloat16)
    wide_count = lax.axis_size("wide")
    operands = (
        share(middle_low[0].T, 1),
        share(down_low[0].T, 1),
        share_half(up_low[0]),
        share_half(act_low[0]),
    )
    if FF // (4 * wide_count) == lanes:
        grad_mats_ffn = ffn_weight_grads(*operands, wide_count)
    else:
        blocks = jnp.stack([jnp.dot(*operands[::2], preferred_element_type=jnp.float32),
                            jnp.dot(*operands[1::2], preferred_element_type=jnp.float32)])
        blocks = blocks.reshape(2, D, wide_count, 2, -1).transpose(2, 3, 0, 1, 4)
        grad_mats_ffn = in_routes(blocks, wide_count)
    grad_ffn, parts = tied(grad_ffn, grad_mats_ffn)
    parts = reduce_step(parts, wide_count, 0)
    grad_middle = grad_ffn + project_back(up_low, w_up)
    grad_attn, grad_gain_one, grad_shift_one = first_pull(grad_middle)
    attn_low = grad_attn.astype(jnp.bfloat16)
    grad_context = to_heads(project_back(attn_low, w_out).astype(jnp.bfloat16))
    attn_prob = jnp.exp(attn_scores(queries, key_proj, allowed) - log_total)
    prob_low = attn_prob.astype(jnp.bfloat16)
    grad_prob = jnp.einsum(
        "bnqhe,bnkhe->bnhqk", grad_context, to_heads(values), preferred_element_type=jnp.float32
    )
    grad_value = jnp.einsum(
        "bnhqk,bnqhe->bnkhe", prob_low, grad_context, preferred_element_type=jnp.float32
    )
    grad_value = grad_value.reshape(count, length, model_width).astype(jnp.bfloat16)
    grad_scores = attn_prob * (grad_prob - jnp.sum(grad_prob * attn_prob, -1, keepdims=True))
    grad_raw = (grad_scores * (model_width // HEADS) ** (-0.5)).astype(jnp.bfloat16)
    late_keys, parts = tied(key_proj, parts)
    parts = reduce_step(parts, wide_count, 1)
    grad_query = jnp.einsum(
        "bnhqk,bnkhe->bnqhe", grad_raw, to_heads(late_keys), preferred_element_type=jnp.float32
    )
    grad_query = grad_query.reshape(count, length, model_width).astype(jnp.bfloat16)
    grad_key = jnp.einsum(
        "bnhqk,bnqhe->bnkhe", grad_raw, to_heads(queries), preferred_element_type=jnp.float32
    )
    grad_key = grad_key.reshape(count, length, model_width).astype(jnp.bfloat16)
    grad_query, parts = tied(grad_query, parts)
    parts = reduce_step(parts, wide_count, 2)
    grad_hidden = (
        grad_attn
        + project_back(grad_query, w_query)
        + project_back(grad_key, w_key)
        + project_back(grad_value, w_value)
    )
    grad_hidden, parts = tied(grad_hidden, parts)
    for step in range(3, len(routes(wide_count)[0])):
        parts = reduce_step(parts, wide_count, step)
    operands = (
        share(inputs[0].T, 1),
        swap_pick(inputs[0].T, context[0].T, 1),
        swap_pick(grad_query[0], grad_key[0], 0),
        swap_pick(grad_value[0], attn_low[0], 0),
    )
    if D // wide_count == lanes:
        grad_mats_attn = attn_weight_grads(*operands, wide_count)
    else:
        blocks = jnp.stack([jnp.dot(*operands[::2], preferred_element_type=jnp.float32),
                            jnp.dot(*operands[1::2], preferred_element_type=jnp.float32)])
        blocks = blocks.reshape(2, 1, D, wide_count, -1).transpose(3, 0, 1, 2, 4)
        grad_mats_attn = in_routes(blocks, wide_count)
    matrices = (grad_mats_attn, parts)
    vector_grads = jnp.stack(
        [
            grad_gain_one,
            grad_shift_one,
            grad_gain_two,
            grad_shift_two,
            col_sum(grad_query),
            col_sum(grad_value),
            col_sum(attn_low),
            col_sum(down_low),
        ]
    )
    return (grad_hidden, matrices, col_sum(up_low), vector_grads)


def slab_product(matrix, columns):
    return jnp.einsum(
        "kde,kec->kdc", matrix, columns, precision=high, preferred_element_type=jnp.float32
    )


def newton_cols(moment, gram):
    norms = jnp.sqrt(jnp.trace(gram, axis1=1, axis2=2))
    scaling = 1.0 / (norms + 1e-07)
    current = moment * scaling[:, None, None]
    gram = gram * (scaling * scaling)[:, None, None]
    for step_idx in range(NS_ITERS):
        if step_idx + 1 < NS_ITERS:
            poly = ns_b * gram + ns_c * jnp.einsum("kde,kef->kdf", gram, gram)
            current = ns_a * current + slab_product(poly, current)
            half = ns_a * gram + jnp.einsum("kde,kef->kdf", poly, gram)
            gram = ns_a * half + jnp.einsum("kde,kef->kdf", half, poly)
        else:
            once = slab_product(gram, current)
            current = ns_a * current + ns_b * once + ns_c * slab_product(gram, once)
    return current


def gather_columns(columns, with_pair):
    wide_count = lax.axis_size("wide")
    return gather_relative(columns[0].astype(jnp.bfloat16), wide_count, 0, tile, with_pair)


def gram_of(found):
    return jnp.einsum("wdc,wec->de", found, found, preferred_element_type=jnp.float32)[None]


def relative_order(part, taken):
    names = [bit for bit in wide_bits(lax.axis_size("wide"))[::-1] + [("pair", 1)] if bit in taken]
    dims = [names.index(bit) for bit in taken[::-1]]
    split = part.reshape((2,) * len(taken) + part.shape[1:])
    turn = [dims.index(place) for place in range(len(taken))]
    split = split.transpose(turn + list(range(len(taken), split.ndim)))
    return split.reshape(part.shape)


def muon_cols(master, new_moment, gram, long_side):
    change = lr_muon * muon_shape * math.sqrt(long_side) * newton_cols(new_moment, gram)
    return master - change


def adam_step(master, first_moment, second, gradient):
    new_first = beta_one * first_moment + (1.0 - beta_one) * gradient
    new_second = beta_two * second + (1.0 - beta_two) * gradient * gradient
    first_hat = new_first / (1.0 - beta_one**ADAM_STEP)
    second_hat = new_second / (1.0 - beta_two**ADAM_STEP)
    return (master - lr_adam * first_hat / (jnp.sqrt(second_hat) + adam_eps), new_first, new_second)


def square_sum(arrays):
    running = jnp.zeros((), jnp.float32)
    for member in arrays:
        running = running + jnp.sum(member * member)
    return running


everyone = ("wide", "pair", "side")
side_bit = ("side", 1)


def swap_all(blocks, axes=everyone):
    return lax.all_to_all(blocks, axes, 0, 0, tiled=True)


def spread(values, devices):
    size = values.shape[0]
    row = jnp.pad(values, (0, -size % lanes))
    return swap_all(jnp.broadcast_to(row[None], (devices, row.shape[0])))[:, :size]


def wide_bits(wide_count):
    return [("wide", 1 << k) for k in range(wide_count.bit_length() - 1)]


def routes(wide_count, with_pair=True):
    bits = wide_bits(wide_count)
    near, far, across = bits[:1], bits[1:], [("pair", 1)] if with_pair else []
    return [across + near + far, near + far + across, far + across + near]


def my_bit(bit):
    axis, mask = bit
    return lax.axis_index(axis) // mask % 2


def exchange(values, bit):
    axis, mask = bit
    steps = [(here, here ^ mask) for here in range(lax.axis_size(axis))]
    return lax.ppermute(values, axis, steps)


def halve(values, bit, dim):
    mine = lax.dynamic_index_in_dim(values, my_bit(bit), dim, keepdims=False)
    theirs = lax.dynamic_index_in_dim(values, 1 - my_bit(bit), dim, keepdims=False)
    return mine + exchange(theirs, bit)


def double(values, bit, dim):
    theirs = exchange(values, bit)
    first = my_bit(bit) == 0
    pair = [jnp.where(first, values, theirs), jnp.where(first, theirs, values)]
    return jnp.stack(pair, axis=dim)


def cuts(length, unit):
    whole = length // unit
    sizes = [(whole + 2) // 3 * unit, (whole + 1) // 3 * unit]
    sizes.append(length - sum(sizes))
    starts = [0, sizes[0], sizes[0] + sizes[1]]
    return [(start, start + size) for start, size in zip(starts, sizes) if size]


def reduce_blocks(values, wide_count, axis, unit):
    bits = wide_bits(wide_count)[::-1] + [("pair", 1)]
    parts = []
    for route, (start, stop) in zip(routes(wide_count), cuts(values.shape[2 + axis], unit)):
        part = lax.slice_in_dim(values, start, stop, axis=2 + axis)
        part = part.reshape((2,) * len(bits) + part.shape[2:])
        left = list(bits)
        for bit in route:
            part = halve(part, bit, left.index(bit))
            left.remove(bit)
        parts.append(part)
    return jnp.concatenate(parts, axis=axis)


def here16():
    return lax.axis_index("wide") * 2 + lax.axis_index("pair")


def reduce_step(parts, wide_count, step):
    return [
        part[0] + exchange(part[1], route[step])
        for part, route in zip(parts, routes(wide_count))
    ]


def tied(value, parts):
    value, *parts = lax.optimization_barrier((value, *parts))
    return value, parts


def reduce_relative(parts, wide_count):
    done = []
    for part, route in zip(parts, routes(wide_count)):
        for bit in route:
            part = part[0] + exchange(part[1], bit)
        done.append(part)
    return done


def reduce_rows(values, wide_count):
    bits = wide_bits(wide_count)[::-1] + [("pair", 1)]
    parts = []
    for route, (start, stop) in zip(routes(wide_count), cuts(values.shape[-1], lanes)):
        part = values[..., start:stop].reshape((2,) * len(bits) + (values.shape[1], stop - start))
        left = list(bits)
        for bit in route:
            dim = left.index(bit)
            left.remove(bit)
            keep = lax.index_in_dim(part, 0, dim, keepdims=False)
            part = keep + exchange(lax.index_in_dim(part, 1, dim, keepdims=False), bit)
        parts.append(part)
    return jnp.concatenate(parts, axis=-1)


def gather_relative(block, wide_count, axis, unit, with_pair=True):
    parts = []
    for route, (start, stop) in zip(routes(wide_count, with_pair), cuts(block.shape[axis], unit)):
        part = lax.slice_in_dim(block, start, stop, axis=axis)[None]
        for bit in route[::-1]:
            part = jnp.concatenate([part, exchange(part, bit)])
        parts.append(relative_order(part, route[::-1]))
    return jnp.concatenate(parts, axis=1 + axis)


def route_shape(route, covered):
    wide = [bit for bit in route if bit not in covered]
    shape = tuple(2 if bit in covered else 1 for bit in route)

    def index(step):
        low = 1 << len(covered) - 1
        return tuple(
            0 if bit in covered else step * low // bit[1] % 2 for bit in route
        )

    assert wide
    return shape, index


def weight_grads(kernel, operands, column_specs, covered, steps, members, wide_count):
    here = jnp.stack([lax.axis_index("wide"), lax.axis_index("pair")]).astype(jnp.int32)
    shapes, specs = [], []
    for route, (start, stop) in zip(routes(wide_count), cuts(D, tile)):
        block, index = route_shape(route, covered)
        tail = (members, stop - start, lanes)
        shapes.append(jax.ShapeDtypeStruct((2,) * len(route) + tail, jnp.float32))
        specs.append(
            pl.BlockSpec(block + tail, lambda step, _, index=index: index(step) + (0, 0, 0))
        )
    return pl.pallas_call(
        kernel,
        grid_spec=pltpu.PrefetchScalarGridSpec(
            num_scalar_prefetch=1, grid=(steps,), in_specs=column_specs, out_specs=specs
        ),
        out_shape=shapes,
    )(here, *operands)


def put(refs, wide_count, covered, where, member, values):
    for ref, route, (start, stop) in zip(refs, routes(wide_count), cuts(D, tile)):
        place = tuple(where[bit] if bit in covered else 0 for bit in route)
        ref[place + (member,)] = values[start:stop]


def ffn_grads_kernel(here, up_rows, down_rows, up_cols, down_cols, *refs, wide_count):
    flip = here[1] == 0
    pair = ("pair", 1)
    for member, (rows, cols) in enumerate(((up_rows, up_cols), (down_rows, down_cols))):
        both = jnp.dot(rows[...], cols[...], preferred_element_type=jnp.float32)
        low, top = both[:, :lanes], both[:, lanes:]
        put(refs, wide_count, [pair], {pair: 0}, member, jnp.where(flip, low, top))
        put(refs, wide_count, [pair], {pair: 1}, member, jnp.where(flip, top, low))


def ffn_weight_grads(up_rows, down_rows, up_cols, down_cols, wide_count):
    whole = pl.BlockSpec(up_rows.shape, lambda step, here: (0, 0))
    cols = pl.BlockSpec((up_cols.shape[0], 2 * lanes), lambda step, here: (0, step ^ here[0]))
    kernel = functools.partial(ffn_grads_kernel, wide_count=wide_count)
    operands = (up_rows, down_rows, up_cols, down_cols)
    specs = [whole, whole, cols, cols]
    return weight_grads(kernel, operands, specs, [("pair", 1)], wide_count, 2, wide_count)


def attn_grads_kernel(here, one_rows, two_rows, one_cols, two_cols, *refs, wide_count):
    swap = here[0] % 2 == 0
    flip = here[1] == 0
    pair, near = ("pair", 1), ("wide", 1)
    blocks = []
    for rows, cols in ((one_rows, one_cols), (two_rows, two_cols)):
        both = jnp.dot(rows[...], cols[...], preferred_element_type=jnp.float32)
        low, top = both[:, :lanes], both[:, lanes:]
        blocks.append((jnp.where(swap, low, top), jnp.where(swap, top, low)))
    for step in range(2):
        one, two = blocks[0][step], blocks[1][step]
        first, second = jnp.where(flip, one, two), jnp.where(flip, two, one)
        put(refs, wide_count, [pair, near], {pair: 0, near: step}, 0, first)
        put(refs, wide_count, [pair, near], {pair: 1, near: step}, 0, second)


def attn_weight_grads(one_rows, two_rows, one_cols, two_cols, wide_count):
    whole = pl.BlockSpec(one_rows.shape, lambda step, here: (0, 0))
    cols = pl.BlockSpec((one_cols.shape[0], 2 * lanes), lambda step, here: (0, step ^ here[0] // 2))
    kernel = functools.partial(attn_grads_kernel, wide_count=wide_count)
    operands = (one_rows, two_rows, one_cols, two_cols)
    specs = [whole, whole, cols, cols]
    covered = [("pair", 1), ("wide", 1)]
    return weight_grads(kernel, operands, specs, covered, wide_count // 2, 1, wide_count)


def in_routes(blocks, wide_count):
    count = wide_count * 2
    order = jnp.arange(count) ^ here16()
    blocks = jnp.take(blocks.reshape((count,) + blocks.shape[2:]), order, axis=0)
    bits = wide_bits(wide_count)[::-1] + [("pair", 1)]
    parts = []
    for route, (start, stop) in zip(routes(wide_count), cuts(D, tile)):
        part = blocks[:, :, start:stop].reshape((2,) * len(bits) + blocks[:, :, start:stop].shape[1:])
        dims = [bits.index(bit) for bit in route]
        parts.append(part.transpose(dims + list(range(len(bits), part.ndim))))
    return parts


def gather_blocks(block, wide_count, axis, unit):
    bits = wide_bits(wide_count)[::-1] + [("pair", 1)]
    parts = []
    for route, (start, stop) in zip(routes(wide_count), cuts(block.shape[axis], unit)):
        part = lax.slice_in_dim(block, start, stop, axis=axis)
        have = []
        for bit in route[::-1]:
            have = sorted(have + [bit], key=bits.index)
            part = double(part, bit, have.index(bit))
        parts.append(part.reshape((wide_count, 2) + part.shape[len(bits) :]))
    return jnp.concatenate(parts, axis=2 + axis)


def select_rows(index, rows, precision=None):
    hits = index[:, None] == jnp.arange(rows.shape[0], dtype=jnp.int32)[None, :]
    return jnp.dot(
        hits.astype(rows.dtype), rows, precision=precision, preferred_element_type=jnp.float32
    )


def logit_grads_kernel(facts, logits_ref, source_ref, rows_ref, grad_ref, loss_ref, dec_ref):
    step = pl.program_id(0)

    @pl.when(step == 0)
    def _():
        loss_ref[...] = jnp.zeros_like(loss_ref)
        dec_ref[...] = jnp.zeros_like(dec_ref)

    columns = lax.broadcasted_iota(jnp.int32, logits_ref.shape, 1) + facts[0]
    is_word = columns < V
    rows = rows_ref[...]
    log_prob = logits_ref[...] - rows[:, 0:1]
    source_log = source_ref[0].astype(jnp.float32) - rows[:, 1:2]
    source_prob = jnp.where(is_word, jnp.exp(source_log), 0.0)
    hits = columns == rows[:, 3:4].astype(jnp.int32)
    keep = is_word & (rows[:, 2:3] > 0.5)
    losses = source_prob * (source_log - log_prob) - jnp.where(hits, log_prob, 0.0)
    loss_ref[...] += jnp.sum(jnp.where(keep, losses, 0.0), axis=0, keepdims=True)
    grads = 2.0 * jnp.exp(log_prob) - jnp.where(hits, 1.0, 0.0) - source_prob
    grads = jnp.where(keep, grads, 0.0).astype(jnp.bfloat16)
    grad_ref[...] = grads
    dec_ref[...] += jnp.sum(grads.astype(jnp.float32), axis=0, keepdims=True)


def logit_grads(facts, logits, source, row_facts, devices):
    owned = logits.shape[1]
    group = devices // 2

    def source_block(step, facts):
        return ((step % group ^ facts[1]) * 2 + (step // group ^ facts[2]), 0, 0)

    line = pl.BlockSpec((1, owned), lambda step, facts: (0, 0))
    grads, losses, dec = pl.pallas_call(
        logit_grads_kernel,
        grid_spec=pltpu.PrefetchScalarGridSpec(
            num_scalar_prefetch=1,
            grid=(devices,),
            in_specs=[
                pl.BlockSpec((MPW, owned), lambda step, facts: (step, 0)),
                pl.BlockSpec((1, MPW, owned), source_block),
                pl.BlockSpec((MPW, 4), lambda step, facts: (step, 0)),
            ],
            out_specs=[pl.BlockSpec((MPW, owned), lambda step, facts: (step, 0)), line, line],
        ),
        out_shape=[
            jax.ShapeDtypeStruct(logits.shape, jnp.bfloat16),
            jax.ShapeDtypeStruct((1, owned), jnp.float32),
            jax.ShapeDtypeStruct((1, owned), jnp.float32),
        ],
    )(facts, logits, source, row_facts)
    return grads, losses, dec[0]


def pick_rows(values, index):
    hits = index[:, None] == jnp.arange(values.shape[0], dtype=jnp.int32)[None, :]
    return jnp.sum(jnp.where(hits[:, :, None], values[None], 0), axis=1)


def add_rows(index, rows, count):
    hits = jnp.arange(count, dtype=jnp.int32)[:, None] == index[None, :]
    return jnp.dot(
        hits.astype(rows.dtype), rows, precision=high, preferred_element_type=jnp.float32
    )


def position_plan(devices, owned):
    group = devices // 2
    place = np.arange(SEQ)
    owner = (V + place) // owned
    target = 2 * (place % WINDOW % group) + place // WINDOW
    rank = np.zeros(SEQ, np.int64)
    seen = {}
    for p in range(SEQ):
        pair = (owner[p], target[p])
        rank[p] = seen.get(pair, 0)
        seen[pair] = rank[p] + 1
    assert rank.max() < slots
    return owner, target, rank


def flat_blocks(size, devices):
    total = size * devices
    starts = [dev * size // (tile * lanes) * tile for dev in range(devices)] + [total // lanes]
    ends = [-(-(dev + 1) * size // (tile * lanes)) * tile for dev in range(devices)]
    rows = max(end - start for start, end in zip(starts, ends))
    return starts, rows


def place_flat(share, device, devices):
    size = share.shape[0]
    _, rows = flat_blocks(size, devices)
    offset = device * size % (tile * lanes)
    block = lax.dynamic_update_slice(jnp.zeros((rows * lanes,), share.dtype), share, (offset,))
    return block.reshape(rows, lanes)


def join_kernel(blocks_ref, out_ref, *, starts):
    rows = blocks_ref.shape[1]
    for dev in range(len(starts) - 1):
        length = starts[dev + 1] - starts[dev]
        out_ref[starts[dev] : starts[dev + 1]] = blocks_ref[dev, :length]
    for dev in range(1, len(starts) - 1):
        length = starts[dev] - starts[dev - 1]
        if length < rows:
            shared = slice(starts[dev], starts[dev] + tile)
            both = blocks_ref[dev, :tile].astype(jnp.float32)
            both += blocks_ref[dev - 1, length : length + tile].astype(jnp.float32)
            out_ref[shared] = both.astype(out_ref.dtype)


def join_flat(blocks, size):
    starts, _ = flat_blocks(size, blocks.shape[0])
    starts[-1] += -starts[-1] % tile
    return pl.pallas_call(
        functools.partial(join_kernel, starts=starts),
        out_shape=jax.ShapeDtypeStruct((starts[-1], lanes), blocks.dtype),
    )(blocks)


def split_kernel(front_ref, rest_ref, out_ref, *, starts):
    front, rows = front_ref.shape[0], out_ref.shape[1]
    total = front + rest_ref.shape[0]
    for dev, start in enumerate(starts[:-1]):
        stop = min(start + rows, total)
        middle = min(max(start, front), stop)
        if start < middle:
            out_ref[dev, : middle - start] = front_ref[start:middle]
        if middle < stop:
            out_ref[dev, middle - start : stop - start] = rest_ref[middle - front : stop - front]
        if stop < start + rows:
            left = start + rows - stop
            out_ref[dev, rows - left :] = jnp.zeros((left, lanes), out_ref.dtype)


def scatter_flat(front, rest, size, device, devices):
    wide_count = lax.axis_size("wide")
    starts, rows = flat_blocks(size, devices)
    blocks = pl.pallas_call(
        functools.partial(split_kernel, starts=starts),
        out_shape=jax.ShapeDtypeStruct((devices, rows, lanes), front.dtype),
    )(front, rest)
    bits = wide_bits(wide_count)[::-1] + [("pair", 1), side_bit]
    part = blocks.reshape((2,) * len(bits) + blocks.shape[1:])
    for bit in [side_bit] + routes(wide_count)[0]:
        part = halve(part, bit, bits.index(bit))
        bits.remove(bit)
    return lax.dynamic_slice(part.reshape(-1), (device * size % (tile * lanes),), (size,))


def shards(
    token_ids,
    live_lengths,
    key_keep,
    buckets,
    mask_pos,
    mask_labels,
    mask_counts,
    source_logits,
    embed_table,
    embed_first,
    embed_second,
    attn_mats,
    attn_moment,
    ffn_mats,
    ffn_moment,
    other_params,
    other_first,
    other_second,
):
    wide_count = lax.axis_size("wide")
    narrow_count = lax.axis_size("pair") * 2
    devices = wide_count * narrow_count
    device = lax.axis_index(everyone).astype(jnp.int32)
    owned = embed_table.shape[0]
    size = other_params.shape[0]
    col_width = attn_mats.shape[2]
    ffn_width = ffn_mats.shape[2]
    kinds = attn_mats.shape[0]
    table_low = embed_table.astype(jnp.bfloat16)

    attn_own = attn_mats.astype(jnp.bfloat16)
    other_own = place_flat(other_params.astype(jnp.bfloat16), device, devices)
    if col_width == lanes:
        merged = jnp.concatenate([attn_own.reshape(-1, lanes), other_own])
        merged = lax.all_gather(merged, everyone)
        attn_all, other_all = merged[:, : kinds * D], merged[:, kinds * D :]
    else:
        attn_all = lax.all_gather(attn_own, everyone)
        other_all = lax.all_gather(other_own, everyone)
    other_flat = join_flat(other_all, size)
    attn_all = attn_all.reshape(wide_count, narrow_count * kinds, D, col_width)
    attn_low = attn_all.transpose(1, 2, 0, 3).reshape(narrow_count * kinds, D, D)
    ffn_all = lax.all_gather(ffn_mats.astype(jnp.bfloat16), everyone)
    bias_rows = V // lanes
    up_rows = bias_rows + L * FF // lanes
    vec_rows = up_rows + NV * D // lanes
    dec_bias = lax.dynamic_slice(other_flat.reshape(-1), (device * owned,), (owned,))
    dec_bias = dec_bias.astype(jnp.float32)
    up_biases = other_flat[bias_rows:up_rows].reshape(devices // 2, 2, ffn_width)
    up_biases = up_biases.transpose(1, 0, 2).reshape(L, FF).astype(jnp.float32)
    vectors = other_flat[up_rows:vec_rows].reshape(NV, D).astype(jnp.float32)
    head_weight = other_flat[vec_rows : vec_rows + D * D // lanes].reshape(D, D)

    win_count = token_ids.shape[0]
    assert win_count == 1 and SEQ == 2 * WINDOW
    group = devices // 2
    per_place = WINDOW // group
    half = device % 2
    owner_of, target_of, rank_of = position_plan(devices, owned)
    tokens = token_ids.reshape(-1)
    token_owner = tokens // owned
    token_local = tokens - token_owner * owned
    order = jnp.arange(WINDOW, dtype=jnp.int32)
    earlier = order[None, :] < order[:, None]
    same = tokens[:, None] == tokens[None, :]
    is_first = ~jnp.any(same & earlier, axis=1)
    same_owner = token_owner[:, None] == token_owner[None, :]
    rank = jnp.sum((same_owner & earlier & is_first[None, :]).astype(jnp.int32), axis=1)
    taken = np.zeros((devices, devices), np.int32)
    np.add.at(taken, (target_of, owner_of), 1)
    taken_here = lax.dynamic_index_in_dim(jnp.asarray(taken), device, 0, keepdims=False)
    owners = jnp.arange(devices, dtype=jnp.int32)
    offset = jnp.sum(jnp.where(token_owner[:, None] == owners[None, :], taken_here[None], 0), 1)
    first_slot = jnp.where(is_first, offset + rank, 0)
    slot = jnp.sum(jnp.where(same & is_first[None, :], first_slot[None, :], 0), axis=1)

    def address(round_idx):
        there = slot - round_idx * slots
        return jnp.where((there >= 0) & (there < slots), token_owner * slots + there, -1)

    def requests(addresses):
        cells = jnp.arange(devices * slots, dtype=jnp.int32)
        hits = (cells[:, None] == addresses[None, :]) & is_first[None, :]
        return jnp.sum(jnp.where(hits, token_local[None, :] + 1, 0), axis=1)

    now = address(0)
    labels_at = slots + 2
    message = jnp.concatenate(
        [
            requests(now).reshape(devices, slots),
            jnp.broadcast_to(jnp.max(slot)[None, None], (devices, 1)),
            jnp.broadcast_to(mask_counts.reshape(1, 1), (devices, 1)),
            jnp.broadcast_to(mask_labels.reshape(1, MPW), (devices, MPW)),
            jnp.zeros((devices, lanes - labels_at - MPW), jnp.int32),
        ],
        axis=1,
    )
    message = swap_all(message)
    rounds = jnp.max(message[:, slots]) // slots + 1
    counts_all = message[:, slots + 1]
    labels_all = message[:, labels_at : labels_at + MPW].reshape(-1)
    masked_total = jnp.sum(counts_all).astype(jnp.float32)
    place = np.arange(SEQ)
    cell_of = jnp.asarray(target_of * slots + rank_of, jnp.int32)
    local_of = jnp.asarray(V + place - owner_of * owned + 1, jnp.int32)
    mine = jnp.asarray(owner_of, jnp.int32) == device
    cells = jnp.arange(devices * slots, dtype=jnp.int32)
    place_hits = (cells[:, None] == cell_of[None, :]) & mine[None, :]
    place_rows = jnp.sum(jnp.where(place_hits, local_of[None, :], 0), axis=1)
    asked = message[:, :slots].reshape(-1) + place_rows - 1
    held = (owner_of * slots + rank_of).reshape(2, per_place, group).transpose(0, 2, 1)
    held = jnp.asarray(held.reshape(devices, per_place), jnp.int32)
    held = lax.dynamic_index_in_dim(held, half * group + device // 2, 0, keepdims=False)

    def fetch(asked_rows):
        rows = select_rows(asked_rows, table_low).astype(jnp.bfloat16)
        return swap_all(rows.reshape(devices, slots, D)).reshape(-1, D)

    def ask_again(addresses):
        return swap_all(requests(addresses).reshape(devices, slots)).reshape(-1) - 1

    fetched = fetch(asked)
    source_own = source_logits.reshape(MPW, V)
    source_max = jnp.max(source_own, axis=1).astype(jnp.float32)
    source_sum = jnp.sum(jnp.exp(source_own.astype(jnp.float32) - source_max[:, None]), axis=1)
    source_total = source_max + jnp.log(source_sum)
    source_cut = jnp.pad(source_own, ((0, 0), (0, devices * owned - V)))
    source_cut = source_cut.reshape(MPW, devices, owned).transpose(1, 0, 2)
    fetched, source_cut, source_total = lax.optimization_barrier(
        (fetched, source_cut, source_total)
    )
    ffn_all, source_cut = lax.optimization_barrier((ffn_all, source_cut))
    ffn_low = ffn_all.reshape(devices // 2, 2, 2 * L, D, ffn_width)
    ffn_low = ffn_low.transpose(2, 3, 1, 0, 4).reshape(2 * L, D, FF)
    source_here = swap_all(source_cut)
    token_rows = select_rows(now, fetched)
    place_part = select_rows(held, fetched).astype(jnp.bfloat16)
    place_all = gather_blocks(place_part, wide_count, 1, 128).reshape(group, per_place, D)
    place_all = place_all.transpose(1, 0, 2).reshape(WINDOW, D).astype(jnp.float32)

    def more_rows(state):
        round_idx, rows = state
        addresses = address(round_idx)
        return (round_idx + 1, rows + select_rows(addresses, fetch(ask_again(addresses))))

    _, token_rows = lax.while_loop(
        lambda state: state[0] < rounds, more_rows, (jnp.int32(1), token_rows)
    )

    is_valid = (order[None, :] < live_lengths[:, None]) & (key_keep == 1)
    key_ok = is_valid.reshape(win_count, 1, 1, 1, WINDOW)
    bucket_ids = buckets.reshape(win_count, 1, WINDOW)
    same_bucket = bucket_ids[:, :, None, :, None] == bucket_ids[:, :, None, None, :]
    allowed = same_bucket & key_ok | jnp.eye(WINDOW, dtype=bool)
    embedded = (token_rows + place_all).reshape(win_count, WINDOW, D)
    hidden, embed_pull = jax.vjp(layer_norm, embedded, vectors[0], vectors[1])
    params = (
        attn_low[0],
        attn_low[1],
        attn_low[2],
        attn_low[3],
        ffn_low[0],
        ffn_low[1],
        up_biases[0],
        vectors[2:10],
    )
    hidden, stored = layer_forward(hidden, params, allowed)
    picks = mask_pos.reshape(-1)
    head_in = select_rows(picks, hidden.reshape(WINDOW, D).astype(jnp.bfloat16))
    head_in = head_in.astype(jnp.bfloat16)
    head_pre = jnp.dot(head_in, head_weight, preferred_element_type=jnp.float32) + vectors[NV - 3]
    head_out, head_pull = jax.vjp(head_tail, head_pre, vectors[NV - 2], vectors[NV - 1])
    head_low = head_out.astype(jnp.bfloat16)

    rows_all = devices * MPW
    side = lax.axis_index("side").astype(jnp.int32)
    here = here16().astype(jnp.int32)
    order_rows = jnp.arange(devices, dtype=jnp.int32)
    rank_of_dev = (order_rows % 2 ^ side) * group + (order_rows // 2 ^ here)
    dev_of_rank = (order_rows % group ^ here) * 2 + (order_rows // group ^ side)
    head_all = gather_relative(head_low, wide_count, 1, lanes)
    head_all = jnp.concatenate([head_all, exchange(head_all, side_bit)]).reshape(rows_all, D)
    labels_all = pick_rows(labels_all.reshape(devices, MPW), dev_of_rank).reshape(rows_all, 1)
    is_live = jnp.arange(MPW, dtype=jnp.int32)[None, :] < pick_rows(counts_all[:, None], dev_of_rank)
    word_ids = device * owned + jnp.arange(owned, dtype=jnp.int32)
    is_word = (word_ids < V)[None, :]
    logits = jnp.einsum("rd,vd->rv", head_all, table_low, preferred_element_type=jnp.float32)
    logits = jnp.where(is_word, logits + dec_bias[None, :], masked_fill)
    top_here = jnp.max(logits, axis=1)
    sum_here = jnp.sum(jnp.exp(logits - top_here[:, None]), axis=1)
    stats = jnp.concatenate(
        [
            top_here.reshape(devices, MPW),
            sum_here.reshape(devices, MPW),
            jnp.zeros((devices, 2 * lanes - 2 * MPW), jnp.float32),
        ],
        axis=1,
    )
    stats, source_here = lax.optimization_barrier((stats, source_here))
    stats = swap_all(pick_rows(stats, rank_of_dev))
    tops = stats[:, :MPW]
    top = jnp.max(tops, axis=0)
    total = top + jnp.log(jnp.sum(stats[:, MPW : 2 * MPW] * jnp.exp(tops - top[None]), axis=0))
    totals = spread(jnp.concatenate([total, source_total]), devices)
    totals = pick_rows(totals, dev_of_rank)
    row_facts = jnp.concatenate(
        [
            totals[:, :MPW].reshape(rows_all, 1),
            totals[:, MPW:].reshape(rows_all, 1),
            is_live.reshape(rows_all, 1).astype(jnp.float32),
            labels_all.astype(jnp.float32),
        ],
        axis=1,
    )
    place_facts = jnp.stack([device * owned, here, side]).astype(jnp.int32)
    grad_logits, losses, grad_dec = logit_grads(
        place_facts, logits, source_here, row_facts, devices
    )
    loss_part = jnp.sum(losses)
    give = jnp.dot(grad_logits[rows_all // 2 :], table_low, preferred_element_type=jnp.float32)
    got = exchange(give, side_bit)
    keep = jnp.dot(grad_logits[: rows_all // 2], table_low, preferred_element_type=jnp.float32)
    grad_head_out = reduce_rows((keep + got).reshape(group, MPW, D), wide_count)
    grad_words = jnp.einsum("rv,rd->vd", grad_logits, head_all, preferred_element_type=jnp.float32)
    grad_head_out, grad_words = lax.optimization_barrier((grad_head_out, grad_words))

    grad_pre, grad_head_gain, grad_head_shift = head_pull(grad_head_out)
    pre_low = grad_pre.astype(jnp.bfloat16)
    grad_head_w = jnp.einsum("rd,rf->df", head_in, pre_low, preferred_element_type=jnp.float32)
    grad_head_in = jnp.einsum("rf,df->rd", pre_low, head_weight, preferred_element_type=jnp.float32)
    grad_hidden = add_rows(picks, grad_head_in, WINDOW).reshape(win_count, WINDOW, D)
    grad_hidden, layer_mats, up_grad, vec_grads = layer_backward(
        grad_hidden, stored, params, allowed
    )
    grad_embed, grad_emb_gain, grad_emb_shift = embed_pull(grad_hidden)
    flat_embed = grad_embed.reshape(WINDOW, D)

    ffn_parts, attn_parts = layer_mats[1], layer_mats[0]
    flat_embed, ffn_parts = tied(flat_embed, ffn_parts)
    ffn_grad = jnp.concatenate(ffn_parts, axis=1)
    dec_block = jnp.zeros((devices * owned,), jnp.float32)
    dec_block = lax.dynamic_update_slice(dec_block, grad_dec, (device * owned,))[:V]
    vector_block = jnp.concatenate(
        [jnp.stack([grad_emb_gain, grad_emb_shift])]
        + [vec_grads]
        + [jnp.stack([jnp.sum(pre_low.astype(jnp.float32), 0), grad_head_gain, grad_head_shift])],
        axis=0,
    )
    front = jnp.concatenate(
        [
            dec_block.reshape(-1, lanes),
            up_grad.reshape(2, devices // 2, ffn_width).transpose(1, 0, 2).reshape(-1, lanes),
            vector_block.reshape(-1, lanes),
        ]
    )
    other_grad = scatter_flat(front, grad_head_w.reshape(-1, lanes), size, device, devices)

    place_grad = flat_embed.reshape(per_place, group, D).transpose(1, 0, 2)
    place_grad = place_grad.reshape(wide_count, narrow_count // 2, per_place, D)
    place_grad = reduce_blocks(place_grad, wide_count, 1, 128)
    place_grad, attn_parts = tied(place_grad, attn_parts)
    attn_grad = jnp.concatenate(reduce_relative(attn_parts, wide_count), axis=1)
    sent = add_rows(now, flat_embed, devices * slots) + add_rows(held, place_grad, devices * slots)
    arrived = swap_all(sent.reshape(devices, slots, D)).reshape(-1, D)
    table_grad = grad_words + add_rows(asked, arrived, owned)

    def more_grads(state):
        round_idx, grads = state
        addresses = address(round_idx)
        asked_rows = ask_again(addresses)
        sent = add_rows(addresses, flat_embed, devices * slots)
        arrived = swap_all(sent.reshape(devices, slots, D)).reshape(-1, D)
        return (round_idx + 1, grads + add_rows(asked_rows, arrived, owned))

    _, table_grad = lax.while_loop(
        lambda state: state[0] < rounds, more_grads, (jnp.int32(1), table_grad)
    )

    squares = square_sum((table_grad, attn_grad, ffn_grad, other_grad))
    sums = jnp.sum(spread(jnp.stack([squares, loss_part]), devices), axis=0)
    grad_norm = jnp.sqrt(sums[0]) / masked_total
    loss_value = sums[1] / masked_total
    factor = jnp.minimum(1.0, clip_limit / grad_norm)
    scaling = factor / masked_total

    attn_moment_new = mu_muon * attn_moment + attn_grad * scaling
    ffn_moment_new = mu_muon * ffn_moment + ffn_grad * scaling
    second = lax.axis_index("side") == 1
    keep = jnp.where(second, ffn_moment_new[1], ffn_moment_new[0])
    got = exchange(jnp.where(second, ffn_moment_new[0], ffn_moment_new[1]), side_bit)
    ffn_pair = jnp.concatenate([keep, got], axis=1)[None]
    attn_found = gather_columns(attn_moment_new, False)
    ffn_found = gather_columns(ffn_pair, True)
    attn_new = muon_cols(attn_mats, attn_moment_new, gram_of(attn_found), D)
    ffn_turn = newton_cols(ffn_pair, gram_of(ffn_found))[0]
    keep, give = ffn_turn[:, :ffn_width], ffn_turn[:, ffn_width:]
    got = exchange(give, side_bit)
    ffn_turn = jnp.stack([jnp.where(second, got, keep), jnp.where(second, keep, got)])
    ffn_new = ffn_mats - lr_muon * muon_shape * math.sqrt(max(D, FF)) * ffn_turn
    embed_new, embed_first_new, embed_second_new = adam_step(
        embed_table, embed_first, embed_second, table_grad * scaling
    )
    other_new, other_first_new, other_second_new = adam_step(
        other_params, other_first, other_second, other_grad * scaling
    )
    return (
        loss_value,
        grad_norm,
        embed_new,
        embed_first_new,
        embed_second_new,
        attn_new,
        attn_moment_new,
        ffn_new,
        ffn_moment_new,
        other_new,
        other_first_new,
        other_second_new,
    )


def solution(mesh):
    wide_count, narrow_count = mesh.shape["wide"], mesh.shape["narrow"]
    assert narrow_count % 2 == 0
    split = Mesh(
        np.asarray(mesh.devices).reshape(wide_count, narrow_count // 2, 2), everyone
    )
    rows, narrow = P(everyone), ("pair", "side")
    attn_spec, ffn_spec = P(narrow, None, "wide"), P(None, None, everyone)
    in_specs = (rows,) * 11 + (attn_spec,) * 2 + (ffn_spec,) * 2 + (rows,) * 3
    out_specs = (P(), P()) + (rows,) * 3 + (attn_spec,) * 2 + (ffn_spec,) * 2 + (rows,) * 3

    return jax.shard_map(
        shards, mesh=split, in_specs=in_specs, out_specs=out_specs, check_vma=False
    )
```

```python
import functools
import math

import jax
import jax.numpy as jnp
import numpy as np
from jax import lax
from jax.experimental import pallas as pl
from jax.experimental.pallas import tpu as pltpu
from jax.sharding import Mesh
from jax.sharding import PartitionSpec as P

D = 1024
FF = 4096
HEADS = 16
L = 1
V = 30720
SEQ = 1024
WINDOW = 512
NS_ITERS = 3
ADAM_STEP = 5
MPW = 80
NV = 13


high = lax.Precision.HIGH
lanes = 128
tile = 16
slots = 32
ln_eps = 1e-05
masked_fill = -1e30
clip_limit = 0.3
ns_a = 3.4445
ns_b = -4.775
ns_c = 2.0315
mu_muon = 0.95
lr_muon = 0.1
muon_shape = 0.2
lr_adam = 0.01
beta_one = 0.9
beta_two = 0.999
adam_eps = 1e-08


def layer_norm(inputs, gain_vec, shift_vec):
    center = inputs - jnp.mean(inputs, -1, keepdims=True)
    spread = jnp.mean(center * center, -1, keepdims=True)
    return center * lax.rsqrt(spread + ln_eps) * gain_vec + shift_vec


def exact_gelu(inputs):
    return jax.nn.gelu(inputs, approximate=False)


def head_tail(head_pre, gain_vec, shift_vec):
    return layer_norm(exact_gelu(head_pre), gain_vec, shift_vec)


def project(inputs, weight):
    return jnp.einsum("bsd,df->bsf", inputs, weight, preferred_element_type=jnp.float32)


def project_back(gradients, weight):
    return jnp.einsum("bsf,df->bsd", gradients, weight, preferred_element_type=jnp.float32)


def col_sum(inputs):
    return jnp.sum(inputs.astype(jnp.float32), axis=(0, 1))


def to_heads(inputs):
    return inputs.reshape(
        inputs.shape[0], inputs.shape[1] // WINDOW, WINDOW, HEADS, inputs.shape[2] // HEADS
    )


def attn_scores(queries, key_proj, allowed):
    raw_scores = jnp.einsum(
        "bnqhe,bnkhe->bnhqk",
        to_heads(queries),
        to_heads(key_proj),
        preferred_element_type=jnp.float32,
    )
    return jnp.where(allowed, raw_scores * (queries.shape[2] // HEADS) ** (-0.5), masked_fill)


def share(values, axis):
    return jnp.concatenate([values, exchange(values, side_bit)], axis=axis)


def swap_pick(for_first, for_second, axis):
    first = lax.axis_index("side") == 0
    keep = jnp.where(first, for_first, for_second)
    got = exchange(jnp.where(first, for_second, for_first), side_bit)
    return jnp.concatenate([keep, got], axis=axis)


def share_half(values):
    side = lax.axis_index("side")
    half = values.shape[1] // 2
    keep = lax.dynamic_slice_in_dim(values, side * half, half, axis=1)
    got = exchange(lax.dynamic_slice_in_dim(values, (1 - side) * half, half, axis=1), side_bit)
    return jnp.concatenate([keep, got])


def layer_forward(hidden, params, allowed):
    w_query, w_key, w_value, w_out, w_up, w_down, up_bias, vectors = params
    count, length, model_width = hidden.shape
    inputs = hidden.astype(jnp.bfloat16)
    queries = (project(inputs, w_query) + vectors[4]).astype(jnp.bfloat16)
    key_proj = project(inputs, w_key).astype(jnp.bfloat16)
    values = (project(inputs, w_value) + vectors[5]).astype(jnp.bfloat16)
    scores = attn_scores(queries, key_proj, allowed)
    log_total = jax.nn.logsumexp(scores, axis=-1, keepdims=True)
    prob_low = jnp.exp(scores - log_total).astype(jnp.bfloat16)
    context = jnp.einsum(
        "bnhqk,bnkhe->bnqhe", prob_low, to_heads(values), preferred_element_type=jnp.float32
    )
    context = context.reshape(count, length, model_width).astype(jnp.bfloat16)
    attn_sum = hidden + (project(context, w_out) + vectors[6])
    middle, first_pull = jax.vjp(layer_norm, attn_sum, vectors[0], vectors[1])
    middle_low = middle.astype(jnp.bfloat16)
    up_proj = project(middle_low, w_up) + up_bias
    activated, gelu_pull = jax.vjp(exact_gelu, up_proj)
    act_low = activated.astype(jnp.bfloat16)
    ffn_sum = middle + (project_back(act_low, w_down) + vectors[7])
    output, second_pull = jax.vjp(layer_norm, ffn_sum, vectors[2], vectors[3])
    stored = (
        inputs,
        queries,
        key_proj,
        values,
        log_total,
        context,
        first_pull,
        middle_low,
        gelu_pull,
        act_low,
        second_pull,
    )
    shared = (
        share(middle_low[0].T, 1),
        share_half(act_low[0]),
        share(inputs[0].T, 1),
        swap_pick(inputs[0].T, context[0].T, 1),
    )
    return (output, stored, shared)


def layer_backward(grad_out, stored, shared, params, allowed):
    w_query, w_key, w_value, w_out, w_up, w_down, _, _ = params
    (_, queries, key_proj, values, log_total, _, first_pull, _, gelu_pull, _, second_pull) = stored
    count, length, model_width = grad_out.shape
    grad_ffn, grad_gain_two, grad_shift_two = second_pull(grad_out)
    down_low = grad_ffn.astype(jnp.bfloat16)
    (grad_up,) = gelu_pull(project(down_low, w_down))
    up_low = grad_up.astype(jnp.bfloat16)
    wide_count = lax.axis_size("wide")
    operands = (
        shared[0],
        share(down_low[0].T, 1),
        share_half(up_low[0]),
        shared[1],
    )
    if FF // (4 * wide_count) == lanes:
        grad_mats_ffn = ffn_weight_grads(*operands, wide_count)
    else:
        blocks = jnp.stack([jnp.dot(*operands[::2], preferred_element_type=jnp.float32),
                            jnp.dot(*operands[1::2], preferred_element_type=jnp.float32)])
        blocks = blocks.reshape(2, D, wide_count, 2, -1).transpose(2, 3, 0, 1, 4)
        grad_mats_ffn = in_routes(blocks, wide_count)
    grad_ffn, parts = tied(grad_ffn, grad_mats_ffn)
    parts = reduce_step(parts, wide_count, 0)
    grad_middle = grad_ffn + project_back(up_low, w_up)
    grad_attn, grad_gain_one, grad_shift_one = first_pull(grad_middle)
    attn_low = grad_attn.astype(jnp.bfloat16)
    grad_context = to_heads(project_back(attn_low, w_out).astype(jnp.bfloat16))
    attn_prob = jnp.exp(attn_scores(queries, key_proj, allowed) - log_total)
    prob_low = attn_prob.astype(jnp.bfloat16)
    grad_prob = jnp.einsum(
        "bnqhe,bnkhe->bnhqk", grad_context, to_heads(values), preferred_element_type=jnp.float32
    )
    grad_value = jnp.einsum(
        "bnhqk,bnqhe->bnkhe", prob_low, grad_context, preferred_element_type=jnp.float32
    )
    grad_value = grad_value.reshape(count, length, model_width).astype(jnp.bfloat16)
    grad_scores = attn_prob * (grad_prob - jnp.sum(grad_prob * attn_prob, -1, keepdims=True))
    grad_raw = (grad_scores * (model_width // HEADS) ** (-0.5)).astype(jnp.bfloat16)
    late_keys, parts = tied(key_proj, parts)
    parts = reduce_step(parts, wide_count, 1)
    grad_query = jnp.einsum(
        "bnhqk,bnkhe->bnqhe", grad_raw, to_heads(late_keys), preferred_element_type=jnp.float32
    )
    grad_query = grad_query.reshape(count, length, model_width).astype(jnp.bfloat16)
    grad_key = jnp.einsum(
        "bnhqk,bnqhe->bnkhe", grad_raw, to_heads(queries), preferred_element_type=jnp.float32
    )
    grad_key = grad_key.reshape(count, length, model_width).astype(jnp.bfloat16)
    grad_query, parts = tied(grad_query, parts)
    parts = reduce_step(parts, wide_count, 2)
    grad_hidden = (
        grad_attn
        + project_back(grad_query, w_query)
        + project_back(grad_key, w_key)
        + project_back(grad_value, w_value)
    )
    grad_hidden, parts = tied(grad_hidden, parts)
    for step in range(3, len(routes(wide_count)[0])):
        parts = reduce_step(parts, wide_count, step)
    operands = (
        shared[2],
        shared[3],
        swap_pick(grad_query[0], grad_key[0], 0),
        swap_pick(grad_value[0], attn_low[0], 0),
    )
    if D // wide_count == lanes:
        grad_mats_attn = attn_weight_grads(*operands, wide_count)
    else:
        blocks = jnp.stack([jnp.dot(*operands[::2], preferred_element_type=jnp.float32),
                            jnp.dot(*operands[1::2], preferred_element_type=jnp.float32)])
        blocks = blocks.reshape(2, 1, D, wide_count, -1).transpose(3, 0, 1, 2, 4)
        grad_mats_attn = in_routes(blocks, wide_count)
    matrices = (grad_mats_attn, parts)
    vector_grads = jnp.stack(
        [
            grad_gain_one,
            grad_shift_one,
            grad_gain_two,
            grad_shift_two,
            col_sum(grad_query),
            col_sum(grad_value),
            col_sum(attn_low),
            col_sum(down_low),
        ]
    )
    return (grad_hidden, matrices, col_sum(up_low), vector_grads)


def slab_product(matrix, columns):
    return jnp.einsum(
        "kde,kec->kdc", matrix, columns, precision=high, preferred_element_type=jnp.float32
    )


def newton_cols(moment, gram):
    norms = jnp.sqrt(jnp.trace(gram, axis1=1, axis2=2))
    scaling = 1.0 / (norms + 1e-07)
    current = moment * scaling[:, None, None]
    gram = gram * (scaling * scaling)[:, None, None]
    for step_idx in range(NS_ITERS):
        if step_idx + 1 < NS_ITERS:
            poly = ns_b * gram + ns_c * jnp.einsum("kde,kef->kdf", gram, gram)
            current = ns_a * current + slab_product(poly, current)
            half = ns_a * gram + jnp.einsum("kde,kef->kdf", poly, gram)
            gram = ns_a * half + jnp.einsum("kde,kef->kdf", half, poly)
        else:
            once = slab_product(gram, current)
            current = ns_a * current + ns_b * once + ns_c * slab_product(gram, once)
    return current


def gram_of(found):
    return jnp.einsum("wdc,wec->de", found, found, preferred_element_type=jnp.float32)[None]


def relative_order(part, taken):
    names = [bit for bit in wide_bits(lax.axis_size("wide"))[::-1] + [("pair", 1)] if bit in taken]
    dims = [names.index(bit) for bit in taken[::-1]]
    split = part.reshape((2,) * len(taken) + part.shape[1:])
    turn = [dims.index(place) for place in range(len(taken))]
    split = split.transpose(turn + list(range(len(taken), split.ndim)))
    return split.reshape(part.shape)


def muon_cols(master, new_moment, gram, long_side):
    change = lr_muon * muon_shape * math.sqrt(long_side) * newton_cols(new_moment, gram)
    return master - change


def adam_step(master, first_moment, second, gradient):
    new_first = beta_one * first_moment + (1.0 - beta_one) * gradient
    new_second = beta_two * second + (1.0 - beta_two) * gradient * gradient
    first_hat = new_first / (1.0 - beta_one**ADAM_STEP)
    second_hat = new_second / (1.0 - beta_two**ADAM_STEP)
    return (master - lr_adam * first_hat / (jnp.sqrt(second_hat) + adam_eps), new_first, new_second)


def square_sum(arrays):
    running = jnp.zeros((), jnp.float32)
    for member in arrays:
        running = running + jnp.sum(member * member)
    return running


everyone = ("wide", "pair", "side")
side_bit = ("side", 1)


def swap_all(blocks, axes=everyone):
    return lax.all_to_all(blocks, axes, 0, 0, tiled=True)


def spread(values, devices):
    size = values.shape[0]
    row = jnp.pad(values, (0, -size % lanes))
    return swap_all(jnp.broadcast_to(row[None], (devices, row.shape[0])))[:, :size]


def wide_bits(wide_count):
    return [("wide", 1 << k) for k in range(wide_count.bit_length() - 1)]


def routes(wide_count, with_pair=True):
    bits = wide_bits(wide_count)
    near, far, across = bits[:1], bits[1:], [("pair", 1)] if with_pair else []
    return [across + near + far, near + far + across, far + across + near]


def my_bit(bit):
    axis, mask = bit
    return lax.axis_index(axis) // mask % 2


def exchange(values, bit):
    axis, mask = bit
    steps = [(here, here ^ mask) for here in range(lax.axis_size(axis))]
    return lax.ppermute(values, axis, steps)


def halve(values, bit, dim):
    mine = lax.dynamic_index_in_dim(values, my_bit(bit), dim, keepdims=False)
    theirs = lax.dynamic_index_in_dim(values, 1 - my_bit(bit), dim, keepdims=False)
    return mine + exchange(theirs, bit)


def double(values, bit, dim):
    theirs = exchange(values, bit)
    first = my_bit(bit) == 0
    pair = [jnp.where(first, values, theirs), jnp.where(first, theirs, values)]
    return jnp.stack(pair, axis=dim)


def cuts(length, unit):
    whole = length // unit
    sizes = [(whole + 2) // 3 * unit, (whole + 1) // 3 * unit]
    sizes.append(length - sum(sizes))
    starts = [0, sizes[0], sizes[0] + sizes[1]]
    return [(start, start + size) for start, size in zip(starts, sizes) if size]


def here16():
    return lax.axis_index("wide") * 2 + lax.axis_index("pair")


def lockstep(*groups):
    flat = lax.optimization_barrier(sum((list(group) for group in groups), []))
    found = []
    for group in groups:
        found.append(flat[: len(group)])
        flat = flat[len(group) :]
    return found


def reduce_step(parts, wide_count, step):
    return [
        part[0] + exchange(part[1], route[step])
        for part, route in zip(parts, routes(wide_count))
    ]


def tied(value, parts):
    value, *parts = lax.optimization_barrier((value, *parts))
    return value, parts


def static_step(part, left, bit):
    dim = left.index(bit)
    keep = lax.index_in_dim(part, 0, dim, keepdims=False)
    return keep + exchange(lax.index_in_dim(part, 1, dim, keepdims=False), bit)


def route_parts(values, wide_count):
    bits = wide_bits(wide_count)[::-1] + [("pair", 1)]
    return [
        values[..., start:stop].reshape((2,) * len(bits) + (values.shape[1], stop - start))
        for start, stop in cuts(values.shape[-1], lanes)
    ]


def route_step(parts, wide_count, step, static):
    bits = wide_bits(wide_count)[::-1] + [("pair", 1)]
    found = []
    for part, route in zip(parts, routes(wide_count)):
        left = [bit for bit in bits if bit not in route[:step]]
        if static:
            found.append(static_step(part, left, route[step]))
        else:
            found.append(halve(part, route[step], left.index(route[step])))
    return found


def reduce_rows(values, wide_count):
    parts = route_parts(values, wide_count)
    for step in range(len(routes(wide_count)[0])):
        (parts,) = lockstep(route_step(parts, wide_count, step, True))
    return jnp.concatenate(parts, axis=-1)


def gather_start(block, axis, unit):
    return [
        lax.slice_in_dim(block, start, stop, axis=axis)[None]
        for start, stop in cuts(block.shape[axis], unit)
    ]


def gather_step(parts, wide_count, step, with_pair=True):
    return [
        jnp.concatenate([part, exchange(part, route[::-1][step])])
        for part, route in zip(parts, routes(wide_count, with_pair))
    ]


def gather_end(parts, wide_count, axis, with_pair=True):
    ordered = [
        relative_order(part, route[::-1])
        for part, route in zip(parts, routes(wide_count, with_pair))
    ]
    return jnp.concatenate(ordered, axis=1 + axis)


def gather_relative(block, wide_count, axis, unit):
    parts = gather_start(block, axis, unit)
    for step in range(len(routes(wide_count)[0])):
        (parts,) = lockstep(gather_step(parts, wide_count, step))
    return gather_end(parts, wide_count, axis)


def route_shape(route, covered):
    wide = [bit for bit in route if bit not in covered]
    shape = tuple(2 if bit in covered else 1 for bit in route)

    def index(step):
        low = 1 << len(covered) - 1
        return tuple(
            0 if bit in covered else step * low // bit[1] % 2 for bit in route
        )

    assert wide
    return shape, index


def weight_grads(kernel, operands, column_specs, covered, steps, members, wide_count):
    here = jnp.stack([lax.axis_index("wide"), lax.axis_index("pair")]).astype(jnp.int32)
    shapes, specs = [], []
    for route, (start, stop) in zip(routes(wide_count), cuts(D, tile)):
        block, index = route_shape(route, covered)
        tail = (members, stop - start, lanes)
        shapes.append(jax.ShapeDtypeStruct((2,) * len(route) + tail, jnp.float32))
        specs.append(
            pl.BlockSpec(block + tail, lambda step, _, index=index: index(step) + (0, 0, 0))
        )
    return pl.pallas_call(
        kernel,
        grid_spec=pltpu.PrefetchScalarGridSpec(
            num_scalar_prefetch=1, grid=(steps,), in_specs=column_specs, out_specs=specs
        ),
        out_shape=shapes,
    )(here, *operands)


def put(refs, wide_count, covered, where, member, values):
    for ref, route, (start, stop) in zip(refs, routes(wide_count), cuts(D, tile)):
        place = tuple(where[bit] if bit in covered else 0 for bit in route)
        ref[place + (member,)] = values[start:stop]


def ffn_grads_kernel(here, up_rows, down_rows, up_cols, down_cols, *refs, wide_count):
    flip = here[1] == 0
    pair = ("pair", 1)
    for member, (rows, cols) in enumerate(((up_rows, up_cols), (down_rows, down_cols))):
        both = jnp.dot(rows[...], cols[...], preferred_element_type=jnp.float32)
        low, top = both[:, :lanes], both[:, lanes:]
        put(refs, wide_count, [pair], {pair: 0}, member, jnp.where(flip, low, top))
        put(refs, wide_count, [pair], {pair: 1}, member, jnp.where(flip, top, low))


def ffn_weight_grads(up_rows, down_rows, up_cols, down_cols, wide_count):
    whole = pl.BlockSpec(up_rows.shape, lambda step, here: (0, 0))
    cols = pl.BlockSpec((up_cols.shape[0], 2 * lanes), lambda step, here: (0, step ^ here[0]))
    kernel = functools.partial(ffn_grads_kernel, wide_count=wide_count)
    operands = (up_rows, down_rows, up_cols, down_cols)
    specs = [whole, whole, cols, cols]
    return weight_grads(kernel, operands, specs, [("pair", 1)], wide_count, 2, wide_count)


def attn_grads_kernel(here, one_rows, two_rows, one_cols, two_cols, *refs, wide_count):
    swap = here[0] % 2 == 0
    flip = here[1] == 0
    pair, near = ("pair", 1), ("wide", 1)
    blocks = []
    for rows, cols in ((one_rows, one_cols), (two_rows, two_cols)):
        both = jnp.dot(rows[...], cols[...], preferred_element_type=jnp.float32)
        low, top = both[:, :lanes], both[:, lanes:]
        blocks.append((jnp.where(swap, low, top), jnp.where(swap, top, low)))
    for step in range(2):
        one, two = blocks[0][step], blocks[1][step]
        first, second = jnp.where(flip, one, two), jnp.where(flip, two, one)
        put(refs, wide_count, [pair, near], {pair: 0, near: step}, 0, first)
        put(refs, wide_count, [pair, near], {pair: 1, near: step}, 0, second)


def attn_weight_grads(one_rows, two_rows, one_cols, two_cols, wide_count):
    whole = pl.BlockSpec(one_rows.shape, lambda step, here: (0, 0))
    cols = pl.BlockSpec((one_cols.shape[0], 2 * lanes), lambda step, here: (0, step ^ here[0] // 2))
    kernel = functools.partial(attn_grads_kernel, wide_count=wide_count)
    operands = (one_rows, two_rows, one_cols, two_cols)
    specs = [whole, whole, cols, cols]
    covered = [("pair", 1), ("wide", 1)]
    return weight_grads(kernel, operands, specs, covered, wide_count // 2, 1, wide_count)


def in_routes(blocks, wide_count):
    count = wide_count * 2
    order = jnp.arange(count) ^ here16()
    blocks = jnp.take(blocks.reshape((count,) + blocks.shape[2:]), order, axis=0)
    bits = wide_bits(wide_count)[::-1] + [("pair", 1)]
    parts = []
    for route, (start, stop) in zip(routes(wide_count), cuts(D, tile)):
        part = blocks[:, :, start:stop].reshape((2,) * len(bits) + blocks[:, :, start:stop].shape[1:])
        dims = [bits.index(bit) for bit in route]
        parts.append(part.transpose(dims + list(range(len(bits), part.ndim))))
    return parts


def gather_blocks(block, wide_count, axis, unit):
    bits = wide_bits(wide_count)[::-1] + [("pair", 1)]
    parts = []
    for route, (start, stop) in zip(routes(wide_count), cuts(block.shape[axis], unit)):
        part = lax.slice_in_dim(block, start, stop, axis=axis)
        have = []
        for bit in route[::-1]:
            have = sorted(have + [bit], key=bits.index)
            part = double(part, bit, have.index(bit))
        parts.append(part.reshape((wide_count, 2) + part.shape[len(bits) :]))
    return jnp.concatenate(parts, axis=2 + axis)


def select_rows(index, rows, precision=None):
    hits = index[:, None] == jnp.arange(rows.shape[0], dtype=jnp.int32)[None, :]
    return jnp.dot(
        hits.astype(rows.dtype), rows, precision=precision, preferred_element_type=jnp.float32
    )


def logit_grads_kernel(facts, logits_ref, source_ref, rows_ref, grad_ref, loss_ref, dec_ref):
    step = pl.program_id(0)

    @pl.when(step == 0)
    def _():
        loss_ref[...] = jnp.zeros_like(loss_ref)
        dec_ref[...] = jnp.zeros_like(dec_ref)

    columns = lax.broadcasted_iota(jnp.int32, logits_ref.shape, 1) + facts[0]
    is_word = columns < V
    rows = rows_ref[...]
    log_prob = logits_ref[...] - rows[:, 0:1]
    source_log = source_ref[0].astype(jnp.float32) - rows[:, 1:2]
    source_prob = jnp.where(is_word, jnp.exp(source_log), 0.0)
    hits = columns == rows[:, 3:4].astype(jnp.int32)
    keep = is_word & (rows[:, 2:3] > 0.5)
    losses = source_prob * (source_log - log_prob) - jnp.where(hits, log_prob, 0.0)
    loss_ref[...] += jnp.sum(jnp.where(keep, losses, 0.0), axis=0, keepdims=True)
    grads = 2.0 * jnp.exp(log_prob) - jnp.where(hits, 1.0, 0.0) - source_prob
    grads = jnp.where(keep, grads, 0.0).astype(jnp.bfloat16)
    grad_ref[...] = grads
    dec_ref[...] += jnp.sum(grads.astype(jnp.float32), axis=0, keepdims=True)


def logit_grads(facts, logits, source, row_facts, devices):
    owned = logits.shape[1]
    group = devices // 2

    def source_block(step, facts):
        return ((step % group ^ facts[1]) * 2 + (step // group ^ facts[2]), 0, 0)

    line = pl.BlockSpec((1, owned), lambda step, facts: (0, 0))
    grads, losses, dec = pl.pallas_call(
        logit_grads_kernel,
        grid_spec=pltpu.PrefetchScalarGridSpec(
            num_scalar_prefetch=1,
            grid=(devices,),
            in_specs=[
                pl.BlockSpec((MPW, owned), lambda step, facts: (step, 0)),
                pl.BlockSpec((1, MPW, owned), source_block),
                pl.BlockSpec((MPW, 4), lambda step, facts: (step, 0)),
            ],
            out_specs=[pl.BlockSpec((MPW, owned), lambda step, facts: (step, 0)), line, line],
        ),
        out_shape=[
            jax.ShapeDtypeStruct(logits.shape, jnp.bfloat16),
            jax.ShapeDtypeStruct((1, owned), jnp.float32),
            jax.ShapeDtypeStruct((1, owned), jnp.float32),
        ],
    )(facts, logits, source, row_facts)
    return grads, losses, dec[0]


def pick_rows(values, index):
    hits = index[:, None] == jnp.arange(values.shape[0], dtype=jnp.int32)[None, :]
    return jnp.sum(jnp.where(hits[:, :, None], values[None], 0), axis=1)


def add_rows(index, rows, count):
    hits = jnp.arange(count, dtype=jnp.int32)[:, None] == index[None, :]
    return jnp.dot(
        hits.astype(rows.dtype), rows, precision=high, preferred_element_type=jnp.float32
    )


def position_plan(devices, owned):
    group = devices // 2
    place = np.arange(SEQ)
    owner = (V + place) // owned
    target = 2 * (place % WINDOW % group) + place // WINDOW
    rank = np.zeros(SEQ, np.int64)
    seen = {}
    for p in range(SEQ):
        pair = (owner[p], target[p])
        rank[p] = seen.get(pair, 0)
        seen[pair] = rank[p] + 1
    assert rank.max() < slots
    return owner, target, rank


def flat_blocks(size, devices):
    total = size * devices
    starts = [dev * size // (tile * lanes) * tile for dev in range(devices)] + [total // lanes]
    ends = [-(-(dev + 1) * size // (tile * lanes)) * tile for dev in range(devices)]
    rows = max(end - start for start, end in zip(starts, ends))
    return starts, rows


def place_flat(share, device, devices):
    size = share.shape[0]
    _, rows = flat_blocks(size, devices)
    offset = device * size % (tile * lanes)
    block = lax.dynamic_update_slice(jnp.zeros((rows * lanes,), share.dtype), share, (offset,))
    return block.reshape(rows, lanes)


def join_kernel(blocks_ref, out_ref, *, starts):
    rows = blocks_ref.shape[1]
    for dev in range(len(starts) - 1):
        length = starts[dev + 1] - starts[dev]
        out_ref[starts[dev] : starts[dev + 1]] = blocks_ref[dev, :length]
    for dev in range(1, len(starts) - 1):
        length = starts[dev] - starts[dev - 1]
        if length < rows:
            shared = slice(starts[dev], starts[dev] + tile)
            both = blocks_ref[dev, :tile].astype(jnp.float32)
            both += blocks_ref[dev - 1, length : length + tile].astype(jnp.float32)
            out_ref[shared] = both.astype(out_ref.dtype)


def join_flat(blocks, size):
    starts, _ = flat_blocks(size, blocks.shape[0])
    starts[-1] += -starts[-1] % tile
    return pl.pallas_call(
        functools.partial(join_kernel, starts=starts),
        out_shape=jax.ShapeDtypeStruct((starts[-1], lanes), blocks.dtype),
    )(blocks)


def unpack_kernel(*refs):
    half = len(refs) * 2 // 3
    for place, out_ref in enumerate(refs[half:]):
        out_ref[:, :lanes] = refs[2 * place][...].reshape(D, lanes)
        out_ref[:, lanes:] = refs[2 * place + 1][...].reshape(D, lanes)


def unpack_attn(merged, wide_count, narrow_count):
    specs = [
        pl.BlockSpec((1, D, lanes), lambda step, add=step_add, kind=kind: (
            (2 * step + add) * narrow_count + kind, 0, 0
        ))
        for kind in range(narrow_count)
        for step_add in range(2)
    ]
    return pl.pallas_call(
        unpack_kernel,
        grid=(wide_count // 2,),
        in_specs=specs,
        out_specs=[pl.BlockSpec((D, 2 * lanes), lambda step: (0, step))] * narrow_count,
        out_shape=[jax.ShapeDtypeStruct((D, D), merged.dtype)] * narrow_count,
    )(*[merged] * len(specs))


def unpack_ffn(blocks, wide_count):
    specs = [
        pl.BlockSpec((1, 1, D, lanes), lambda step, kind=kind, pair=pair: (
            step % wide_count * 4 + pair * 2 + step // wide_count, kind, 0, 0
        ))
        for kind in range(2)
        for pair in range(2)
    ]
    return pl.pallas_call(
        unpack_kernel,
        grid=(2 * wide_count,),
        in_specs=specs,
        out_specs=[pl.BlockSpec((D, 2 * lanes), lambda step: (0, step))] * 2,
        out_shape=[jax.ShapeDtypeStruct((D, FF), blocks.dtype)] * 2,
    )(*[blocks] * 4)


def split_kernel(front_ref, rest_ref, out_ref, *, starts):
    front, rows = front_ref.shape[0], out_ref.shape[1]
    total = front + rest_ref.shape[0]
    for dev, start in enumerate(starts[:-1]):
        stop = min(start + rows, total)
        middle = min(max(start, front), stop)
        if start < middle:
            out_ref[dev, : middle - start] = front_ref[start:middle]
        if middle < stop:
            out_ref[dev, middle - start : stop - start] = rest_ref[middle - front : stop - front]
        if stop < start + rows:
            left = start + rows - stop
            out_ref[dev, rows - left :] = jnp.zeros((left, lanes), out_ref.dtype)


def scatter_flat(front, rest, size, devices):
    wide_count = lax.axis_size("wide")
    starts, rows = flat_blocks(size, devices)
    blocks = pl.pallas_call(
        functools.partial(split_kernel, starts=starts),
        out_shape=jax.ShapeDtypeStruct((devices, rows, lanes), front.dtype),
    )(front, rest)
    bits = wide_bits(wide_count)[::-1] + [("pair", 1), side_bit]
    part = blocks.reshape((2,) * len(bits) + blocks.shape[1:])
    return halve(part, side_bit, len(bits) - 1)


def other_step(part, wide_count, step):
    bits = wide_bits(wide_count)[::-1] + [("pair", 1)]
    route = routes(wide_count)[0]
    left = [bit for bit in bits if bit not in route[:step]]
    return halve(part, route[step], left.index(route[step]))


def own_share(part, size, device):
    return lax.dynamic_slice(part.reshape(-1), (device * size % (tile * lanes),), (size,))


def shards(
    token_ids,
    live_lengths,
    key_keep,
    buckets,
    mask_pos,
    mask_labels,
    mask_counts,
    source_logits,
    embed_table,
    embed_first,
    embed_second,
    attn_mats,
    attn_moment,
    ffn_mats,
    ffn_moment,
    other_params,
    other_first,
    other_second,
):
    wide_count = lax.axis_size("wide")
    narrow_count = lax.axis_size("pair") * 2
    devices = wide_count * narrow_count
    device = lax.axis_index(everyone).astype(jnp.int32)
    owned = embed_table.shape[0]
    size = other_params.shape[0]
    col_width = attn_mats.shape[2]
    ffn_width = ffn_mats.shape[2]
    kinds = attn_mats.shape[0]
    table_low = embed_table.astype(jnp.bfloat16)

    attn_own = attn_mats.astype(jnp.bfloat16)
    other_own = place_flat(other_params.astype(jnp.bfloat16), device, devices)
    if col_width == lanes:
        merged = jnp.concatenate([attn_own.reshape(-1, lanes), other_own])
        merged = lax.all_gather(merged, everyone)
        other_all = merged[:, kinds * D :]
        attn_low = unpack_attn(merged, wide_count, narrow_count)
    else:
        attn_all = lax.all_gather(attn_own, everyone)
        other_all = lax.all_gather(other_own, everyone)
        attn_all = attn_all.reshape(wide_count, narrow_count * kinds, D, col_width)
        attn_low = attn_all.transpose(1, 2, 0, 3).reshape(narrow_count * kinds, D, D)
    other_flat = join_flat(other_all, size)
    ffn_all = lax.all_gather(ffn_mats.astype(jnp.bfloat16), everyone)
    bias_rows = V // lanes
    up_rows = bias_rows + L * FF // lanes
    vec_rows = up_rows + NV * D // lanes
    dec_bias = lax.dynamic_slice(other_flat.reshape(-1), (device * owned,), (owned,))
    dec_bias = dec_bias.astype(jnp.float32)
    up_biases = other_flat[bias_rows:up_rows].reshape(devices // 2, 2, ffn_width)
    up_biases = up_biases.transpose(1, 0, 2).reshape(L, FF).astype(jnp.float32)
    vectors = other_flat[up_rows:vec_rows].reshape(NV, D).astype(jnp.float32)
    head_weight = other_flat[vec_rows : vec_rows + D * D // lanes].reshape(D, D)

    win_count = token_ids.shape[0]
    assert win_count == 1 and SEQ == 2 * WINDOW
    group = devices // 2
    per_place = WINDOW // group
    half = device % 2
    owner_of, target_of, rank_of = position_plan(devices, owned)
    tokens = token_ids.reshape(-1)
    token_owner = tokens // owned
    token_local = tokens - token_owner * owned
    order = jnp.arange(WINDOW, dtype=jnp.int32)
    earlier = order[None, :] < order[:, None]
    same = tokens[:, None] == tokens[None, :]
    is_first = ~jnp.any(same & earlier, axis=1)
    same_owner = token_owner[:, None] == token_owner[None, :]
    rank = jnp.sum((same_owner & earlier & is_first[None, :]).astype(jnp.int32), axis=1)
    taken = np.zeros((devices, devices), np.int32)
    np.add.at(taken, (target_of, owner_of), 1)
    taken_here = lax.dynamic_index_in_dim(jnp.asarray(taken), device, 0, keepdims=False)
    owners = jnp.arange(devices, dtype=jnp.int32)
    offset = jnp.sum(jnp.where(token_owner[:, None] == owners[None, :], taken_here[None], 0), 1)
    first_slot = jnp.where(is_first, offset + rank, 0)
    slot = jnp.sum(jnp.where(same & is_first[None, :], first_slot[None, :], 0), axis=1)

    def address(round_idx):
        there = slot - round_idx * slots
        return jnp.where((there >= 0) & (there < slots), token_owner * slots + there, -1)

    def requests(addresses):
        cells = jnp.arange(devices * slots, dtype=jnp.int32)
        hits = (cells[:, None] == addresses[None, :]) & is_first[None, :]
        return jnp.sum(jnp.where(hits, token_local[None, :] + 1, 0), axis=1)

    now = address(0)
    labels_at = slots + 2
    message = jnp.concatenate(
        [
            requests(now).reshape(devices, slots),
            jnp.broadcast_to(jnp.max(slot)[None, None], (devices, 1)),
            jnp.broadcast_to(mask_counts.reshape(1, 1), (devices, 1)),
            jnp.broadcast_to(mask_labels.reshape(1, MPW), (devices, MPW)),
            jnp.zeros((devices, lanes - labels_at - MPW), jnp.int32),
        ],
        axis=1,
    )
    message = swap_all(message)
    rounds = jnp.max(message[:, slots]) // slots + 1
    counts_all = message[:, slots + 1]
    labels_all = message[:, labels_at : labels_at + MPW].reshape(-1)
    masked_total = jnp.sum(counts_all).astype(jnp.float32)
    place = np.arange(SEQ)
    cell_of = jnp.asarray(target_of * slots + rank_of, jnp.int32)
    local_of = jnp.asarray(V + place - owner_of * owned + 1, jnp.int32)
    mine = jnp.asarray(owner_of, jnp.int32) == device
    cells = jnp.arange(devices * slots, dtype=jnp.int32)
    place_hits = (cells[:, None] == cell_of[None, :]) & mine[None, :]
    place_rows = jnp.sum(jnp.where(place_hits, local_of[None, :], 0), axis=1)
    asked = message[:, :slots].reshape(-1) + place_rows - 1
    held = (owner_of * slots + rank_of).reshape(2, per_place, group).transpose(0, 2, 1)
    held = jnp.asarray(held.reshape(devices, per_place), jnp.int32)
    held = lax.dynamic_index_in_dim(held, half * group + device // 2, 0, keepdims=False)

    def fetch(asked_rows):
        rows = select_rows(asked_rows, table_low).astype(jnp.bfloat16)
        return swap_all(rows.reshape(devices, slots, D)).reshape(-1, D)

    def ask_again(addresses):
        return swap_all(requests(addresses).reshape(devices, slots)).reshape(-1) - 1

    fetched = fetch(asked)
    source_own = source_logits.reshape(MPW, V)
    source_max = jnp.max(source_own, axis=1).astype(jnp.float32)
    source_sum = jnp.sum(jnp.exp(source_own.astype(jnp.float32) - source_max[:, None]), axis=1)
    source_total = source_max + jnp.log(source_sum)
    source_cut = jnp.pad(source_own, ((0, 0), (0, devices * owned - V)))
    source_cut = source_cut.reshape(MPW, devices, owned).transpose(1, 0, 2)
    fetched, source_cut, source_total = lax.optimization_barrier(
        (fetched, source_cut, source_total)
    )
    if ffn_width == lanes:
        ffn_low = unpack_ffn(ffn_all, wide_count)
    else:
        ffn_low = ffn_all.reshape(devices // 2, 2, 2 * L, D, ffn_width)
        ffn_low = ffn_low.transpose(2, 3, 1, 0, 4).reshape(2 * L, D, FF)
    source_here = swap_all(source_cut)
    token_rows = select_rows(now, fetched)
    place_part = select_rows(held, fetched).astype(jnp.bfloat16)
    place_all = gather_blocks(place_part, wide_count, 1, 128).reshape(group, per_place, D)
    place_all = place_all.transpose(1, 0, 2).reshape(WINDOW, D).astype(jnp.float32)

    def more_rows(state):
        round_idx, rows = state
        addresses = address(round_idx)
        return (round_idx + 1, rows + select_rows(addresses, fetch(ask_again(addresses))))

    _, token_rows = lax.while_loop(
        lambda state: state[0] < rounds, more_rows, (jnp.int32(1), token_rows)
    )

    is_valid = (order[None, :] < live_lengths[:, None]) & (key_keep == 1)
    key_ok = is_valid.reshape(win_count, 1, 1, 1, WINDOW)
    bucket_ids = buckets.reshape(win_count, 1, WINDOW)
    same_bucket = bucket_ids[:, :, None, :, None] == bucket_ids[:, :, None, None, :]
    allowed = same_bucket & key_ok | jnp.eye(WINDOW, dtype=bool)
    embedded = (token_rows + place_all).reshape(win_count, WINDOW, D)
    hidden, embed_pull = jax.vjp(layer_norm, embedded, vectors[0], vectors[1])
    params = (
        attn_low[0],
        attn_low[1],
        attn_low[2],
        attn_low[3],
        ffn_low[0],
        ffn_low[1],
        up_biases[0],
        vectors[2:10],
    )
    hidden, stored, shared = layer_forward(hidden, params, allowed)
    picks = mask_pos.reshape(-1)
    head_in = select_rows(picks, hidden.reshape(WINDOW, D).astype(jnp.bfloat16))
    head_in = head_in.astype(jnp.bfloat16)
    head_pre = jnp.dot(head_in, head_weight, preferred_element_type=jnp.float32) + vectors[NV - 3]
    head_out, head_pull = jax.vjp(head_tail, head_pre, vectors[NV - 2], vectors[NV - 1])
    head_low = head_out.astype(jnp.bfloat16)

    rows_all = devices * MPW
    side = lax.axis_index("side").astype(jnp.int32)
    here = here16().astype(jnp.int32)
    order_rows = jnp.arange(devices, dtype=jnp.int32)
    rank_of_dev = (order_rows % 2 ^ side) * group + (order_rows // 2 ^ here)
    dev_of_rank = (order_rows % group ^ here) * 2 + (order_rows // group ^ side)
    head_all = gather_relative(head_low, wide_count, 1, lanes)
    head_all, *shared = lax.optimization_barrier((head_all, *shared))
    head_all = jnp.concatenate([head_all, exchange(head_all, side_bit)]).reshape(rows_all, D)
    labels_all = pick_rows(labels_all.reshape(devices, MPW), dev_of_rank).reshape(rows_all, 1)
    is_live = jnp.arange(MPW, dtype=jnp.int32)[None, :] < pick_rows(counts_all[:, None], dev_of_rank)
    word_ids = device * owned + jnp.arange(owned, dtype=jnp.int32)
    is_word = (word_ids < V)[None, :]
    logits = jnp.einsum("rd,vd->rv", head_all, table_low, preferred_element_type=jnp.float32)
    logits = jnp.where(is_word, logits + dec_bias[None, :], masked_fill)
    top_here = jnp.max(logits, axis=1)
    sum_here = jnp.sum(jnp.exp(logits - top_here[:, None]), axis=1)
    stats = jnp.concatenate(
        [
            top_here.reshape(devices, MPW),
            sum_here.reshape(devices, MPW),
            jnp.zeros((devices, 2 * lanes - 2 * MPW), jnp.float32),
        ],
        axis=1,
    )
    stats, source_here = lax.optimization_barrier((stats, source_here))
    stats = swap_all(pick_rows(stats, rank_of_dev))
    tops = stats[:, :MPW]
    top = jnp.max(tops, axis=0)
    total = top + jnp.log(jnp.sum(stats[:, MPW : 2 * MPW] * jnp.exp(tops - top[None]), axis=0))
    totals = spread(jnp.concatenate([total, source_total]), devices)
    totals = pick_rows(totals, dev_of_rank)
    row_facts = jnp.concatenate(
        [
            totals[:, :MPW].reshape(rows_all, 1),
            totals[:, MPW:].reshape(rows_all, 1),
            is_live.reshape(rows_all, 1).astype(jnp.float32),
            labels_all.astype(jnp.float32),
        ],
        axis=1,
    )
    place_facts = jnp.stack([device * owned, here, side]).astype(jnp.int32)
    grad_logits, losses, grad_dec = logit_grads(
        place_facts, logits, source_here, row_facts, devices
    )
    loss_part = jnp.sum(losses)
    give = jnp.dot(grad_logits[rows_all // 2 :], table_low, preferred_element_type=jnp.float32)
    got = exchange(give, side_bit)
    keep = jnp.dot(grad_logits[: rows_all // 2], table_low, preferred_element_type=jnp.float32)
    grad_head_out = reduce_rows((keep + got).reshape(group, MPW, D), wide_count)
    grad_words = jnp.einsum("rv,rd->vd", grad_logits, head_all, preferred_element_type=jnp.float32)
    grad_head_out, grad_words = lax.optimization_barrier((grad_head_out, grad_words))

    grad_pre, grad_head_gain, grad_head_shift = head_pull(grad_head_out)
    pre_low = grad_pre.astype(jnp.bfloat16)
    grad_head_w = jnp.einsum("rd,rf->df", head_in, pre_low, preferred_element_type=jnp.float32)
    grad_head_in = jnp.einsum("rf,df->rd", pre_low, head_weight, preferred_element_type=jnp.float32)
    grad_hidden = add_rows(picks, grad_head_in, WINDOW).reshape(win_count, WINDOW, D)
    grad_hidden, layer_mats, up_grad, vec_grads = layer_backward(
        grad_hidden, stored, shared, params, allowed
    )
    grad_embed, grad_emb_gain, grad_emb_shift = embed_pull(grad_hidden)
    flat_embed = grad_embed.reshape(WINDOW, D)

    ffn_parts, attn_parts = layer_mats[1], layer_mats[0]
    flat_embed, ffn_parts = tied(flat_embed, ffn_parts)
    dec_block = jnp.zeros((devices * owned,), jnp.float32)
    dec_block = lax.dynamic_update_slice(dec_block, grad_dec, (device * owned,))[:V]
    vector_block = jnp.concatenate(
        [jnp.stack([grad_emb_gain, grad_emb_shift])]
        + [vec_grads]
        + [jnp.stack([jnp.sum(pre_low.astype(jnp.float32), 0), grad_head_gain, grad_head_shift])],
        axis=0,
    )
    front = jnp.concatenate(
        [
            dec_block.reshape(-1, lanes),
            up_grad.reshape(2, devices // 2, ffn_width).transpose(1, 0, 2).reshape(-1, lanes),
            vector_block.reshape(-1, lanes),
        ]
    )
    other_part = scatter_flat(front, grad_head_w.reshape(-1, lanes), size, devices)

    place_grad = flat_embed.reshape(per_place, group, D).transpose(1, 0, 2)
    ffn_grad = jnp.concatenate(ffn_parts, axis=1)
    sent = add_rows(now, flat_embed, devices * slots)
    arrived = swap_all(sent.reshape(devices, slots, D))
    place_parts = route_parts(place_grad.reshape(group, per_place, D), wide_count)
    for step in range(len(routes(wide_count)[0])):
        place_parts, attn_parts, (other_part,) = lockstep(
            route_step(place_parts, wide_count, step, False),
            reduce_step(attn_parts, wide_count, step),
            [other_step(other_part, wide_count, step)],
        )
    attn_grad = jnp.concatenate(attn_parts, axis=1)
    other_grad = own_share(other_part, size, device)
    place_grad = jnp.concatenate(place_parts, axis=-1)
    place_grad = gather_relative(place_grad, wide_count, 1, lanes)
    place_grad = jnp.concatenate([place_grad, exchange(place_grad, side_bit)])
    turn = jnp.arange(devices, dtype=jnp.int32)[:, None]
    place_ids = (turn // group ^ side) * WINDOW + (turn % group ^ here)
    place_ids = place_ids + jnp.arange(per_place, dtype=jnp.int32)[None, :] * group
    place_ids = (V - device * owned + place_ids).reshape(-1)
    table_grad = grad_words + add_rows(asked, arrived.reshape(-1, D), owned)
    table_grad = table_grad + add_rows(place_ids, place_grad.reshape(SEQ, D), owned)

    def more_grads(state):
        round_idx, grads = state
        addresses = address(round_idx)
        asked_rows = ask_again(addresses)
        sent = add_rows(addresses, flat_embed, devices * slots)
        arrived = swap_all(sent.reshape(devices, slots, D)).reshape(-1, D)
        return (round_idx + 1, grads + add_rows(asked_rows, arrived, owned))

    _, table_grad = lax.while_loop(
        lambda state: state[0] < rounds, more_grads, (jnp.int32(1), table_grad)
    )

    squares = square_sum((table_grad, attn_grad, ffn_grad, other_grad))
    sums = jnp.sum(spread(jnp.stack([squares, loss_part]), devices), axis=0)
    grad_norm = jnp.sqrt(sums[0]) / masked_total
    loss_value = sums[1] / masked_total
    factor = jnp.minimum(1.0, clip_limit / grad_norm)
    scaling = factor / masked_total

    attn_moment_new = mu_muon * attn_moment + attn_grad * scaling
    ffn_moment_new = mu_muon * ffn_moment + ffn_grad * scaling
    second = lax.axis_index("side") == 1
    keep = jnp.where(second, ffn_moment_new[1], ffn_moment_new[0])
    got = exchange(jnp.where(second, ffn_moment_new[0], ffn_moment_new[1]), side_bit)
    ffn_pair = jnp.concatenate([keep, got], axis=1)[None]
    attn_parts = gather_start(attn_moment_new[0].astype(jnp.bfloat16), 0, tile)
    ffn_parts = gather_start(ffn_pair[0].astype(jnp.bfloat16), 0, tile)
    steps = len(routes(wide_count)[0])
    for step in range(steps - 1):
        attn_parts, ffn_parts = lockstep(
            gather_step(attn_parts, wide_count, step, False),
            gather_step(ffn_parts, wide_count, step),
        )
    attn_found = gather_end(attn_parts, wide_count, 0, False)
    ffn_found = gather_end(gather_step(ffn_parts, wide_count, steps - 1), wide_count, 0)
    attn_new = muon_cols(attn_mats, attn_moment_new, gram_of(attn_found), D)
    ffn_turn = newton_cols(ffn_pair, gram_of(ffn_found))[0]
    keep, give = ffn_turn[:, :ffn_width], ffn_turn[:, ffn_width:]
    got = exchange(give, side_bit)
    ffn_turn = jnp.stack([jnp.where(second, got, keep), jnp.where(second, keep, got)])
    ffn_new = ffn_mats - lr_muon * muon_shape * math.sqrt(max(D, FF)) * ffn_turn
    embed_new, embed_first_new, embed_second_new = adam_step(
        embed_table, embed_first, embed_second, table_grad * scaling
    )
    other_new, other_first_new, other_second_new = adam_step(
        other_params, other_first, other_second, other_grad * scaling
    )
    return (
        loss_value,
        grad_norm,
        embed_new,
        embed_first_new,
        embed_second_new,
        attn_new,
        attn_moment_new,
        ffn_new,
        ffn_moment_new,
        other_new,
        other_first_new,
        other_second_new,
    )


def solution(mesh):
    wide_count, narrow_count = mesh.shape["wide"], mesh.shape["narrow"]
    assert narrow_count % 2 == 0
    split = Mesh(
        np.asarray(mesh.devices).reshape(wide_count, narrow_count // 2, 2), everyone
    )
    rows, narrow = P(everyone), ("pair", "side")
    attn_spec, ffn_spec = P(narrow, None, "wide"), P(None, None, everyone)
    in_specs = (rows,) * 11 + (attn_spec,) * 2 + (ffn_spec,) * 2 + (rows,) * 3
    out_specs = (P(), P()) + (rows,) * 3 + (attn_spec,) * 2 + (ffn_spec,) * 2 + (rows,) * 3

    return jax.shard_map(
        shards, mesh=split, in_specs=in_specs, out_specs=out_specs, check_vma=False
    )
```

```python
import functools
import math

import jax
import jax.numpy as jnp
import numpy as np
from jax import lax
from jax.experimental import pallas as pl
from jax.experimental.pallas import tpu as pltpu
from jax.sharding import Mesh
from jax.sharding import PartitionSpec as P

D = 1024
FF = 4096
HEADS = 16
L = 1
V = 30720
SEQ = 1024
WINDOW = 512
NS_ITERS = 3
ADAM_STEP = 5
MPW = 80
NV = 13


high = lax.Precision.HIGH
lanes = 128
tile = 16
slots = 32
ln_eps = 1e-05
masked_fill = -1e30
clip_limit = 0.3
ns_a = 3.4445
ns_b = -4.775
ns_c = 2.0315
mu_muon = 0.95
lr_muon = 0.1
muon_shape = 0.2
lr_adam = 0.01
beta_one = 0.9
beta_two = 0.999
adam_eps = 1e-08


def layer_norm(inputs, gain_vec, shift_vec):
    center = inputs - jnp.mean(inputs, -1, keepdims=True)
    spread = jnp.mean(center * center, -1, keepdims=True)
    return center * lax.rsqrt(spread + ln_eps) * gain_vec + shift_vec


def exact_gelu(inputs):
    return jax.nn.gelu(inputs, approximate=False)


def head_tail(head_pre, gain_vec, shift_vec):
    return layer_norm(exact_gelu(head_pre), gain_vec, shift_vec)


def project(inputs, weight):
    return jnp.einsum("bsd,df->bsf", inputs, weight, preferred_element_type=jnp.float32)


def project_back(gradients, weight):
    return jnp.einsum("bsf,df->bsd", gradients, weight, preferred_element_type=jnp.float32)


def col_sum(inputs):
    return jnp.sum(inputs.astype(jnp.float32), axis=(0, 1))


def to_heads(inputs):
    return inputs.reshape(
        inputs.shape[0], inputs.shape[1] // WINDOW, WINDOW, HEADS, inputs.shape[2] // HEADS
    )


def attn_scores(queries, key_proj, allowed):
    raw_scores = jnp.einsum(
        "bnqhe,bnkhe->bnhqk",
        to_heads(queries),
        to_heads(key_proj),
        preferred_element_type=jnp.float32,
    )
    return jnp.where(allowed, raw_scores * (queries.shape[2] // HEADS) ** (-0.5), masked_fill)


def share(values, axis):
    return jnp.concatenate([values, exchange(values, side_bit)], axis=axis)


def swap_pick(for_first, for_second, axis):
    first = lax.axis_index("side") == 0
    keep = jnp.where(first, for_first, for_second)
    got = exchange(jnp.where(first, for_second, for_first), side_bit)
    return jnp.concatenate([keep, got], axis=axis)


def share_half(values):
    side = lax.axis_index("side")
    half = values.shape[1] // 2
    keep = lax.dynamic_slice_in_dim(values, side * half, half, axis=1)
    got = exchange(lax.dynamic_slice_in_dim(values, (1 - side) * half, half, axis=1), side_bit)
    return jnp.concatenate([keep, got])


def layer_forward(hidden, params, allowed):
    w_query, w_key, w_value, w_out, w_up, w_down, up_bias, vectors = params
    count, length, model_width = hidden.shape
    inputs = hidden.astype(jnp.bfloat16)
    queries = (project(inputs, w_query) + vectors[4]).astype(jnp.bfloat16)
    key_proj = project(inputs, w_key).astype(jnp.bfloat16)
    values = (project(inputs, w_value) + vectors[5]).astype(jnp.bfloat16)
    scores = attn_scores(queries, key_proj, allowed)
    log_total = jax.nn.logsumexp(scores, axis=-1, keepdims=True)
    prob_low = jnp.exp(scores - log_total).astype(jnp.bfloat16)
    context = jnp.einsum(
        "bnhqk,bnkhe->bnqhe", prob_low, to_heads(values), preferred_element_type=jnp.float32
    )
    context = context.reshape(count, length, model_width).astype(jnp.bfloat16)
    attn_sum = hidden + (project(context, w_out) + vectors[6])
    middle, first_pull = jax.vjp(layer_norm, attn_sum, vectors[0], vectors[1])
    middle_low = middle.astype(jnp.bfloat16)
    up_proj = project(middle_low, w_up) + up_bias
    activated, gelu_pull = jax.vjp(exact_gelu, up_proj)
    act_low = activated.astype(jnp.bfloat16)
    ffn_sum = middle + (project_back(act_low, w_down) + vectors[7])
    output, second_pull = jax.vjp(layer_norm, ffn_sum, vectors[2], vectors[3])
    stored = (
        inputs,
        queries,
        key_proj,
        values,
        log_total,
        context,
        first_pull,
        middle_low,
        gelu_pull,
        act_low,
        second_pull,
    )
    shared = (
        share(middle_low[0].T, 1),
        share_half(act_low[0]),
        share(inputs[0].T, 1),
        swap_pick(inputs[0].T, context[0].T, 1),
    )
    return (output, stored, shared)


def layer_backward(grad_out, stored, shared, params, allowed):
    w_query, w_key, w_value, w_out, w_up, w_down, _, _ = params
    (_, queries, key_proj, values, log_total, _, first_pull, _, gelu_pull, _, second_pull) = stored
    count, length, model_width = grad_out.shape
    grad_ffn, grad_gain_two, grad_shift_two = second_pull(grad_out)
    down_low = grad_ffn.astype(jnp.bfloat16)
    (grad_up,) = gelu_pull(project(down_low, w_down))
    up_low = grad_up.astype(jnp.bfloat16)
    wide_count = lax.axis_size("wide")
    operands = (
        shared[0],
        share(down_low[0].T, 1),
        share_half(up_low[0]),
        shared[1],
    )
    if FF // (4 * wide_count) == lanes:
        grad_mats_ffn = ffn_weight_grads(*operands, wide_count)
    else:
        blocks = jnp.stack([jnp.dot(*operands[::2], preferred_element_type=jnp.float32),
                            jnp.dot(*operands[1::2], preferred_element_type=jnp.float32)])
        blocks = blocks.reshape(2, D, wide_count, 2, -1).transpose(2, 3, 0, 1, 4)
        grad_mats_ffn = in_routes(blocks, wide_count)
    grad_ffn, parts = tied(grad_ffn, grad_mats_ffn)
    parts = reduce_step(parts, wide_count, 0)
    grad_middle = grad_ffn + project_back(up_low, w_up)
    grad_attn, grad_gain_one, grad_shift_one = first_pull(grad_middle)
    attn_low = grad_attn.astype(jnp.bfloat16)
    grad_context = to_heads(project_back(attn_low, w_out).astype(jnp.bfloat16))
    attn_prob = jnp.exp(attn_scores(queries, key_proj, allowed) - log_total)
    prob_low = attn_prob.astype(jnp.bfloat16)
    grad_prob = jnp.einsum(
        "bnqhe,bnkhe->bnhqk", grad_context, to_heads(values), preferred_element_type=jnp.float32
    )
    grad_value = jnp.einsum(
        "bnhqk,bnqhe->bnkhe", prob_low, grad_context, preferred_element_type=jnp.float32
    )
    grad_value = grad_value.reshape(count, length, model_width).astype(jnp.bfloat16)
    grad_scores = attn_prob * (grad_prob - jnp.sum(grad_prob * attn_prob, -1, keepdims=True))
    grad_raw = (grad_scores * (model_width // HEADS) ** (-0.5)).astype(jnp.bfloat16)
    late_keys, parts = tied(key_proj, parts)
    parts = reduce_step(parts, wide_count, 1)
    grad_query = jnp.einsum(
        "bnhqk,bnkhe->bnqhe", grad_raw, to_heads(late_keys), preferred_element_type=jnp.float32
    )
    grad_query = grad_query.reshape(count, length, model_width).astype(jnp.bfloat16)
    grad_key = jnp.einsum(
        "bnhqk,bnqhe->bnkhe", grad_raw, to_heads(queries), preferred_element_type=jnp.float32
    )
    grad_key = grad_key.reshape(count, length, model_width).astype(jnp.bfloat16)
    grad_query, parts = tied(grad_query, parts)
    parts = reduce_step(parts, wide_count, 2)
    operands = (
        shared[2],
        shared[3],
        swap_pick(grad_query[0], grad_key[0], 0),
        swap_pick(grad_value[0], attn_low[0], 0),
    )
    if D // wide_count == lanes:
        attn_parts = attn_weight_grads(*operands, wide_count)
    else:
        blocks = jnp.stack([jnp.dot(*operands[::2], preferred_element_type=jnp.float32),
                            jnp.dot(*operands[1::2], preferred_element_type=jnp.float32)])
        blocks = blocks.reshape(2, 1, D, wide_count, -1).transpose(3, 0, 1, 2, 4)
        attn_parts = in_routes(blocks, wide_count)
    last_query, attn_parts = tied(grad_query, attn_parts)
    attn_parts = reduce_step(attn_parts, wide_count, 0)
    grad_hidden = (
        grad_attn
        + project_back(last_query, w_query)
        + project_back(grad_key, w_key)
        + project_back(grad_value, w_value)
    )
    grad_hidden, parts = tied(grad_hidden, parts)
    for step in range(3, len(routes(wide_count)[0])):
        parts = reduce_step(parts, wide_count, step)
    matrices = (attn_parts, parts)
    vector_grads = jnp.stack(
        [
            grad_gain_one,
            grad_shift_one,
            grad_gain_two,
            grad_shift_two,
            col_sum(grad_query),
            col_sum(grad_value),
            col_sum(attn_low),
            col_sum(down_low),
        ]
    )
    return (grad_hidden, matrices, col_sum(up_low), vector_grads)


def slab_product(matrix, columns):
    return jnp.einsum(
        "kde,kec->kdc", matrix, columns, precision=high, preferred_element_type=jnp.float32
    )


def newton_cols(moment, gram):
    norms = jnp.sqrt(jnp.trace(gram, axis1=1, axis2=2))
    scaling = 1.0 / (norms + 1e-07)
    current = moment * scaling[:, None, None]
    gram = gram * (scaling * scaling)[:, None, None]
    for step_idx in range(NS_ITERS):
        if step_idx + 1 < NS_ITERS:
            poly = ns_b * gram + ns_c * jnp.einsum("kde,kef->kdf", gram, gram)
            current = ns_a * current + slab_product(poly, current)
            half = ns_a * gram + jnp.einsum("kde,kef->kdf", poly, gram)
            gram = ns_a * half + jnp.einsum("kde,kef->kdf", half, poly)
        else:
            once = slab_product(gram, current)
            current = ns_a * current + ns_b * once + ns_c * slab_product(gram, once)
    return current


def gram_of(found):
    return jnp.einsum("wdc,wec->de", found, found, preferred_element_type=jnp.float32)[None]


def relative_order(part, taken):
    names = [bit for bit in wide_bits(lax.axis_size("wide"))[::-1] + [("pair", 1)] if bit in taken]
    dims = [names.index(bit) for bit in taken[::-1]]
    split = part.reshape((2,) * len(taken) + part.shape[1:])
    turn = [dims.index(place) for place in range(len(taken))]
    split = split.transpose(turn + list(range(len(taken), split.ndim)))
    return split.reshape(part.shape)


def muon_cols(master, new_moment, gram, long_side):
    change = lr_muon * muon_shape * math.sqrt(long_side) * newton_cols(new_moment, gram)
    return master - change


def adam_step(master, first_moment, second, gradient):
    new_first = beta_one * first_moment + (1.0 - beta_one) * gradient
    new_second = beta_two * second + (1.0 - beta_two) * gradient * gradient
    first_hat = new_first / (1.0 - beta_one**ADAM_STEP)
    second_hat = new_second / (1.0 - beta_two**ADAM_STEP)
    return (master - lr_adam * first_hat / (jnp.sqrt(second_hat) + adam_eps), new_first, new_second)


def square_sum(arrays):
    running = jnp.zeros((), jnp.float32)
    for member in arrays:
        running = running + jnp.sum(member * member)
    return running


everyone = ("wide", "pair", "side")
side_bit = ("side", 1)


def swap_all(blocks, axes=everyone):
    return lax.all_to_all(blocks, axes, 0, 0, tiled=True)


def spread(values, devices):
    size = values.shape[0]
    row = jnp.pad(values, (0, -size % lanes))
    return swap_all(jnp.broadcast_to(row[None], (devices, row.shape[0])))[:, :size]


def wide_bits(wide_count):
    return [("wide", 1 << k) for k in range(wide_count.bit_length() - 1)]


def routes(wide_count, with_pair=True):
    bits = wide_bits(wide_count)
    near, far, across = bits[:1], bits[1:], [("pair", 1)] if with_pair else []
    last = far[1:]
    return [across + near + far, near + far[:1] + across + last, far[:1] + across + near + last]


def my_bit(bit):
    axis, mask = bit
    return lax.axis_index(axis) // mask % 2


def exchange(values, bit):
    axis, mask = bit
    steps = [(here, here ^ mask) for here in range(lax.axis_size(axis))]
    return lax.ppermute(values, axis, steps)


def halve(values, bit, dim):
    mine = lax.dynamic_index_in_dim(values, my_bit(bit), dim, keepdims=False)
    theirs = lax.dynamic_index_in_dim(values, 1 - my_bit(bit), dim, keepdims=False)
    return mine + exchange(theirs, bit)


def double(values, bit, dim):
    theirs = exchange(values, bit)
    first = my_bit(bit) == 0
    pair = [jnp.where(first, values, theirs), jnp.where(first, theirs, values)]
    return jnp.stack(pair, axis=dim)


def cuts(length, unit):
    whole = length // unit
    sizes = [(whole + 2) // 3 * unit, (whole + 1) // 3 * unit]
    sizes.append(length - sum(sizes))
    starts = [0, sizes[0], sizes[0] + sizes[1]]
    return [(start, start + size) for start, size in zip(starts, sizes) if size]


def here16():
    return lax.axis_index("wide") * 2 + lax.axis_index("pair")


def lockstep(*groups):
    flat = lax.optimization_barrier(sum((list(group) for group in groups), []))
    found = []
    for group in groups:
        found.append(flat[: len(group)])
        flat = flat[len(group) :]
    return found


def reduce_step(parts, wide_count, step):
    return [
        part[0] + exchange(part[1], route[step])
        for part, route in zip(parts, routes(wide_count))
    ]


def tied(value, parts):
    value, *parts = lax.optimization_barrier((value, *parts))
    return value, parts


def static_step(part, left, bit):
    dim = left.index(bit)
    keep = lax.index_in_dim(part, 0, dim, keepdims=False)
    return keep + exchange(lax.index_in_dim(part, 1, dim, keepdims=False), bit)


def route_parts(values, wide_count):
    bits = wide_bits(wide_count)[::-1] + [("pair", 1)]
    return [
        values[..., start:stop].reshape((2,) * len(bits) + (values.shape[1], stop - start))
        for start, stop in cuts(values.shape[-1], lanes)
    ]


def route_step(parts, wide_count, step, static):
    bits = wide_bits(wide_count)[::-1] + [("pair", 1)]
    found = []
    for part, route in zip(parts, routes(wide_count)):
        left = [bit for bit in bits if bit not in route[:step]]
        if static:
            found.append(static_step(part, left, route[step]))
        else:
            found.append(halve(part, route[step], left.index(route[step])))
    return found


def reduce_rows(values, wide_count):
    parts = route_parts(values, wide_count)
    for step in range(len(routes(wide_count)[0])):
        (parts,) = lockstep(route_step(parts, wide_count, step, True))
    return jnp.concatenate(parts, axis=-1)


def gather_start(block, axis, unit):
    return [
        lax.slice_in_dim(block, start, stop, axis=axis)[None]
        for start, stop in cuts(block.shape[axis], unit)
    ]


def gather_step(parts, wide_count, step, with_pair=True):
    return [
        jnp.concatenate([part, exchange(part, route[::-1][step])])
        for part, route in zip(parts, routes(wide_count, with_pair))
    ]


def gather_end(parts, wide_count, axis, with_pair=True):
    ordered = [
        relative_order(part, route[::-1])
        for part, route in zip(parts, routes(wide_count, with_pair))
    ]
    return jnp.concatenate(ordered, axis=1 + axis)


def gather_relative(block, wide_count, axis, unit):
    parts = gather_start(block, axis, unit)
    for step in range(len(routes(wide_count)[0])):
        (parts,) = lockstep(gather_step(parts, wide_count, step))
    return gather_end(parts, wide_count, axis)


def route_shape(route, covered):
    wide = [bit for bit in route if bit not in covered]
    shape = tuple(2 if bit in covered else 1 for bit in route)

    def index(step):
        low = 1 << len(covered) - 1
        return tuple(
            0 if bit in covered else step * low // bit[1] % 2 for bit in route
        )

    assert wide
    return shape, index


def weight_grads(kernel, operands, column_specs, covered, steps, members, wide_count):
    here = jnp.stack([lax.axis_index("wide"), lax.axis_index("pair")]).astype(jnp.int32)
    shapes, specs = [], []
    for route, (start, stop) in zip(routes(wide_count), cuts(D, tile)):
        block, index = route_shape(route, covered)
        tail = (members, stop - start, lanes)
        shapes.append(jax.ShapeDtypeStruct((2,) * len(route) + tail, jnp.float32))
        specs.append(
            pl.BlockSpec(block + tail, lambda step, _, index=index: index(step) + (0, 0, 0))
        )
    return pl.pallas_call(
        kernel,
        grid_spec=pltpu.PrefetchScalarGridSpec(
            num_scalar_prefetch=1, grid=(steps,), in_specs=column_specs, out_specs=specs
        ),
        out_shape=shapes,
    )(here, *operands)


def put(refs, wide_count, covered, where, member, values):
    for ref, route, (start, stop) in zip(refs, routes(wide_count), cuts(D, tile)):
        place = tuple(where[bit] if bit in covered else 0 for bit in route)
        ref[place + (member,)] = values[start:stop]


def ffn_grads_kernel(here, up_rows, down_rows, up_cols, down_cols, *refs, wide_count):
    flip = here[1] == 0
    pair = ("pair", 1)
    for member, (rows, cols) in enumerate(((up_rows, up_cols), (down_rows, down_cols))):
        both = jnp.dot(rows[...], cols[...], preferred_element_type=jnp.float32)
        low, top = both[:, :lanes], both[:, lanes:]
        put(refs, wide_count, [pair], {pair: 0}, member, jnp.where(flip, low, top))
        put(refs, wide_count, [pair], {pair: 1}, member, jnp.where(flip, top, low))


def ffn_weight_grads(up_rows, down_rows, up_cols, down_cols, wide_count):
    whole = pl.BlockSpec(up_rows.shape, lambda step, here: (0, 0))
    cols = pl.BlockSpec((up_cols.shape[0], 2 * lanes), lambda step, here: (0, step ^ here[0]))
    kernel = functools.partial(ffn_grads_kernel, wide_count=wide_count)
    operands = (up_rows, down_rows, up_cols, down_cols)
    specs = [whole, whole, cols, cols]
    return weight_grads(kernel, operands, specs, [("pair", 1)], wide_count, 2, wide_count)


def attn_grads_kernel(here, one_rows, two_rows, one_cols, two_cols, *refs, wide_count):
    swap = here[0] % 2 == 0
    flip = here[1] == 0
    pair, near = ("pair", 1), ("wide", 1)
    blocks = []
    for rows, cols in ((one_rows, one_cols), (two_rows, two_cols)):
        both = jnp.dot(rows[...], cols[...], preferred_element_type=jnp.float32)
        low, top = both[:, :lanes], both[:, lanes:]
        blocks.append((jnp.where(swap, low, top), jnp.where(swap, top, low)))
    for step in range(2):
        one, two = blocks[0][step], blocks[1][step]
        first, second = jnp.where(flip, one, two), jnp.where(flip, two, one)
        put(refs, wide_count, [pair, near], {pair: 0, near: step}, 0, first)
        put(refs, wide_count, [pair, near], {pair: 1, near: step}, 0, second)


def attn_weight_grads(one_rows, two_rows, one_cols, two_cols, wide_count):
    whole = pl.BlockSpec(one_rows.shape, lambda step, here: (0, 0))
    cols = pl.BlockSpec((one_cols.shape[0], 2 * lanes), lambda step, here: (0, step ^ here[0] // 2))
    kernel = functools.partial(attn_grads_kernel, wide_count=wide_count)
    operands = (one_rows, two_rows, one_cols, two_cols)
    specs = [whole, whole, cols, cols]
    covered = [("pair", 1), ("wide", 1)]
    return weight_grads(kernel, operands, specs, covered, wide_count // 2, 1, wide_count)


def in_routes(blocks, wide_count):
    count = wide_count * 2
    order = jnp.arange(count) ^ here16()
    blocks = jnp.take(blocks.reshape((count,) + blocks.shape[2:]), order, axis=0)
    bits = wide_bits(wide_count)[::-1] + [("pair", 1)]
    parts = []
    for route, (start, stop) in zip(routes(wide_count), cuts(D, tile)):
        part = blocks[:, :, start:stop].reshape((2,) * len(bits) + blocks[:, :, start:stop].shape[1:])
        dims = [bits.index(bit) for bit in route]
        parts.append(part.transpose(dims + list(range(len(bits), part.ndim))))
    return parts


def gather_blocks(block, wide_count, axis, unit):
    bits = wide_bits(wide_count)[::-1] + [("pair", 1)]
    parts = []
    for route, (start, stop) in zip(routes(wide_count), cuts(block.shape[axis], unit)):
        part = lax.slice_in_dim(block, start, stop, axis=axis)
        have = []
        for bit in route[::-1]:
            have = sorted(have + [bit], key=bits.index)
            part = double(part, bit, have.index(bit))
        parts.append(part.reshape((wide_count, 2) + part.shape[len(bits) :]))
    return jnp.concatenate(parts, axis=2 + axis)


def select_rows(index, rows, precision=None):
    hits = index[:, None] == jnp.arange(rows.shape[0], dtype=jnp.int32)[None, :]
    return jnp.dot(
        hits.astype(rows.dtype), rows, precision=precision, preferred_element_type=jnp.float32
    )


def logit_grads_kernel(facts, logits_ref, source_ref, rows_ref, grad_ref, loss_ref, dec_ref):
    step = pl.program_id(0)

    @pl.when(step == 0)
    def _():
        loss_ref[...] = jnp.zeros_like(loss_ref)
        dec_ref[...] = jnp.zeros_like(dec_ref)

    columns = lax.broadcasted_iota(jnp.int32, logits_ref.shape, 1) + facts[0]
    is_word = columns < V
    rows = rows_ref[...]
    log_prob = logits_ref[...] - rows[:, 0:1]
    source_log = source_ref[0].astype(jnp.float32) - rows[:, 1:2]
    source_prob = jnp.where(is_word, jnp.exp(source_log), 0.0)
    hits = columns == rows[:, 3:4].astype(jnp.int32)
    keep = is_word & (rows[:, 2:3] > 0.5)
    losses = source_prob * (source_log - log_prob) - jnp.where(hits, log_prob, 0.0)
    loss_ref[...] += jnp.sum(jnp.where(keep, losses, 0.0), axis=0, keepdims=True)
    grads = 2.0 * jnp.exp(log_prob) - jnp.where(hits, 1.0, 0.0) - source_prob
    grads = jnp.where(keep, grads, 0.0).astype(jnp.bfloat16)
    grad_ref[...] = grads
    dec_ref[...] += jnp.sum(grads.astype(jnp.float32), axis=0, keepdims=True)


def logit_grads(facts, logits, source, row_facts, devices):
    owned = logits.shape[1]
    group = devices // 2

    def source_block(step, facts):
        return ((step % group ^ facts[1]) * 2 + (step // group ^ facts[2]), 0, 0)

    line = pl.BlockSpec((1, owned), lambda step, facts: (0, 0))
    grads, losses, dec = pl.pallas_call(
        logit_grads_kernel,
        grid_spec=pltpu.PrefetchScalarGridSpec(
            num_scalar_prefetch=1,
            grid=(devices,),
            in_specs=[
                pl.BlockSpec((MPW, owned), lambda step, facts: (step, 0)),
                pl.BlockSpec((1, MPW, owned), source_block),
                pl.BlockSpec((MPW, 4), lambda step, facts: (step, 0)),
            ],
            out_specs=[pl.BlockSpec((MPW, owned), lambda step, facts: (step, 0)), line, line],
        ),
        out_shape=[
            jax.ShapeDtypeStruct(logits.shape, jnp.bfloat16),
            jax.ShapeDtypeStruct((1, owned), jnp.float32),
            jax.ShapeDtypeStruct((1, owned), jnp.float32),
        ],
    )(facts, logits, source, row_facts)
    return grads, losses, dec[0]


def pick_rows(values, index):
    hits = index[:, None] == jnp.arange(values.shape[0], dtype=jnp.int32)[None, :]
    return jnp.sum(jnp.where(hits[:, :, None], values[None], 0), axis=1)


def add_rows(index, rows, count):
    hits = jnp.arange(count, dtype=jnp.int32)[:, None] == index[None, :]
    return jnp.dot(
        hits.astype(rows.dtype), rows, precision=high, preferred_element_type=jnp.float32
    )


def flat_blocks(size, devices):
    total = size * devices
    starts = [dev * size // (tile * lanes) * tile for dev in range(devices)] + [total // lanes]
    ends = [-(-(dev + 1) * size // (tile * lanes)) * tile for dev in range(devices)]
    rows = max(end - start for start, end in zip(starts, ends))
    return starts, rows


def place_flat(share, device, devices):
    size = share.shape[0]
    _, rows = flat_blocks(size, devices)
    offset = device * size % (tile * lanes)
    block = lax.dynamic_update_slice(jnp.zeros((rows * lanes,), share.dtype), share, (offset,))
    return block.reshape(rows, lanes)


def join_kernel(blocks_ref, out_ref, *, starts):
    rows = blocks_ref.shape[1]
    for dev in range(len(starts) - 1):
        length = starts[dev + 1] - starts[dev]
        out_ref[starts[dev] : starts[dev + 1]] = blocks_ref[dev, :length]
    for dev in range(1, len(starts) - 1):
        length = starts[dev] - starts[dev - 1]
        if length < rows:
            shared = slice(starts[dev], starts[dev] + tile)
            both = blocks_ref[dev, :tile].astype(jnp.float32)
            both += blocks_ref[dev - 1, length : length + tile].astype(jnp.float32)
            out_ref[shared] = both.astype(out_ref.dtype)


def join_flat(blocks, size):
    starts, _ = flat_blocks(size, blocks.shape[0])
    starts[-1] += -starts[-1] % tile
    return pl.pallas_call(
        functools.partial(join_kernel, starts=starts),
        out_shape=jax.ShapeDtypeStruct((starts[-1], lanes), blocks.dtype),
    )(blocks)


def unpack_kernel(*refs):
    half = len(refs) * 2 // 3
    for place, out_ref in enumerate(refs[half:]):
        out_ref[:, :lanes] = refs[2 * place][...].reshape(D, lanes)
        out_ref[:, lanes:] = refs[2 * place + 1][...].reshape(D, lanes)


def unpack_attn(merged, wide_count, narrow_count):
    specs = [
        pl.BlockSpec((1, D, lanes), lambda step, add=step_add, kind=kind: (
            (2 * step + add) * narrow_count + kind, 0, 0
        ))
        for kind in range(narrow_count)
        for step_add in range(2)
    ]
    return pl.pallas_call(
        unpack_kernel,
        grid=(wide_count // 2,),
        in_specs=specs,
        out_specs=[pl.BlockSpec((D, 2 * lanes), lambda step: (0, step))] * narrow_count,
        out_shape=[jax.ShapeDtypeStruct((D, D), merged.dtype)] * narrow_count,
    )(*[merged] * len(specs))


def unpack_ffn(blocks, wide_count):
    specs = [
        pl.BlockSpec((1, 1, D, lanes), lambda step, kind=kind, pair=pair: (
            step % wide_count * 4 + pair * 2 + step // wide_count, kind, 0, 0
        ))
        for kind in range(2)
        for pair in range(2)
    ]
    return pl.pallas_call(
        unpack_kernel,
        grid=(2 * wide_count,),
        in_specs=specs,
        out_specs=[pl.BlockSpec((D, 2 * lanes), lambda step: (0, step))] * 2,
        out_shape=[jax.ShapeDtypeStruct((D, FF), blocks.dtype)] * 2,
    )(*[blocks] * 4)


def split_kernel(front_ref, rest_ref, out_ref, *, starts):
    front, rows = front_ref.shape[0], out_ref.shape[1]
    total = front + rest_ref.shape[0]
    for dev, start in enumerate(starts[:-1]):
        stop = min(start + rows, total)
        middle = min(max(start, front), stop)
        if start < middle:
            out_ref[dev, : middle - start] = front_ref[start:middle]
        if middle < stop:
            out_ref[dev, middle - start : stop - start] = rest_ref[middle - front : stop - front]
        if stop < start + rows:
            left = start + rows - stop
            out_ref[dev, rows - left :] = jnp.zeros((left, lanes), out_ref.dtype)


def scatter_flat(front, rest, size, devices):
    wide_count = lax.axis_size("wide")
    starts, rows = flat_blocks(size, devices)
    blocks = pl.pallas_call(
        functools.partial(split_kernel, starts=starts),
        out_shape=jax.ShapeDtypeStruct((devices, rows, lanes), front.dtype),
    )(front, rest)
    bits = wide_bits(wide_count)[::-1] + [("pair", 1), side_bit]
    part = blocks.reshape((2,) * len(bits) + blocks.shape[1:])
    return halve(part, side_bit, len(bits) - 1)


def other_step(part, wide_count, step):
    bits = wide_bits(wide_count)[::-1] + [("pair", 1)]
    route = routes(wide_count)[0]
    left = [bit for bit in bits if bit not in route[:step]]
    return halve(part, route[step], left.index(route[step]))


def own_share(part, size, device):
    return lax.dynamic_slice(part.reshape(-1), (device * size % (tile * lanes),), (size,))


def shards(
    token_ids,
    live_lengths,
    key_keep,
    buckets,
    mask_pos,
    mask_labels,
    mask_counts,
    source_logits,
    embed_table,
    embed_first,
    embed_second,
    attn_mats,
    attn_moment,
    ffn_mats,
    ffn_moment,
    other_params,
    other_first,
    other_second,
):
    wide_count = lax.axis_size("wide")
    narrow_count = lax.axis_size("pair") * 2
    devices = wide_count * narrow_count
    device = lax.axis_index(everyone).astype(jnp.int32)
    owned = embed_table.shape[0]
    size = other_params.shape[0]
    col_width = attn_mats.shape[2]
    ffn_width = ffn_mats.shape[2]
    kinds = attn_mats.shape[0]
    table_low = embed_table.astype(jnp.bfloat16)

    attn_own = attn_mats.astype(jnp.bfloat16)
    other_own = place_flat(other_params.astype(jnp.bfloat16), device, devices)
    if col_width == lanes:
        merged = jnp.concatenate([attn_own.reshape(-1, lanes), other_own])
        merged = lax.all_gather(merged, everyone)
        other_all = merged[:, kinds * D :]
        attn_low = unpack_attn(merged, wide_count, narrow_count)
    else:
        attn_all = lax.all_gather(attn_own, everyone)
        other_all = lax.all_gather(other_own, everyone)
        attn_all = attn_all.reshape(wide_count, narrow_count * kinds, D, col_width)
        attn_low = attn_all.transpose(1, 2, 0, 3).reshape(narrow_count * kinds, D, D)
    other_flat = join_flat(other_all, size)
    ffn_all = lax.all_gather(ffn_mats.astype(jnp.bfloat16), everyone)
    bias_rows = V // lanes
    up_rows = bias_rows + L * FF // lanes
    vec_rows = up_rows + NV * D // lanes
    dec_bias = lax.dynamic_slice(other_flat.reshape(-1), (device * owned,), (owned,))
    dec_bias = dec_bias.astype(jnp.float32)
    up_biases = other_flat[bias_rows:up_rows].reshape(devices // 2, 2, ffn_width)
    up_biases = up_biases.transpose(1, 0, 2).reshape(L, FF).astype(jnp.float32)
    vectors = other_flat[up_rows:vec_rows].reshape(NV, D).astype(jnp.float32)
    head_weight = other_flat[vec_rows : vec_rows + D * D // lanes].reshape(D, D)

    win_count = token_ids.shape[0]
    assert win_count == 1 and SEQ == 2 * WINDOW
    group = devices // 2
    per_place = WINDOW // group
    tokens = token_ids.reshape(-1)
    token_owner = tokens // owned
    token_local = tokens - token_owner * owned
    order = jnp.arange(WINDOW, dtype=jnp.int32)
    earlier = order[None, :] < order[:, None]
    same = tokens[:, None] == tokens[None, :]
    is_first = ~jnp.any(same & earlier, axis=1)
    same_owner = token_owner[:, None] == token_owner[None, :]
    rank = jnp.sum((same_owner & earlier & is_first[None, :]).astype(jnp.int32), axis=1)
    first_slot = jnp.where(is_first, rank, 0)
    slot = jnp.sum(jnp.where(same & is_first[None, :], first_slot[None, :], 0), axis=1)

    def address(round_idx):
        there = slot - round_idx * slots
        return jnp.where((there >= 0) & (there < slots), token_owner * slots + there, -1)

    def requests(addresses):
        cells = jnp.arange(devices * slots, dtype=jnp.int32)
        hits = (cells[:, None] == addresses[None, :]) & is_first[None, :]
        return jnp.sum(jnp.where(hits, token_local[None, :] + 1, 0), axis=1)

    now = address(0)
    labels_at = slots + 2
    message = jnp.concatenate(
        [
            requests(now).reshape(devices, slots),
            jnp.broadcast_to(jnp.max(slot)[None, None], (devices, 1)),
            jnp.broadcast_to(mask_counts.reshape(1, 1), (devices, 1)),
            jnp.broadcast_to(mask_labels.reshape(1, MPW), (devices, MPW)),
            jnp.zeros((devices, lanes - labels_at - MPW), jnp.int32),
        ],
        axis=1,
    )
    message = swap_all(message)
    rounds = jnp.max(message[:, slots]) // slots + 1
    counts_all = message[:, slots + 1]
    labels_all = message[:, labels_at : labels_at + MPW].reshape(-1)
    masked_total = jnp.sum(counts_all).astype(jnp.float32)
    asked = message[:, :slots].reshape(-1) - 1
    place_rows = V - device * owned + jnp.arange(SEQ, dtype=jnp.int32)
    place_rows = select_rows(place_rows, table_low).astype(jnp.bfloat16)
    place_rows = halve(place_rows.reshape(2, group, per_place, D), side_bit, 0)
    place_parts = route_parts(place_rows, wide_count)
    for step in range(len(routes(wide_count)[0])):
        (place_parts,) = lockstep(route_step(place_parts, wide_count, step, False))
    place_own = jnp.concatenate(place_parts, axis=-1)
    place_all = gather_blocks(place_own, wide_count, 1, lanes).reshape(WINDOW, D)

    def fetch(asked_rows):
        rows = select_rows(asked_rows, table_low).astype(jnp.bfloat16)
        return swap_all(rows.reshape(devices, slots, D)).reshape(-1, D)

    def ask_again(addresses):
        return swap_all(requests(addresses).reshape(devices, slots)).reshape(-1) - 1

    fetched = fetch(asked)
    source_own = source_logits.reshape(MPW, V)
    source_max = jnp.max(source_own, axis=1).astype(jnp.float32)
    source_sum = jnp.sum(jnp.exp(source_own.astype(jnp.float32) - source_max[:, None]), axis=1)
    source_total = source_max + jnp.log(source_sum)
    source_cut = jnp.pad(source_own, ((0, 0), (0, devices * owned - V)))
    source_cut = source_cut.reshape(MPW, devices, owned).transpose(1, 0, 2)
    fetched, source_cut, source_total, place_all = lax.optimization_barrier(
        (fetched, source_cut, source_total, place_all)
    )
    if ffn_width == lanes:
        ffn_low = unpack_ffn(ffn_all, wide_count)
    else:
        ffn_low = ffn_all.reshape(devices // 2, 2, 2 * L, D, ffn_width)
        ffn_low = ffn_low.transpose(2, 3, 1, 0, 4).reshape(2 * L, D, FF)
    source_here = swap_all(source_cut)
    token_rows = select_rows(now, fetched)

    def more_rows(state):
        round_idx, rows = state
        addresses = address(round_idx)
        return (round_idx + 1, rows + select_rows(addresses, fetch(ask_again(addresses))))

    _, token_rows = lax.while_loop(
        lambda state: state[0] < rounds, more_rows, (jnp.int32(1), token_rows)
    )

    is_valid = (order[None, :] < live_lengths[:, None]) & (key_keep == 1)
    key_ok = is_valid.reshape(win_count, 1, 1, 1, WINDOW)
    bucket_ids = buckets.reshape(win_count, 1, WINDOW)
    same_bucket = bucket_ids[:, :, None, :, None] == bucket_ids[:, :, None, None, :]
    allowed = same_bucket & key_ok | jnp.eye(WINDOW, dtype=bool)
    embedded = (token_rows + place_all.astype(jnp.float32)).reshape(win_count, WINDOW, D)
    hidden, embed_pull = jax.vjp(layer_norm, embedded, vectors[0], vectors[1])
    params = (
        attn_low[0],
        attn_low[1],
        attn_low[2],
        attn_low[3],
        ffn_low[0],
        ffn_low[1],
        up_biases[0],
        vectors[2:10],
    )
    hidden, stored, shared = layer_forward(hidden, params, allowed)
    picks = mask_pos.reshape(-1)
    head_in = select_rows(picks, hidden.reshape(WINDOW, D).astype(jnp.bfloat16))
    head_in = head_in.astype(jnp.bfloat16)
    head_pre = jnp.dot(head_in, head_weight, preferred_element_type=jnp.float32) + vectors[NV - 3]
    head_out, head_pull = jax.vjp(head_tail, head_pre, vectors[NV - 2], vectors[NV - 1])
    head_low = head_out.astype(jnp.bfloat16)

    rows_all = devices * MPW
    side = lax.axis_index("side").astype(jnp.int32)
    here = here16().astype(jnp.int32)
    order_rows = jnp.arange(devices, dtype=jnp.int32)
    rank_of_dev = (order_rows % 2 ^ side) * group + (order_rows // 2 ^ here)
    dev_of_rank = (order_rows % group ^ here) * 2 + (order_rows // group ^ side)
    head_all = gather_relative(head_low, wide_count, 1, lanes)
    head_all, *shared = lax.optimization_barrier((head_all, *shared))
    head_all = jnp.concatenate([head_all, exchange(head_all, side_bit)]).reshape(rows_all, D)
    labels_all = pick_rows(labels_all.reshape(devices, MPW), dev_of_rank).reshape(rows_all, 1)
    is_live = jnp.arange(MPW, dtype=jnp.int32)[None, :] < pick_rows(counts_all[:, None], dev_of_rank)
    word_ids = device * owned + jnp.arange(owned, dtype=jnp.int32)
    is_word = (word_ids < V)[None, :]
    logits = jnp.einsum("rd,vd->rv", head_all, table_low, preferred_element_type=jnp.float32)
    logits = jnp.where(is_word, logits + dec_bias[None, :], masked_fill)
    top_here = jnp.max(logits, axis=1)
    sum_here = jnp.sum(jnp.exp(logits - top_here[:, None]), axis=1)
    stats = jnp.concatenate(
        [
            top_here.reshape(devices, MPW),
            sum_here.reshape(devices, MPW),
            jnp.zeros((devices, 2 * lanes - 2 * MPW), jnp.float32),
        ],
        axis=1,
    )
    stats, source_here = lax.optimization_barrier((stats, source_here))
    stats = swap_all(pick_rows(stats, rank_of_dev))
    tops = stats[:, :MPW]
    top = jnp.max(tops, axis=0)
    total = top + jnp.log(jnp.sum(stats[:, MPW : 2 * MPW] * jnp.exp(tops - top[None]), axis=0))
    totals = spread(jnp.concatenate([total, source_total]), devices)
    totals = pick_rows(totals, dev_of_rank)
    row_facts = jnp.concatenate(
        [
            totals[:, :MPW].reshape(rows_all, 1),
            totals[:, MPW:].reshape(rows_all, 1),
            is_live.reshape(rows_all, 1).astype(jnp.float32),
            labels_all.astype(jnp.float32),
        ],
        axis=1,
    )
    place_facts = jnp.stack([device * owned, here, side]).astype(jnp.int32)
    grad_logits, losses, grad_dec = logit_grads(
        place_facts, logits, source_here, row_facts, devices
    )
    loss_part = jnp.sum(losses)
    give = jnp.dot(grad_logits[rows_all // 2 :], table_low, preferred_element_type=jnp.float32)
    got = exchange(give, side_bit)
    keep = jnp.dot(grad_logits[: rows_all // 2], table_low, preferred_element_type=jnp.float32)
    grad_head_out = reduce_rows((keep + got).reshape(group, MPW, D), wide_count)
    grad_words = jnp.einsum("rv,rd->vd", grad_logits, head_all, preferred_element_type=jnp.float32)
    grad_head_out, grad_words = lax.optimization_barrier((grad_head_out, grad_words))

    grad_pre, grad_head_gain, grad_head_shift = head_pull(grad_head_out)
    pre_low = grad_pre.astype(jnp.bfloat16)
    grad_head_w = jnp.einsum("rd,rf->df", head_in, pre_low, preferred_element_type=jnp.float32)
    grad_head_in = jnp.einsum("rf,df->rd", pre_low, head_weight, preferred_element_type=jnp.float32)
    grad_hidden = add_rows(picks, grad_head_in, WINDOW).reshape(win_count, WINDOW, D)
    grad_hidden, layer_mats, up_grad, vec_grads = layer_backward(
        grad_hidden, stored, shared, params, allowed
    )
    grad_embed, grad_emb_gain, grad_emb_shift = embed_pull(grad_hidden)
    flat_embed = grad_embed.reshape(WINDOW, D)

    ffn_parts, attn_parts = layer_mats[1], layer_mats[0]
    (flat_embed,), ffn_parts, attn_parts = lockstep([flat_embed], ffn_parts, attn_parts)
    dec_block = jnp.zeros((devices * owned,), jnp.float32)
    dec_block = lax.dynamic_update_slice(dec_block, grad_dec, (device * owned,))[:V]
    vector_block = jnp.concatenate(
        [jnp.stack([grad_emb_gain, grad_emb_shift])]
        + [vec_grads]
        + [jnp.stack([jnp.sum(pre_low.astype(jnp.float32), 0), grad_head_gain, grad_head_shift])],
        axis=0,
    )
    front = jnp.concatenate(
        [
            dec_block.reshape(-1, lanes),
            up_grad.reshape(2, devices // 2, ffn_width).transpose(1, 0, 2).reshape(-1, lanes),
            vector_block.reshape(-1, lanes),
        ]
    )
    other_part = scatter_flat(front, grad_head_w.reshape(-1, lanes), size, devices)

    place_grad = flat_embed.reshape(group, per_place, D)
    ffn_grad = jnp.concatenate(ffn_parts, axis=1)
    sent = add_rows(now, flat_embed, devices * slots)
    arrived = swap_all(sent.reshape(devices, slots, D))
    place_parts = route_parts(place_grad.reshape(group, per_place, D), wide_count)
    steps = len(routes(wide_count)[0])
    for step in range(steps):
        place_parts, attn_parts, (other_part,) = lockstep(
            route_step(place_parts, wide_count, step, False),
            reduce_step(attn_parts, wide_count, step + 1) if step + 1 < steps else attn_parts,
            [other_step(other_part, wide_count, step)],
        )
    attn_grad = jnp.concatenate(attn_parts, axis=1)
    other_grad = own_share(other_part, size, device)
    place_grad = jnp.concatenate(place_parts, axis=-1)
    place_grad = gather_relative(place_grad, wide_count, 1, lanes)
    place_grad = jnp.concatenate([place_grad, exchange(place_grad, side_bit)])
    turn = jnp.arange(devices, dtype=jnp.int32)[:, None]
    place_ids = (turn // group ^ side) * WINDOW + (turn % group ^ here) * per_place
    place_ids = place_ids + jnp.arange(per_place, dtype=jnp.int32)[None, :]
    place_ids = (V - device * owned + place_ids).reshape(-1)
    table_grad = grad_words + add_rows(asked, arrived.reshape(-1, D), owned)
    table_grad = table_grad + add_rows(place_ids, place_grad.reshape(SEQ, D), owned)

    def more_grads(state):
        round_idx, grads = state
        addresses = address(round_idx)
        asked_rows = ask_again(addresses)
        sent = add_rows(addresses, flat_embed, devices * slots)
        arrived = swap_all(sent.reshape(devices, slots, D)).reshape(-1, D)
        return (round_idx + 1, grads + add_rows(asked_rows, arrived, owned))

    _, table_grad = lax.while_loop(
        lambda state: state[0] < rounds, more_grads, (jnp.int32(1), table_grad)
    )

    squares = square_sum((table_grad, attn_grad, ffn_grad, other_grad))
    sums = jnp.sum(spread(jnp.stack([squares, loss_part]), devices), axis=0)
    grad_norm = jnp.sqrt(sums[0]) / masked_total
    loss_value = sums[1] / masked_total
    factor = jnp.minimum(1.0, clip_limit / grad_norm)
    scaling = factor / masked_total

    attn_moment_new = mu_muon * attn_moment + attn_grad * scaling
    ffn_moment_new = mu_muon * ffn_moment + ffn_grad * scaling
    second = lax.axis_index("side") == 1
    keep = jnp.where(second, ffn_moment_new[1], ffn_moment_new[0])
    got = exchange(jnp.where(second, ffn_moment_new[0], ffn_moment_new[1]), side_bit)
    ffn_pair = jnp.concatenate([keep, got], axis=1)[None]
    attn_parts = gather_start(attn_moment_new[0].astype(jnp.bfloat16), 0, tile)
    ffn_parts = gather_start(ffn_pair[0].astype(jnp.bfloat16), 0, tile)
    steps = len(routes(wide_count)[0])
    for step in range(steps - 2):
        attn_parts, ffn_parts = lockstep(
            gather_step(attn_parts, wide_count, step, False),
            gather_step(ffn_parts, wide_count, step),
        )
    (attn_parts,) = lockstep(gather_step(attn_parts, wide_count, steps - 2, False))
    attn_gram = gram_of(gather_end(attn_parts, wide_count, 0, False))
    ffn_parts = gather_step(ffn_parts, wide_count, steps - 2)
    attn_gram, ffn_parts = tied(attn_gram, ffn_parts)
    ffn_found = gather_end(gather_step(ffn_parts, wide_count, steps - 1), wide_count, 0)
    attn_new = muon_cols(attn_mats, attn_moment_new, attn_gram, D)
    ffn_turn = newton_cols(ffn_pair, gram_of(ffn_found))[0]
    keep, give = ffn_turn[:, :ffn_width], ffn_turn[:, ffn_width:]
    got = exchange(give, side_bit)
    ffn_turn = jnp.stack([jnp.where(second, got, keep), jnp.where(second, keep, got)])
    ffn_new = ffn_mats - lr_muon * muon_shape * math.sqrt(max(D, FF)) * ffn_turn
    embed_new, embed_first_new, embed_second_new = adam_step(
        embed_table, embed_first, embed_second, table_grad * scaling
    )
    other_new, other_first_new, other_second_new = adam_step(
        other_params, other_first, other_second, other_grad * scaling
    )
    return (
        loss_value,
        grad_norm,
        embed_new,
        embed_first_new,
        embed_second_new,
        attn_new,
        attn_moment_new,
        ffn_new,
        ffn_moment_new,
        other_new,
        other_first_new,
        other_second_new,
    )


def solution(mesh):
    wide_count, narrow_count = mesh.shape["wide"], mesh.shape["narrow"]
    assert narrow_count % 2 == 0
    split = Mesh(
        np.asarray(mesh.devices).reshape(wide_count, narrow_count // 2, 2), everyone
    )
    rows, narrow = P(everyone), ("pair", "side")
    attn_spec, ffn_spec = P(narrow, None, "wide"), P(None, None, everyone)
    in_specs = (rows,) * 11 + (attn_spec,) * 2 + (ffn_spec,) * 2 + (rows,) * 3
    out_specs = (P(), P()) + (rows,) * 3 + (attn_spec,) * 2 + (ffn_spec,) * 2 + (rows,) * 3

    return jax.shard_map(
        shards, mesh=split, in_specs=in_specs, out_specs=out_specs, check_vma=False
    )
```

```python
import functools
import math

import jax
import jax.numpy as jnp
import numpy as np
from jax import lax
from jax.experimental import pallas as pl
from jax.experimental.pallas import tpu as pltpu
from jax.sharding import Mesh
from jax.sharding import PartitionSpec as P

D = 1024
FF = 4096
HEADS = 16
L = 1
V = 30720
SEQ = 1024
WINDOW = 512
NS_ITERS = 3
ADAM_STEP = 5
MPW = 80
NV = 13


high = lax.Precision.HIGH
lanes = 128
tile = 16
slots = 32
ln_eps = 1e-05
masked_fill = -1e30
clip_limit = 0.3
ns_a = 3.4445
ns_b = -4.775
ns_c = 2.0315
mu_muon = 0.95
lr_muon = 0.1
muon_shape = 0.2
lr_adam = 0.01
beta_one = 0.9
beta_two = 0.999
adam_eps = 1e-08


def layer_norm(inputs, gain_vec, shift_vec):
    center = inputs - jnp.mean(inputs, -1, keepdims=True)
    spread = jnp.mean(center * center, -1, keepdims=True)
    return center * lax.rsqrt(spread + ln_eps) * gain_vec + shift_vec


def exact_gelu(inputs):
    return jax.nn.gelu(inputs, approximate=False)


def head_tail(head_pre, gain_vec, shift_vec):
    return layer_norm(exact_gelu(head_pre), gain_vec, shift_vec)


def project(inputs, weight):
    return jnp.einsum("bsd,df->bsf", inputs, weight, preferred_element_type=jnp.float32)


def project_back(gradients, weight):
    return jnp.einsum("bsf,df->bsd", gradients, weight, preferred_element_type=jnp.float32)


def col_sum(inputs):
    return jnp.sum(inputs.astype(jnp.float32), axis=(0, 1))


def share(values, axis):
    return jnp.concatenate([values, exchange(values, side_bit)], axis=axis)


def swap_pick(for_first, for_second, axis):
    first = lax.axis_index("side") == 0
    keep = jnp.where(first, for_first, for_second)
    got = exchange(jnp.where(first, for_second, for_first), side_bit)
    return jnp.concatenate([keep, got], axis=axis)


def share_half(values):
    side = lax.axis_index("side")
    half = values.shape[1] // 2
    keep = lax.dynamic_slice_in_dim(values, side * half, half, axis=1)
    got = exchange(lax.dynamic_slice_in_dim(values, (1 - side) * half, half, axis=1), side_bit)
    return jnp.concatenate([keep, got])


def head_scores(q_ref, k_ref, allow_ref, cols):
    scores = lax.dot_general(
        q_ref[:, cols], k_ref[:, cols], (((1,), (1,)), ((), ())), preferred_element_type=jnp.float32
    )
    return jnp.where(allow_ref[...] > 0.0, scores * (D // HEADS) ** (-0.5), masked_fill)


def attend_kernel(q_ref, k_ref, v_ref, allow_ref, out_ref, total_ref):
    width = D // HEADS
    for head in range(q_ref.shape[1] // width):
        cols = slice(head * width, (head + 1) * width)
        scores = head_scores(q_ref, k_ref, allow_ref, cols)
        top = jnp.max(scores, axis=1, keepdims=True)
        total = top + jnp.log(jnp.sum(jnp.exp(scores - top), axis=1, keepdims=True))
        probs = jnp.exp(scores - total).astype(jnp.bfloat16)
        found = jnp.dot(probs, v_ref[:, cols], preferred_element_type=jnp.float32)
        out_ref[:, cols] = found.astype(jnp.bfloat16)
        total_ref[head] = total


def attend_back_kernel(
    q_ref, k_ref, v_ref, allow_ref, total_ref, grad_ref, q_out, k_out, v_out
):
    width = D // HEADS
    rows = (((0,), (0,)), ((), ()))
    for head in range(q_ref.shape[1] // width):
        cols = slice(head * width, (head + 1) * width)
        grads = grad_ref[:, cols]
        probs = jnp.exp(head_scores(q_ref, k_ref, allow_ref, cols) - total_ref[head])
        grad_probs = lax.dot_general(
            grads, v_ref[:, cols], (((1,), (1,)), ((), ())), preferred_element_type=jnp.float32
        )
        grad_value = lax.dot_general(
            probs.astype(jnp.bfloat16), grads, rows, preferred_element_type=jnp.float32
        )
        inner = jnp.sum(grad_probs * probs, axis=1, keepdims=True)
        raw = (probs * (grad_probs - inner) * width ** (-0.5)).astype(jnp.bfloat16)
        grad_query = jnp.dot(raw, k_ref[:, cols], preferred_element_type=jnp.float32)
        grad_key = lax.dot_general(
            raw, q_ref[:, cols], rows, preferred_element_type=jnp.float32
        )
        q_out[:, cols] = grad_query.astype(jnp.bfloat16)
        k_out[:, cols] = grad_key.astype(jnp.bfloat16)
        v_out[:, cols] = grad_value.astype(jnp.bfloat16)


def attend(queries, key_proj, values, allow):
    pair = lanes * HEADS // D
    cols = pl.BlockSpec((WINDOW, lanes), lambda step: (0, step))
    whole = pl.BlockSpec((WINDOW, WINDOW), lambda step: (0, 0))
    return pl.pallas_call(
        attend_kernel,
        grid=(D // lanes,),
        in_specs=[cols, cols, cols, whole],
        out_specs=[cols, pl.BlockSpec((pair, WINDOW, 1), lambda step: (step, 0, 0))],
        out_shape=[
            jax.ShapeDtypeStruct((WINDOW, D), jnp.bfloat16),
            jax.ShapeDtypeStruct((HEADS, WINDOW, 1), jnp.float32),
        ],
    )(queries, key_proj, values, allow)


def attend_back(queries, key_proj, values, allow, totals, grads):
    pair = lanes * HEADS // D
    cols = pl.BlockSpec((WINDOW, lanes), lambda step: (0, step))
    whole = pl.BlockSpec((WINDOW, WINDOW), lambda step: (0, 0))
    total = pl.BlockSpec((pair, WINDOW, 1), lambda step: (step, 0, 0))
    return pl.pallas_call(
        attend_back_kernel,
        grid=(D // lanes,),
        in_specs=[cols, cols, cols, whole, total, cols],
        out_specs=[cols] * 3,
        out_shape=[jax.ShapeDtypeStruct((WINDOW, D), jnp.bfloat16)] * 3,
    )(queries, key_proj, values, allow, totals, grads)


def layer_forward(hidden, params, allowed):
    w_query, w_key, w_value, w_out, w_up, w_down, up_bias, vectors = params
    inputs = hidden.astype(jnp.bfloat16)
    queries = (project(inputs, w_query) + vectors[4]).astype(jnp.bfloat16)
    key_proj = project(inputs, w_key).astype(jnp.bfloat16)
    values = (project(inputs, w_value) + vectors[5]).astype(jnp.bfloat16)
    context, log_total = attend(queries[0], key_proj[0], values[0], allowed)
    context = context[None]
    attn_sum = hidden + (project(context, w_out) + vectors[6])
    middle, first_pull = jax.vjp(layer_norm, attn_sum, vectors[0], vectors[1])
    middle_low = middle.astype(jnp.bfloat16)
    up_proj = project(middle_low, w_up) + up_bias
    activated, gelu_pull = jax.vjp(exact_gelu, up_proj)
    act_low = activated.astype(jnp.bfloat16)
    ffn_sum = middle + (project_back(act_low, w_down) + vectors[7])
    output, second_pull = jax.vjp(layer_norm, ffn_sum, vectors[2], vectors[3])
    stored = (
        inputs,
        queries,
        key_proj,
        values,
        log_total,
        context,
        first_pull,
        middle_low,
        gelu_pull,
        act_low,
        second_pull,
    )
    shared = (
        share(middle_low[0].T, 1),
        share_half(act_low[0]),
        share(inputs[0].T, 1),
        swap_pick(inputs[0].T, context[0].T, 1),
    )
    return (output, stored, shared)


def layer_backward(grad_out, stored, shared, params, allowed):
    w_query, w_key, w_value, w_out, w_up, w_down, _, _ = params
    (_, queries, key_proj, values, log_total, _, first_pull, _, gelu_pull, _, second_pull) = stored
    grad_ffn, grad_gain_two, grad_shift_two = second_pull(grad_out)
    down_low = grad_ffn.astype(jnp.bfloat16)
    (grad_up,) = gelu_pull(project(down_low, w_down))
    up_low = grad_up.astype(jnp.bfloat16)
    wide_count = lax.axis_size("wide")
    operands = (
        shared[0],
        share(down_low[0].T, 1),
        share_half(up_low[0]),
        shared[1],
    )
    if FF // (4 * wide_count) == lanes:
        grad_mats_ffn = ffn_weight_grads(*operands, wide_count)
    else:
        blocks = jnp.stack([jnp.dot(*operands[::2], preferred_element_type=jnp.float32),
                            jnp.dot(*operands[1::2], preferred_element_type=jnp.float32)])
        blocks = blocks.reshape(2, D, wide_count, 2, -1).transpose(2, 3, 0, 1, 4)
        grad_mats_ffn = in_routes(blocks, wide_count)
    grad_ffn, parts = tied(grad_ffn, grad_mats_ffn)
    parts = reduce_step(parts, wide_count, 0)
    grad_middle = grad_ffn + project_back(up_low, w_up)
    grad_attn, grad_gain_one, grad_shift_one = first_pull(grad_middle)
    attn_low = grad_attn.astype(jnp.bfloat16)
    grad_context = project_back(attn_low, w_out).astype(jnp.bfloat16)
    grads = attend_back(queries[0], key_proj[0], values[0], allowed, log_total, grad_context[0])
    grad_query, grad_key, grad_value = (found[None] for found in grads)
    grad_query, parts = tied(grad_query, parts)
    parts = reduce_step(parts, wide_count, 1)
    operands = (
        shared[2],
        shared[3],
        swap_pick(grad_query[0], grad_key[0], 0),
        swap_pick(grad_value[0], attn_low[0], 0),
    )
    if D // wide_count == lanes:
        attn_parts = attn_weight_grads(*operands, wide_count)
    else:
        blocks = jnp.stack([jnp.dot(*operands[::2], preferred_element_type=jnp.float32),
                            jnp.dot(*operands[1::2], preferred_element_type=jnp.float32)])
        blocks = blocks.reshape(2, 1, D, wide_count, -1).transpose(3, 0, 1, 2, 4)
        attn_parts = in_routes(blocks, wide_count)
    grad_hidden = (
        grad_attn
        + project_back(grad_query, w_query)
        + project_back(grad_key, w_key)
        + project_back(grad_value, w_value)
    )
    grad_hidden, parts = tied(grad_hidden, parts)
    parts = reduce_step(parts, wide_count, 2)
    matrices = (attn_parts, parts)
    vector_grads = jnp.stack(
        [
            grad_gain_one,
            grad_shift_one,
            grad_gain_two,
            grad_shift_two,
            col_sum(grad_query),
            col_sum(grad_value),
            col_sum(attn_low),
            col_sum(down_low),
        ]
    )
    return (grad_hidden, matrices, col_sum(up_low), vector_grads)


def slab_product(matrix, columns):
    return jnp.einsum(
        "kde,kec->kdc", matrix, columns, precision=high, preferred_element_type=jnp.float32
    )


def newton_cols(moment, gram):
    norms = jnp.sqrt(jnp.trace(gram, axis1=1, axis2=2))
    scaling = 1.0 / (norms + 1e-07)
    current = moment * scaling[:, None, None]
    gram = gram * (scaling * scaling)[:, None, None]
    for step_idx in range(NS_ITERS):
        if step_idx + 1 < NS_ITERS:
            poly = ns_b * gram + ns_c * jnp.einsum("kde,kef->kdf", gram, gram)
            current = ns_a * current + slab_product(poly, current)
            half = ns_a * gram + jnp.einsum("kde,kef->kdf", poly, gram)
            gram = ns_a * half + jnp.einsum("kde,kef->kdf", half, poly)
        else:
            once = slab_product(gram, current)
            current = ns_a * current + ns_b * once + ns_c * slab_product(gram, once)
    return current


def gram_of(found):
    return jnp.einsum("wdc,wec->de", found, found, preferred_element_type=jnp.float32)[None]


def relative_order(part, taken):
    names = [bit for bit in wide_bits(lax.axis_size("wide"))[::-1] + [("pair", 1)] if bit in taken]
    dims = [names.index(bit) for bit in taken[::-1]]
    split = part.reshape((2,) * len(taken) + part.shape[1:])
    turn = [dims.index(place) for place in range(len(taken))]
    split = split.transpose(turn + list(range(len(taken), split.ndim)))
    return split.reshape(part.shape)


def muon_cols(master, new_moment, gram, long_side):
    change = lr_muon * muon_shape * math.sqrt(long_side) * newton_cols(new_moment, gram)
    return master - change


def adam_step(master, first_moment, second, gradient):
    new_first = beta_one * first_moment + (1.0 - beta_one) * gradient
    new_second = beta_two * second + (1.0 - beta_two) * gradient * gradient
    first_hat = new_first / (1.0 - beta_one**ADAM_STEP)
    second_hat = new_second / (1.0 - beta_two**ADAM_STEP)
    return (master - lr_adam * first_hat / (jnp.sqrt(second_hat) + adam_eps), new_first, new_second)


def square_sum(arrays):
    running = jnp.zeros((), jnp.float32)
    for member in arrays:
        running = running + jnp.sum(member * member)
    return running


everyone = ("wide", "pair", "side")
side_bit = ("side", 1)


def swap_all(blocks, axes=everyone):
    return lax.all_to_all(blocks, axes, 0, 0, tiled=True)


def spread(values, devices):
    size = values.shape[0]
    row = jnp.pad(values, (0, -size % lanes))
    return swap_all(jnp.broadcast_to(row[None], (devices, row.shape[0])))[:, :size]


def wide_bits(wide_count):
    return [("wide", 1 << k) for k in range(wide_count.bit_length() - 1)]


def routes(wide_count, with_pair=True):
    bits = wide_bits(wide_count)
    near, far, across = bits[:1], bits[1:], [("pair", 1)] if with_pair else []
    last = far[1:]
    return [across + near + far, near + far[:1] + across + last, far[:1] + across + near + last]


def my_bit(bit):
    axis, mask = bit
    return lax.axis_index(axis) // mask % 2


def exchange(values, bit):
    axis, mask = bit
    steps = [(here, here ^ mask) for here in range(lax.axis_size(axis))]
    return lax.ppermute(values, axis, steps)


def halve(values, bit, dim):
    mine = lax.dynamic_index_in_dim(values, my_bit(bit), dim, keepdims=False)
    theirs = lax.dynamic_index_in_dim(values, 1 - my_bit(bit), dim, keepdims=False)
    return mine + exchange(theirs, bit)


def double(values, bit, dim):
    theirs = exchange(values, bit)
    first = my_bit(bit) == 0
    pair = [jnp.where(first, values, theirs), jnp.where(first, theirs, values)]
    return jnp.stack(pair, axis=dim)


def cuts(length, unit):
    whole = length // unit
    sizes = [(whole + 2) // 3 * unit, (whole + 1) // 3 * unit]
    sizes.append(length - sum(sizes))
    starts = [0, sizes[0], sizes[0] + sizes[1]]
    return [(start, start + size) for start, size in zip(starts, sizes) if size]


def here16():
    return lax.axis_index("wide") * 2 + lax.axis_index("pair")


def lockstep(*groups):
    flat = lax.optimization_barrier(sum((list(group) for group in groups), []))
    found = []
    for group in groups:
        found.append(flat[: len(group)])
        flat = flat[len(group) :]
    return found


def reduce_step(parts, wide_count, step):
    return [
        part[0] + exchange(part[1], route[step])
        for part, route in zip(parts, routes(wide_count))
    ]


def tied(value, parts):
    value, *parts = lax.optimization_barrier((value, *parts))
    return value, parts


def static_step(part, left, bit):
    dim = left.index(bit)
    keep = lax.index_in_dim(part, 0, dim, keepdims=False)
    return keep + exchange(lax.index_in_dim(part, 1, dim, keepdims=False), bit)


def route_parts(values, wide_count):
    bits = wide_bits(wide_count)[::-1] + [("pair", 1)]
    return [
        values[..., start:stop].reshape((2,) * len(bits) + (values.shape[1], stop - start))
        for start, stop in cuts(values.shape[-1], lanes)
    ]


def route_step(parts, wide_count, step, static):
    bits = wide_bits(wide_count)[::-1] + [("pair", 1)]
    found = []
    for part, route in zip(parts, routes(wide_count)):
        left = [bit for bit in bits if bit not in route[:step]]
        if static:
            found.append(static_step(part, left, route[step]))
        else:
            found.append(halve(part, route[step], left.index(route[step])))
    return found


def reduce_rows(values, wide_count):
    parts = route_parts(values, wide_count)
    for step in range(len(routes(wide_count)[0])):
        (parts,) = lockstep(route_step(parts, wide_count, step, True))
    return jnp.concatenate(parts, axis=-1)


def gather_start(block, axis, unit):
    return [
        lax.slice_in_dim(block, start, stop, axis=axis)[None]
        for start, stop in cuts(block.shape[axis], unit)
    ]


def gather_step(parts, wide_count, step, with_pair=True):
    return [
        jnp.concatenate([part, exchange(part, route[::-1][step])])
        for part, route in zip(parts, routes(wide_count, with_pair))
    ]


def gather_end(parts, wide_count, axis, with_pair=True):
    ordered = [
        relative_order(part, route[::-1])
        for part, route in zip(parts, routes(wide_count, with_pair))
    ]
    return jnp.concatenate(ordered, axis=1 + axis)


def gather_relative(block, wide_count, axis, unit):
    parts = gather_start(block, axis, unit)
    for step in range(len(routes(wide_count)[0])):
        (parts,) = lockstep(gather_step(parts, wide_count, step))
    return gather_end(parts, wide_count, axis)


def route_shape(route, covered):
    wide = [bit for bit in route if bit not in covered]
    shape = tuple(2 if bit in covered else 1 for bit in route)

    def index(step):
        low = 1 << len(covered) - 1
        return tuple(
            0 if bit in covered else step * low // bit[1] % 2 for bit in route
        )

    assert wide
    return shape, index


def weight_grads(kernel, operands, column_specs, covered, steps, members, wide_count):
    here = jnp.stack([lax.axis_index("wide"), lax.axis_index("pair")]).astype(jnp.int32)
    shapes, specs = [], []
    for route, (start, stop) in zip(routes(wide_count), cuts(D, tile)):
        block, index = route_shape(route, covered)
        tail = (members, stop - start, lanes)
        shapes.append(jax.ShapeDtypeStruct((2,) * len(route) + tail, jnp.float32))
        specs.append(
            pl.BlockSpec(block + tail, lambda step, _, index=index: index(step) + (0, 0, 0))
        )
    return pl.pallas_call(
        kernel,
        grid_spec=pltpu.PrefetchScalarGridSpec(
            num_scalar_prefetch=1, grid=(steps,), in_specs=column_specs, out_specs=specs
        ),
        out_shape=shapes,
    )(here, *operands)


def put(refs, wide_count, covered, where, member, values):
    for ref, route, (start, stop) in zip(refs, routes(wide_count), cuts(D, tile)):
        place = tuple(where[bit] if bit in covered else 0 for bit in route)
        ref[place + (member,)] = values[start:stop]


def ffn_grads_kernel(here, up_rows, down_rows, up_cols, down_cols, *refs, wide_count):
    flip = here[1] == 0
    pair = ("pair", 1)
    for member, (rows, cols) in enumerate(((up_rows, up_cols), (down_rows, down_cols))):
        both = jnp.dot(rows[...], cols[...], preferred_element_type=jnp.float32)
        low, top = both[:, :lanes], both[:, lanes:]
        put(refs, wide_count, [pair], {pair: 0}, member, jnp.where(flip, low, top))
        put(refs, wide_count, [pair], {pair: 1}, member, jnp.where(flip, top, low))


def ffn_weight_grads(up_rows, down_rows, up_cols, down_cols, wide_count):
    whole = pl.BlockSpec(up_rows.shape, lambda step, here: (0, 0))
    cols = pl.BlockSpec((up_cols.shape[0], 2 * lanes), lambda step, here: (0, step ^ here[0]))
    kernel = functools.partial(ffn_grads_kernel, wide_count=wide_count)
    operands = (up_rows, down_rows, up_cols, down_cols)
    specs = [whole, whole, cols, cols]
    return weight_grads(kernel, operands, specs, [("pair", 1)], wide_count, 2, wide_count)


def attn_grads_kernel(here, one_rows, two_rows, one_cols, two_cols, *refs, wide_count):
    swap = here[0] % 2 == 0
    flip = here[1] == 0
    pair, near = ("pair", 1), ("wide", 1)
    blocks = []
    for rows, cols in ((one_rows, one_cols), (two_rows, two_cols)):
        both = jnp.dot(rows[...], cols[...], preferred_element_type=jnp.float32)
        low, top = both[:, :lanes], both[:, lanes:]
        blocks.append((jnp.where(swap, low, top), jnp.where(swap, top, low)))
    for step in range(2):
        one, two = blocks[0][step], blocks[1][step]
        first, second = jnp.where(flip, one, two), jnp.where(flip, two, one)
        put(refs, wide_count, [pair, near], {pair: 0, near: step}, 0, first)
        put(refs, wide_count, [pair, near], {pair: 1, near: step}, 0, second)


def attn_weight_grads(one_rows, two_rows, one_cols, two_cols, wide_count):
    whole = pl.BlockSpec(one_rows.shape, lambda step, here: (0, 0))
    cols = pl.BlockSpec((one_cols.shape[0], 2 * lanes), lambda step, here: (0, step ^ here[0] // 2))
    kernel = functools.partial(attn_grads_kernel, wide_count=wide_count)
    operands = (one_rows, two_rows, one_cols, two_cols)
    specs = [whole, whole, cols, cols]
    covered = [("pair", 1), ("wide", 1)]
    return weight_grads(kernel, operands, specs, covered, wide_count // 2, 1, wide_count)


def in_routes(blocks, wide_count):
    count = wide_count * 2
    order = jnp.arange(count) ^ here16()
    blocks = jnp.take(blocks.reshape((count,) + blocks.shape[2:]), order, axis=0)
    bits = wide_bits(wide_count)[::-1] + [("pair", 1)]
    parts = []
    for route, (start, stop) in zip(routes(wide_count), cuts(D, tile)):
        part = blocks[:, :, start:stop].reshape((2,) * len(bits) + blocks[:, :, start:stop].shape[1:])
        dims = [bits.index(bit) for bit in route]
        parts.append(part.transpose(dims + list(range(len(bits), part.ndim))))
    return parts


def gather_blocks(block, wide_count, axis, unit):
    bits = wide_bits(wide_count)[::-1] + [("pair", 1)]
    parts = []
    for route, (start, stop) in zip(routes(wide_count), cuts(block.shape[axis], unit)):
        part = lax.slice_in_dim(block, start, stop, axis=axis)
        have = []
        for bit in route[::-1]:
            have = sorted(have + [bit], key=bits.index)
            part = double(part, bit, have.index(bit))
        parts.append(part.reshape((wide_count, 2) + part.shape[len(bits) :]))
    return jnp.concatenate(parts, axis=2 + axis)


def select_rows(index, rows, precision=None):
    hits = index[:, None] == jnp.arange(rows.shape[0], dtype=jnp.int32)[None, :]
    return jnp.dot(
        hits.astype(rows.dtype), rows, precision=precision, preferred_element_type=jnp.float32
    )


def logit_grads_kernel(facts, logits_ref, source_ref, rows_ref, grad_ref, loss_ref, dec_ref):
    step = pl.program_id(0)

    @pl.when(step == 0)
    def _():
        loss_ref[...] = jnp.zeros_like(loss_ref)
        dec_ref[...] = jnp.zeros_like(dec_ref)

    columns = lax.broadcasted_iota(jnp.int32, logits_ref.shape, 1) + facts[0]
    is_word = columns < V
    rows = rows_ref[...]
    log_prob = logits_ref[...] - rows[:, 0:1]
    source_log = source_ref[0].astype(jnp.float32) - rows[:, 1:2]
    source_prob = jnp.where(is_word, jnp.exp(source_log), 0.0)
    hits = columns == rows[:, 3:4].astype(jnp.int32)
    keep = is_word & (rows[:, 2:3] > 0.5)
    losses = source_prob * (source_log - log_prob) - jnp.where(hits, log_prob, 0.0)
    loss_ref[...] += jnp.sum(jnp.where(keep, losses, 0.0), axis=0, keepdims=True)
    grads = 2.0 * jnp.exp(log_prob) - jnp.where(hits, 1.0, 0.0) - source_prob
    grads = jnp.where(keep, grads, 0.0).astype(jnp.bfloat16)
    grad_ref[...] = grads
    dec_ref[...] += jnp.sum(grads.astype(jnp.float32), axis=0, keepdims=True)


def logit_grads(facts, logits, source, row_facts, devices):
    owned = logits.shape[1]
    group = devices // 2

    def source_block(step, facts):
        return ((step % group ^ facts[1]) * 2 + (step // group ^ facts[2]), 0, 0)

    line = pl.BlockSpec((1, owned), lambda step, facts: (0, 0))
    grads, losses, dec = pl.pallas_call(
        logit_grads_kernel,
        grid_spec=pltpu.PrefetchScalarGridSpec(
            num_scalar_prefetch=1,
            grid=(devices,),
            in_specs=[
                pl.BlockSpec((MPW, owned), lambda step, facts: (step, 0)),
                pl.BlockSpec((1, MPW, owned), source_block),
                pl.BlockSpec((MPW, 4), lambda step, facts: (step, 0)),
            ],
            out_specs=[pl.BlockSpec((MPW, owned), lambda step, facts: (step, 0)), line, line],
        ),
        out_shape=[
            jax.ShapeDtypeStruct(logits.shape, jnp.bfloat16),
            jax.ShapeDtypeStruct((1, owned), jnp.float32),
            jax.ShapeDtypeStruct((1, owned), jnp.float32),
        ],
    )(facts, logits, source, row_facts)
    return grads, losses, dec[0]


def pick_rows(values, index):
    hits = index[:, None] == jnp.arange(values.shape[0], dtype=jnp.int32)[None, :]
    return jnp.sum(jnp.where(hits[:, :, None], values[None], 0), axis=1)


def add_rows(index, rows, count):
    hits = jnp.arange(count, dtype=jnp.int32)[:, None] == index[None, :]
    return jnp.dot(
        hits.astype(rows.dtype), rows, precision=high, preferred_element_type=jnp.float32
    )


def flat_blocks(size, devices):
    total = size * devices
    starts = [dev * size // (tile * lanes) * tile for dev in range(devices)] + [total // lanes]
    ends = [-(-(dev + 1) * size // (tile * lanes)) * tile for dev in range(devices)]
    rows = max(end - start for start, end in zip(starts, ends))
    return starts, rows


def place_flat(share, device, devices):
    size = share.shape[0]
    _, rows = flat_blocks(size, devices)
    offset = device * size % (tile * lanes)
    block = lax.dynamic_update_slice(jnp.zeros((rows * lanes,), share.dtype), share, (offset,))
    return block.reshape(rows, lanes)


def join_kernel(blocks_ref, out_ref, *, starts):
    rows = blocks_ref.shape[1]
    for dev in range(len(starts) - 1):
        length = starts[dev + 1] - starts[dev]
        out_ref[starts[dev] : starts[dev + 1]] = blocks_ref[dev, :length]
    for dev in range(1, len(starts) - 1):
        length = starts[dev] - starts[dev - 1]
        if length < rows:
            shared = slice(starts[dev], starts[dev] + tile)
            both = blocks_ref[dev, :tile].astype(jnp.float32)
            both += blocks_ref[dev - 1, length : length + tile].astype(jnp.float32)
            out_ref[shared] = both.astype(out_ref.dtype)


def join_flat(blocks, size):
    starts, _ = flat_blocks(size, blocks.shape[0])
    starts[-1] += -starts[-1] % tile
    return pl.pallas_call(
        functools.partial(join_kernel, starts=starts),
        out_shape=jax.ShapeDtypeStruct((starts[-1], lanes), blocks.dtype),
    )(blocks)


def unpack_kernel(*refs):
    half = len(refs) * 2 // 3
    for place, out_ref in enumerate(refs[half:]):
        out_ref[:, :lanes] = refs[2 * place][...].reshape(D, lanes)
        out_ref[:, lanes:] = refs[2 * place + 1][...].reshape(D, lanes)


def unpack_attn(merged, wide_count, narrow_count):
    specs = [
        pl.BlockSpec((1, D, lanes), lambda step, add=step_add, kind=kind: (
            (2 * step + add) * narrow_count + kind, 0, 0
        ))
        for kind in range(narrow_count)
        for step_add in range(2)
    ]
    return pl.pallas_call(
        unpack_kernel,
        grid=(wide_count // 2,),
        in_specs=specs,
        out_specs=[pl.BlockSpec((D, 2 * lanes), lambda step: (0, step))] * narrow_count,
        out_shape=[jax.ShapeDtypeStruct((D, D), merged.dtype)] * narrow_count,
    )(*[merged] * len(specs))


def unpack_ffn(blocks, wide_count):
    specs = [
        pl.BlockSpec((1, 1, D, lanes), lambda step, kind=kind, pair=pair: (
            step % wide_count * 4 + pair * 2 + step // wide_count, kind, 0, 0
        ))
        for kind in range(2)
        for pair in range(2)
    ]
    return pl.pallas_call(
        unpack_kernel,
        grid=(2 * wide_count,),
        in_specs=specs,
        out_specs=[pl.BlockSpec((D, 2 * lanes), lambda step: (0, step))] * 2,
        out_shape=[jax.ShapeDtypeStruct((D, FF), blocks.dtype)] * 2,
    )(*[blocks] * 4)


def split_kernel(front_ref, rest_ref, out_ref, *, starts):
    front, rows = front_ref.shape[0], out_ref.shape[1]
    total = front + rest_ref.shape[0]
    for dev, start in enumerate(starts[:-1]):
        stop = min(start + rows, total)
        middle = min(max(start, front), stop)
        if start < middle:
            out_ref[dev, : middle - start] = front_ref[start:middle]
        if middle < stop:
            out_ref[dev, middle - start : stop - start] = rest_ref[middle - front : stop - front]
        if stop < start + rows:
            left = start + rows - stop
            out_ref[dev, rows - left :] = jnp.zeros((left, lanes), out_ref.dtype)


def scatter_flat(front, rest, size, devices):
    wide_count = lax.axis_size("wide")
    starts, rows = flat_blocks(size, devices)
    blocks = pl.pallas_call(
        functools.partial(split_kernel, starts=starts),
        out_shape=jax.ShapeDtypeStruct((devices, rows, lanes), front.dtype),
    )(front, rest)
    bits = wide_bits(wide_count)[::-1] + [("pair", 1), side_bit]
    part = blocks.reshape((2,) * len(bits) + blocks.shape[1:])
    return halve(part, side_bit, len(bits) - 1)


def other_step(part, wide_count, step):
    bits = wide_bits(wide_count)[::-1] + [("pair", 1)]
    route = routes(wide_count)[0]
    left = [bit for bit in bits if bit not in route[:step]]
    return halve(part, route[step], left.index(route[step]))


def own_share(part, size, device):
    return lax.dynamic_slice(part.reshape(-1), (device * size % (tile * lanes),), (size,))


def shards(
    token_ids,
    live_lengths,
    key_keep,
    buckets,
    mask_pos,
    mask_labels,
    mask_counts,
    source_logits,
    embed_table,
    embed_first,
    embed_second,
    attn_mats,
    attn_moment,
    ffn_mats,
    ffn_moment,
    other_params,
    other_first,
    other_second,
):
    wide_count = lax.axis_size("wide")
    narrow_count = lax.axis_size("pair") * 2
    devices = wide_count * narrow_count
    device = lax.axis_index(everyone).astype(jnp.int32)
    owned = embed_table.shape[0]
    size = other_params.shape[0]
    col_width = attn_mats.shape[2]
    ffn_width = ffn_mats.shape[2]
    kinds = attn_mats.shape[0]
    table_low = embed_table.astype(jnp.bfloat16)

    attn_own = attn_mats.astype(jnp.bfloat16)
    other_own = place_flat(other_params.astype(jnp.bfloat16), device, devices)
    if col_width == lanes:
        merged = jnp.concatenate([attn_own.reshape(-1, lanes), other_own])
        merged = lax.all_gather(merged, everyone)
        other_all = merged[:, kinds * D :]
        attn_low = unpack_attn(merged, wide_count, narrow_count)
    else:
        attn_all = lax.all_gather(attn_own, everyone)
        other_all = lax.all_gather(other_own, everyone)
        attn_all = attn_all.reshape(wide_count, narrow_count * kinds, D, col_width)
        attn_low = attn_all.transpose(1, 2, 0, 3).reshape(narrow_count * kinds, D, D)
    other_flat = join_flat(other_all, size)
    ffn_all = lax.all_gather(ffn_mats.astype(jnp.bfloat16), everyone)
    bias_rows = V // lanes
    up_rows = bias_rows + L * FF // lanes
    vec_rows = up_rows + NV * D // lanes
    dec_bias = lax.dynamic_slice(other_flat.reshape(-1), (device * owned,), (owned,))
    dec_bias = dec_bias.astype(jnp.float32)
    up_biases = other_flat[bias_rows:up_rows].reshape(devices // 2, 2, ffn_width)
    up_biases = up_biases.transpose(1, 0, 2).reshape(L, FF).astype(jnp.float32)
    vectors = other_flat[up_rows:vec_rows].reshape(NV, D).astype(jnp.float32)
    head_weight = other_flat[vec_rows : vec_rows + D * D // lanes].reshape(D, D)

    win_count = token_ids.shape[0]
    assert win_count == 1 and SEQ == 2 * WINDOW
    group = devices // 2
    per_place = WINDOW // group
    tokens = token_ids.reshape(-1)
    token_owner = tokens // owned
    token_local = tokens - token_owner * owned
    order = jnp.arange(WINDOW, dtype=jnp.int32)
    earlier = order[None, :] < order[:, None]
    same = tokens[:, None] == tokens[None, :]
    is_first = ~jnp.any(same & earlier, axis=1)
    same_owner = token_owner[:, None] == token_owner[None, :]
    rank = jnp.sum((same_owner & earlier & is_first[None, :]).astype(jnp.int32), axis=1)
    first_slot = jnp.where(is_first, rank, 0)
    slot = jnp.sum(jnp.where(same & is_first[None, :], first_slot[None, :], 0), axis=1)

    def address(round_idx):
        there = slot - round_idx * slots
        return jnp.where((there >= 0) & (there < slots), token_owner * slots + there, -1)

    def requests(addresses):
        cells = jnp.arange(devices * slots, dtype=jnp.int32)
        hits = (cells[:, None] == addresses[None, :]) & is_first[None, :]
        return jnp.sum(jnp.where(hits, token_local[None, :] + 1, 0), axis=1)

    now = address(0)
    labels_at = slots + 2
    message = jnp.concatenate(
        [
            requests(now).reshape(devices, slots),
            jnp.broadcast_to(jnp.max(slot)[None, None], (devices, 1)),
            jnp.broadcast_to(mask_counts.reshape(1, 1), (devices, 1)),
            jnp.broadcast_to(mask_labels.reshape(1, MPW), (devices, MPW)),
            jnp.zeros((devices, lanes - labels_at - MPW), jnp.int32),
        ],
        axis=1,
    )
    message = swap_all(message)
    rounds = jnp.max(message[:, slots]) // slots + 1
    counts_all = message[:, slots + 1]
    labels_all = message[:, labels_at : labels_at + MPW].reshape(-1)
    masked_total = jnp.sum(counts_all).astype(jnp.float32)
    asked = message[:, :slots].reshape(-1) - 1
    place_rows = V - device * owned + jnp.arange(SEQ, dtype=jnp.int32)
    place_rows = select_rows(place_rows, table_low).astype(jnp.bfloat16)
    place_rows = halve(place_rows.reshape(2, group, per_place, D), side_bit, 0)
    place_parts = route_parts(place_rows, wide_count)
    for step in range(len(routes(wide_count)[0])):
        place_parts = route_step(place_parts, wide_count, step, False)
        if step == 0:
            place_parts, (source_own,) = lockstep(
                place_parts, [source_logits.reshape(MPW, V)]
            )
        else:
            (place_parts,) = lockstep(place_parts)
    place_own = jnp.concatenate(place_parts, axis=-1)
    place_all = gather_blocks(place_own, wide_count, 1, lanes).reshape(WINDOW, D)

    def fetch(asked_rows):
        rows = select_rows(asked_rows, table_low).astype(jnp.bfloat16)
        return swap_all(rows.reshape(devices, slots, D)).reshape(-1, D)

    def ask_again(addresses):
        return swap_all(requests(addresses).reshape(devices, slots)).reshape(-1) - 1

    fetched = fetch(asked)
    source_max = jnp.max(source_own, axis=1).astype(jnp.float32)
    source_sum = jnp.sum(jnp.exp(source_own.astype(jnp.float32) - source_max[:, None]), axis=1)
    source_total = source_max + jnp.log(source_sum)
    source_cut = jnp.pad(source_own, ((0, 0), (0, devices * owned - V)))
    source_cut = source_cut.reshape(MPW, devices, owned).transpose(1, 0, 2)
    fetched, source_cut, source_total, place_all = lax.optimization_barrier(
        (fetched, source_cut, source_total, place_all)
    )
    if ffn_width == lanes:
        ffn_low = unpack_ffn(ffn_all, wide_count)
    else:
        ffn_low = ffn_all.reshape(devices // 2, 2, 2 * L, D, ffn_width)
        ffn_low = ffn_low.transpose(2, 3, 1, 0, 4).reshape(2 * L, D, FF)
    source_here = swap_all(source_cut)
    token_rows = select_rows(now, fetched)

    def more_rows(state):
        round_idx, rows = state
        addresses = address(round_idx)
        return (round_idx + 1, rows + select_rows(addresses, fetch(ask_again(addresses))))

    _, token_rows = lax.while_loop(
        lambda state: state[0] < rounds, more_rows, (jnp.int32(1), token_rows)
    )

    is_valid = (order[None, :] < live_lengths[:, None]) & (key_keep == 1)
    same_bucket = buckets.reshape(WINDOW, 1) == buckets.reshape(1, WINDOW)
    allowed = same_bucket & is_valid.reshape(1, WINDOW) | jnp.eye(WINDOW, dtype=bool)
    allowed = allowed.astype(jnp.float32)
    embedded = (token_rows + place_all.astype(jnp.float32)).reshape(win_count, WINDOW, D)
    hidden, embed_pull = jax.vjp(layer_norm, embedded, vectors[0], vectors[1])
    params = (
        attn_low[0],
        attn_low[1],
        attn_low[2],
        attn_low[3],
        ffn_low[0],
        ffn_low[1],
        up_biases[0],
        vectors[2:10],
    )
    hidden, stored, shared = layer_forward(hidden, params, allowed)
    picks = mask_pos.reshape(-1)
    head_in = select_rows(picks, hidden.reshape(WINDOW, D).astype(jnp.bfloat16))
    head_in = head_in.astype(jnp.bfloat16)
    head_pre = jnp.dot(head_in, head_weight, preferred_element_type=jnp.float32) + vectors[NV - 3]
    head_out, head_pull = jax.vjp(head_tail, head_pre, vectors[NV - 2], vectors[NV - 1])
    head_low = head_out.astype(jnp.bfloat16)

    rows_all = devices * MPW
    side = lax.axis_index("side").astype(jnp.int32)
    here = here16().astype(jnp.int32)
    order_rows = jnp.arange(devices, dtype=jnp.int32)
    rank_of_dev = (order_rows % 2 ^ side) * group + (order_rows // 2 ^ here)
    dev_of_rank = (order_rows % group ^ here) * 2 + (order_rows // group ^ side)
    head_all = gather_relative(head_low, wide_count, 1, lanes)
    head_all, *shared = lax.optimization_barrier((head_all, *shared))
    head_all = jnp.concatenate([head_all, exchange(head_all, side_bit)]).reshape(rows_all, D)
    labels_all = pick_rows(labels_all.reshape(devices, MPW), dev_of_rank).reshape(rows_all, 1)
    is_live = jnp.arange(MPW, dtype=jnp.int32)[None, :] < pick_rows(counts_all[:, None], dev_of_rank)
    word_ids = device * owned + jnp.arange(owned, dtype=jnp.int32)
    is_word = (word_ids < V)[None, :]
    logits = jnp.einsum("rd,vd->rv", head_all, table_low, preferred_element_type=jnp.float32)
    logits = jnp.where(is_word, logits + dec_bias[None, :], masked_fill)
    top_here = jnp.max(logits, axis=1)
    sum_here = jnp.sum(jnp.exp(logits - top_here[:, None]), axis=1)
    stats = jnp.concatenate(
        [
            top_here.reshape(devices, MPW),
            sum_here.reshape(devices, MPW),
            jnp.zeros((devices, 2 * lanes - 2 * MPW), jnp.float32),
        ],
        axis=1,
    )
    stats, source_here = lax.optimization_barrier((stats, source_here))
    stats = swap_all(pick_rows(stats, rank_of_dev))
    tops = stats[:, :MPW]
    top = jnp.max(tops, axis=0)
    total = top + jnp.log(jnp.sum(stats[:, MPW : 2 * MPW] * jnp.exp(tops - top[None]), axis=0))
    totals = spread(jnp.concatenate([total, source_total]), devices)
    totals = pick_rows(totals, dev_of_rank)
    row_facts = jnp.concatenate(
        [
            totals[:, :MPW].reshape(rows_all, 1),
            totals[:, MPW:].reshape(rows_all, 1),
            is_live.reshape(rows_all, 1).astype(jnp.float32),
            labels_all.astype(jnp.float32),
        ],
        axis=1,
    )
    place_facts = jnp.stack([device * owned, here, side]).astype(jnp.int32)
    grad_logits, losses, grad_dec = logit_grads(
        place_facts, logits, source_here, row_facts, devices
    )
    loss_part = jnp.sum(losses)
    give = jnp.dot(grad_logits[rows_all // 2 :], table_low, preferred_element_type=jnp.float32)
    got = exchange(give, side_bit)
    keep = jnp.dot(grad_logits[: rows_all // 2], table_low, preferred_element_type=jnp.float32)
    grad_head_out = reduce_rows((keep + got).reshape(group, MPW, D), wide_count)
    grad_words = jnp.einsum("rv,rd->vd", grad_logits, head_all, preferred_element_type=jnp.float32)
    grad_head_out, grad_words = lax.optimization_barrier((grad_head_out, grad_words))

    grad_pre, grad_head_gain, grad_head_shift = head_pull(grad_head_out)
    pre_low = grad_pre.astype(jnp.bfloat16)
    grad_head_w = jnp.einsum("rd,rf->df", head_in, pre_low, preferred_element_type=jnp.float32)
    grad_head_in = jnp.einsum("rf,df->rd", pre_low, head_weight, preferred_element_type=jnp.float32)
    grad_hidden = add_rows(picks, grad_head_in, WINDOW).reshape(win_count, WINDOW, D)
    grad_hidden, layer_mats, up_grad, vec_grads = layer_backward(
        grad_hidden, stored, shared, params, allowed
    )
    grad_embed, grad_emb_gain, grad_emb_shift = embed_pull(grad_hidden)
    flat_embed = grad_embed.reshape(WINDOW, D)

    ffn_parts, attn_parts = layer_mats[1], layer_mats[0]
    flat_embed, ffn_parts = tied(flat_embed, ffn_parts)
    dec_block = jnp.zeros((devices * owned,), jnp.float32)
    dec_block = lax.dynamic_update_slice(dec_block, grad_dec, (device * owned,))[:V]
    vector_block = jnp.concatenate(
        [jnp.stack([grad_emb_gain, grad_emb_shift])]
        + [vec_grads]
        + [jnp.stack([jnp.sum(pre_low.astype(jnp.float32), 0), grad_head_gain, grad_head_shift])],
        axis=0,
    )
    front = jnp.concatenate(
        [
            dec_block.reshape(-1, lanes),
            up_grad.reshape(2, devices // 2, ffn_width).transpose(1, 0, 2).reshape(-1, lanes),
            vector_block.reshape(-1, lanes),
        ]
    )
    other_part = scatter_flat(front, grad_head_w.reshape(-1, lanes), size, devices)

    place_grad = flat_embed.reshape(group, per_place, D)
    sent = add_rows(now, flat_embed, devices * slots)
    arrived = swap_all(sent.reshape(devices, slots, D))
    place_parts = route_parts(place_grad.reshape(group, per_place, D), wide_count)
    steps = len(routes(wide_count)[0])

    def place_step(parts, turn):
        if turn < steps:
            parts = route_step(parts, wide_count, turn, False)
            if turn + 1 == steps:
                parts = gather_start(jnp.concatenate(parts, axis=-1), 1, lanes)
            return parts
        return gather_step(parts, wide_count, turn - steps)

    for step in range(steps):
        if step + 3 < steps:
            ffn_parts = reduce_step(ffn_parts, wide_count, step + 3)
        attn_parts = reduce_step(attn_parts, wide_count, step)
        other_part = other_step(other_part, wide_count, step)
        (place_parts,) = lockstep(place_step(place_parts, 2 * step))
        place_parts, attn_parts, ffn_parts, (other_part,) = lockstep(
            place_step(place_parts, 2 * step + 1), attn_parts, ffn_parts, [other_part]
        )
    ffn_grad = jnp.concatenate(ffn_parts, axis=1)
    attn_grad = jnp.concatenate(attn_parts, axis=1)
    other_grad = own_share(other_part, size, device)
    place_grad = gather_end(place_parts, wide_count, 1)
    place_grad = jnp.concatenate([place_grad, exchange(place_grad, side_bit)])
    turn = jnp.arange(devices, dtype=jnp.int32)[:, None]
    place_ids = (turn // group ^ side) * WINDOW + (turn % group ^ here) * per_place
    place_ids = place_ids + jnp.arange(per_place, dtype=jnp.int32)[None, :]
    place_ids = (V - device * owned + place_ids).reshape(-1)
    table_grad = grad_words + add_rows(asked, arrived.reshape(-1, D), owned)
    table_grad = table_grad + add_rows(place_ids, place_grad.reshape(SEQ, D), owned)

    def more_grads(state):
        round_idx, grads = state
        addresses = address(round_idx)
        asked_rows = ask_again(addresses)
        sent = add_rows(addresses, flat_embed, devices * slots)
        arrived = swap_all(sent.reshape(devices, slots, D)).reshape(-1, D)
        return (round_idx + 1, grads + add_rows(asked_rows, arrived, owned))

    _, table_grad = lax.while_loop(
        lambda state: state[0] < rounds, more_grads, (jnp.int32(1), table_grad)
    )

    squares = square_sum((table_grad, attn_grad, ffn_grad, other_grad))
    sums = jnp.sum(spread(jnp.stack([squares, loss_part]), devices), axis=0)
    grad_norm = jnp.sqrt(sums[0]) / masked_total
    loss_value = sums[1] / masked_total
    factor = jnp.minimum(1.0, clip_limit / grad_norm)
    scaling = factor / masked_total

    attn_moment_new = mu_muon * attn_moment + attn_grad * scaling
    ffn_moment_new = mu_muon * ffn_moment + ffn_grad * scaling
    second = lax.axis_index("side") == 1
    keep = jnp.where(second, ffn_moment_new[1], ffn_moment_new[0])
    got = exchange(jnp.where(second, ffn_moment_new[0], ffn_moment_new[1]), side_bit)
    ffn_pair = jnp.concatenate([keep, got], axis=1)[None]
    attn_parts = gather_start(attn_moment_new[0].astype(jnp.bfloat16), 0, tile)
    ffn_parts = gather_start(ffn_pair[0].astype(jnp.bfloat16), 0, tile)
    steps = len(routes(wide_count)[0])
    for step in range(steps - 2):
        attn_parts, ffn_parts = lockstep(
            gather_step(attn_parts, wide_count, step, False),
            gather_step(ffn_parts, wide_count, step),
        )
    (attn_parts,) = lockstep(gather_step(attn_parts, wide_count, steps - 2, False))
    attn_gram = gram_of(gather_end(attn_parts, wide_count, 0, False))
    ffn_parts = gather_step(ffn_parts, wide_count, steps - 2)
    attn_gram, ffn_parts = tied(attn_gram, ffn_parts)
    ffn_found = gather_end(gather_step(ffn_parts, wide_count, steps - 1), wide_count, 0)
    attn_new = muon_cols(attn_mats, attn_moment_new, attn_gram, D)
    ffn_turn = newton_cols(ffn_pair, gram_of(ffn_found))[0]
    keep, give = ffn_turn[:, :ffn_width], ffn_turn[:, ffn_width:]
    got = exchange(give, side_bit)
    ffn_turn = jnp.stack([jnp.where(second, got, keep), jnp.where(second, keep, got)])
    ffn_new = ffn_mats - lr_muon * muon_shape * math.sqrt(max(D, FF)) * ffn_turn
    embed_new, embed_first_new, embed_second_new = adam_step(
        embed_table, embed_first, embed_second, table_grad * scaling
    )
    other_new, other_first_new, other_second_new = adam_step(
        other_params, other_first, other_second, other_grad * scaling
    )
    return (
        loss_value,
        grad_norm,
        embed_new,
        embed_first_new,
        embed_second_new,
        attn_new,
        attn_moment_new,
        ffn_new,
        ffn_moment_new,
        other_new,
        other_first_new,
        other_second_new,
    )


def solution(mesh):
    wide_count, narrow_count = mesh.shape["wide"], mesh.shape["narrow"]
    assert narrow_count % 2 == 0
    split = Mesh(
        np.asarray(mesh.devices).reshape(wide_count, narrow_count // 2, 2), everyone
    )
    rows, narrow = P(everyone), ("pair", "side")
    attn_spec, ffn_spec = P(narrow, None, "wide"), P(None, None, everyone)
    in_specs = (rows,) * 11 + (attn_spec,) * 2 + (ffn_spec,) * 2 + (rows,) * 3
    out_specs = (P(), P()) + (rows,) * 3 + (attn_spec,) * 2 + (ffn_spec,) * 2 + (rows,) * 3

    return jax.shard_map(
        shards, mesh=split, in_specs=in_specs, out_specs=out_specs, check_vma=False
    )
```

```python
import functools
import math

import jax
import jax.numpy as jnp
import numpy as np
from jax import lax
from jax.experimental import pallas as pl
from jax.experimental.pallas import tpu as pltpu
from jax.sharding import Mesh
from jax.sharding import PartitionSpec as P

D = 1024
FF = 4096
HEADS = 16
L = 1
V = 30720
SEQ = 1024
WINDOW = 512
NS_ITERS = 3
ADAM_STEP = 5
MPW = 80
NV = 13


high = lax.Precision.HIGH
lanes = 128
tile = 16
slots = 32
ln_eps = 1e-05
masked_fill = -1e30
clip_limit = 0.3
ns_a = 3.4445
ns_b = -4.775
ns_c = 2.0315
mu_muon = 0.95
lr_muon = 0.1
muon_shape = 0.2
lr_adam = 0.01
beta_one = 0.9
beta_two = 0.999
adam_eps = 1e-08


def layer_norm(inputs, gain_vec, shift_vec):
    center = inputs - jnp.mean(inputs, -1, keepdims=True)
    spread = jnp.mean(center * center, -1, keepdims=True)
    return center * lax.rsqrt(spread + ln_eps) * gain_vec + shift_vec


def exact_gelu(inputs):
    return jax.nn.gelu(inputs, approximate=False)


def head_tail(head_pre, gain_vec, shift_vec):
    return layer_norm(exact_gelu(head_pre), gain_vec, shift_vec)


def project(inputs, weight):
    return jnp.einsum("bsd,df->bsf", inputs, weight, preferred_element_type=jnp.float32)


def project_back(gradients, weight):
    return jnp.einsum("bsf,df->bsd", gradients, weight, preferred_element_type=jnp.float32)


def col_sum(inputs):
    return jnp.sum(inputs.astype(jnp.float32), axis=(0, 1))


def share(values, axis):
    return jnp.concatenate([values, exchange(values, side_bit)], axis=axis)


def swap_pick(for_first, for_second, axis):
    first = lax.axis_index("side") == 0
    keep = jnp.where(first, for_first, for_second)
    got = exchange(jnp.where(first, for_second, for_first), side_bit)
    return jnp.concatenate([keep, got], axis=axis)


def share_half(values):
    side = lax.axis_index("side")
    half = values.shape[1] // 2
    keep = lax.dynamic_slice_in_dim(values, side * half, half, axis=1)
    got = exchange(lax.dynamic_slice_in_dim(values, (1 - side) * half, half, axis=1), side_bit)
    return jnp.concatenate([keep, got])


def head_scores(q_ref, k_ref, allow_ref, cols):
    scores = lax.dot_general(
        q_ref[:, cols], k_ref[:, cols], (((1,), (1,)), ((), ())), preferred_element_type=jnp.float32
    )
    return jnp.where(allow_ref[...] > 0.0, scores * (D // HEADS) ** (-0.5), masked_fill)


def attend_kernel(q_ref, k_ref, v_ref, allow_ref, out_ref, total_ref):
    width = D // HEADS
    for head in range(q_ref.shape[1] // width):
        cols = slice(head * width, (head + 1) * width)
        scores = head_scores(q_ref, k_ref, allow_ref, cols)
        top = jnp.max(scores, axis=1, keepdims=True)
        total = top + jnp.log(jnp.sum(jnp.exp(scores - top), axis=1, keepdims=True))
        probs = jnp.exp(scores - total).astype(jnp.bfloat16)
        found = jnp.dot(probs, v_ref[:, cols], preferred_element_type=jnp.float32)
        out_ref[:, cols] = found.astype(jnp.bfloat16)
        total_ref[head] = total


def attend_back_kernel(
    q_ref, k_ref, v_ref, allow_ref, total_ref, grad_ref, q_out, k_out, v_out
):
    width = D // HEADS
    rows = (((0,), (0,)), ((), ()))
    for head in range(q_ref.shape[1] // width):
        cols = slice(head * width, (head + 1) * width)
        grads = grad_ref[:, cols]
        probs = jnp.exp(head_scores(q_ref, k_ref, allow_ref, cols) - total_ref[head])
        grad_probs = lax.dot_general(
            grads, v_ref[:, cols], (((1,), (1,)), ((), ())), preferred_element_type=jnp.float32
        )
        grad_value = lax.dot_general(
            probs.astype(jnp.bfloat16), grads, rows, preferred_element_type=jnp.float32
        )
        inner = jnp.sum(grad_probs * probs, axis=1, keepdims=True)
        raw = (probs * (grad_probs - inner) * width ** (-0.5)).astype(jnp.bfloat16)
        grad_query = jnp.dot(raw, k_ref[:, cols], preferred_element_type=jnp.float32)
        grad_key = lax.dot_general(
            raw, q_ref[:, cols], rows, preferred_element_type=jnp.float32
        )
        q_out[:, cols] = grad_query.astype(jnp.bfloat16)
        k_out[:, cols] = grad_key.astype(jnp.bfloat16)
        v_out[:, cols] = grad_value.astype(jnp.bfloat16)


def attend(queries, key_proj, values, allow):
    pair = lanes * HEADS // D
    cols = pl.BlockSpec((WINDOW, lanes), lambda step: (0, step))
    whole = pl.BlockSpec((WINDOW, WINDOW), lambda step: (0, 0))
    return pl.pallas_call(
        attend_kernel,
        grid=(D // lanes,),
        in_specs=[cols, cols, cols, whole],
        out_specs=[cols, pl.BlockSpec((pair, WINDOW, 1), lambda step: (step, 0, 0))],
        out_shape=[
            jax.ShapeDtypeStruct((WINDOW, D), jnp.bfloat16),
            jax.ShapeDtypeStruct((HEADS, WINDOW, 1), jnp.float32),
        ],
    )(queries, key_proj, values, allow)


def attend_back(queries, key_proj, values, allow, totals, grads):
    pair = lanes * HEADS // D
    cols = pl.BlockSpec((WINDOW, lanes), lambda step: (0, step))
    whole = pl.BlockSpec((WINDOW, WINDOW), lambda step: (0, 0))
    total = pl.BlockSpec((pair, WINDOW, 1), lambda step: (step, 0, 0))
    return pl.pallas_call(
        attend_back_kernel,
        grid=(D // lanes,),
        in_specs=[cols, cols, cols, whole, total, cols],
        out_specs=[cols] * 3,
        out_shape=[jax.ShapeDtypeStruct((WINDOW, D), jnp.bfloat16)] * 3,
    )(queries, key_proj, values, allow, totals, grads)


def layer_forward(hidden, params, allowed):
    w_query, w_key, w_value, w_out, w_up, w_down, up_bias, vectors = params
    inputs = hidden.astype(jnp.bfloat16)
    queries = (project(inputs, w_query) + vectors[4]).astype(jnp.bfloat16)
    key_proj = project(inputs, w_key).astype(jnp.bfloat16)
    values = (project(inputs, w_value) + vectors[5]).astype(jnp.bfloat16)
    context, log_total = attend(queries[0], key_proj[0], values[0], allowed)
    context = context[None]
    attn_sum = hidden + (project(context, w_out) + vectors[6])
    middle, first_pull = jax.vjp(layer_norm, attn_sum, vectors[0], vectors[1])
    middle_low = middle.astype(jnp.bfloat16)
    up_proj = project(middle_low, w_up) + up_bias
    activated, gelu_pull = jax.vjp(exact_gelu, up_proj)
    act_low = activated.astype(jnp.bfloat16)
    ffn_sum = middle + (project_back(act_low, w_down) + vectors[7])
    output, second_pull = jax.vjp(layer_norm, ffn_sum, vectors[2], vectors[3])
    stored = (
        inputs,
        queries,
        key_proj,
        values,
        log_total,
        context,
        first_pull,
        middle_low,
        gelu_pull,
        act_low,
        second_pull,
    )
    shared = (
        share(middle_low[0].T, 1),
        share_half(act_low[0]),
        share(inputs[0].T, 1),
        swap_pick(inputs[0].T, context[0].T, 1),
    )
    return (output, stored, shared)


def layer_backward(grad_out, stored, shared, params, allowed):
    w_query, w_key, w_value, w_out, w_up, w_down, _, _ = params
    (_, queries, key_proj, values, log_total, _, first_pull, _, gelu_pull, _, second_pull) = stored
    grad_ffn, grad_gain_two, grad_shift_two = second_pull(grad_out)
    down_low = grad_ffn.astype(jnp.bfloat16)
    (grad_up,) = gelu_pull(project(down_low, w_down))
    up_low = grad_up.astype(jnp.bfloat16)
    wide_count = lax.axis_size("wide")
    operands = (
        shared[0],
        share(down_low[0].T, 1),
        share_half(up_low[0]),
        shared[1],
    )
    if FF // (4 * wide_count) == lanes:
        grad_mats_ffn = ffn_weight_grads(*operands, wide_count)
    else:
        blocks = jnp.stack([jnp.dot(*operands[::2], preferred_element_type=jnp.float32),
                            jnp.dot(*operands[1::2], preferred_element_type=jnp.float32)])
        blocks = blocks.reshape(2, D, wide_count, 2, -1).transpose(2, 3, 0, 1, 4)
        grad_mats_ffn = in_routes(blocks, wide_count)
    grad_ffn, parts = tied(grad_ffn, grad_mats_ffn)
    parts = reduce_step(parts, wide_count, 0)
    grad_middle = grad_ffn + project_back(up_low, w_up)
    grad_attn, grad_gain_one, grad_shift_one = first_pull(grad_middle)
    attn_low = grad_attn.astype(jnp.bfloat16)
    grad_context = project_back(attn_low, w_out).astype(jnp.bfloat16)
    grads = attend_back(queries[0], key_proj[0], values[0], allowed, log_total, grad_context[0])
    grad_query, grad_key, grad_value = (found[None] for found in grads)
    grad_query, parts = tied(grad_query, parts)
    parts = reduce_step(parts, wide_count, 1)
    operands = (
        shared[2],
        shared[3],
        swap_pick(grad_query[0], grad_key[0], 0),
        swap_pick(grad_value[0], attn_low[0], 0),
    )
    if D // wide_count == lanes:
        attn_parts = attn_weight_grads(*operands, wide_count)
    else:
        blocks = jnp.stack([jnp.dot(*operands[::2], preferred_element_type=jnp.float32),
                            jnp.dot(*operands[1::2], preferred_element_type=jnp.float32)])
        blocks = blocks.reshape(2, 1, D, wide_count, -1).transpose(3, 0, 1, 2, 4)
        attn_parts = in_routes(blocks, wide_count)
    grad_hidden = (
        grad_attn
        + project_back(grad_query, w_query)
        + project_back(grad_key, w_key)
        + project_back(grad_value, w_value)
    )
    grad_hidden, parts = tied(grad_hidden, parts)
    parts = reduce_step(parts, wide_count, 2)
    matrices = (attn_parts, parts)
    vector_grads = jnp.stack(
        [
            grad_gain_one,
            grad_shift_one,
            grad_gain_two,
            grad_shift_two,
            col_sum(grad_query),
            col_sum(grad_value),
            col_sum(attn_low),
            col_sum(down_low),
        ]
    )
    return (grad_hidden, matrices, col_sum(up_low), vector_grads)


def slab_product(matrix, columns):
    return jnp.einsum(
        "kde,kec->kdc", matrix, columns, precision=high, preferred_element_type=jnp.float32
    )


def newton_cols(moment, gram):
    norms = jnp.sqrt(jnp.trace(gram, axis1=1, axis2=2))
    scaling = 1.0 / (norms + 1e-07)
    current = moment * scaling[:, None, None]
    gram = gram * (scaling * scaling)[:, None, None]
    for step_idx in range(NS_ITERS):
        if step_idx + 1 < NS_ITERS:
            poly = ns_b * gram + ns_c * jnp.einsum("kde,kef->kdf", gram, gram)
            current = ns_a * current + slab_product(poly, current)
            half = ns_a * gram + jnp.einsum("kde,kef->kdf", poly, gram)
            gram = ns_a * half + jnp.einsum("kde,kef->kdf", half, poly)
        else:
            once = slab_product(gram, current)
            current = ns_a * current + ns_b * once + ns_c * slab_product(gram, once)
    return current


def gram_of(found):
    return jnp.einsum("wdc,wec->de", found, found, preferred_element_type=jnp.float32)[None]


def relative_order(part, taken):
    names = [bit for bit in wide_bits(lax.axis_size("wide"))[::-1] + [("pair", 1)] if bit in taken]
    dims = [names.index(bit) for bit in taken[::-1]]
    split = part.reshape((2,) * len(taken) + part.shape[1:])
    turn = [dims.index(place) for place in range(len(taken))]
    split = split.transpose(turn + list(range(len(taken), split.ndim)))
    return split.reshape(part.shape)


def muon_cols(master, new_moment, gram, long_side):
    change = lr_muon * muon_shape * math.sqrt(long_side) * newton_cols(new_moment, gram)
    return master - change


def adam_step(master, first_moment, second, gradient):
    new_first = beta_one * first_moment + (1.0 - beta_one) * gradient
    new_second = beta_two * second + (1.0 - beta_two) * gradient * gradient
    first_hat = new_first / (1.0 - beta_one**ADAM_STEP)
    second_hat = new_second / (1.0 - beta_two**ADAM_STEP)
    return (master - lr_adam * first_hat / (jnp.sqrt(second_hat) + adam_eps), new_first, new_second)


def square_sum(arrays):
    running = jnp.zeros((), jnp.float32)
    for member in arrays:
        running = running + jnp.sum(member * member)
    return running


everyone = ("wide", "pair", "side")
side_bit = ("side", 1)


def swap_all(blocks, axes=everyone):
    return lax.all_to_all(blocks, axes, 0, 0, tiled=True)


def spread(values, devices):
    size = values.shape[0]
    row = jnp.pad(values, (0, -size % lanes))
    return swap_all(jnp.broadcast_to(row[None], (devices, row.shape[0])))[:, :size]


def wide_bits(wide_count):
    return [("wide", 1 << k) for k in range(wide_count.bit_length() - 1)]


def routes(wide_count, with_pair=True):
    bits = wide_bits(wide_count)
    near, far, across = bits[:1], bits[1:], [("pair", 1)] if with_pair else []
    last = far[1:]
    return [across + near + far, near + far[:1] + across + last, far[:1] + across + near + last]


def my_bit(bit):
    axis, mask = bit
    return lax.axis_index(axis) // mask % 2


def exchange(values, bit):
    axis, mask = bit
    steps = [(here, here ^ mask) for here in range(lax.axis_size(axis))]
    return lax.ppermute(values, axis, steps)


def halve(values, bit, dim):
    mine = lax.dynamic_index_in_dim(values, my_bit(bit), dim, keepdims=False)
    theirs = lax.dynamic_index_in_dim(values, 1 - my_bit(bit), dim, keepdims=False)
    return mine + exchange(theirs, bit)


def double(values, bit, dim):
    theirs = exchange(values, bit)
    first = my_bit(bit) == 0
    pair = [jnp.where(first, values, theirs), jnp.where(first, theirs, values)]
    return jnp.stack(pair, axis=dim)


def cuts(length, unit):
    whole = length // unit
    sizes = [(whole + 2) // 3 * unit, (whole + 1) // 3 * unit]
    sizes.append(length - sum(sizes))
    starts = [0, sizes[0], sizes[0] + sizes[1]]
    return [(start, start + size) for start, size in zip(starts, sizes) if size]


def here16():
    return lax.axis_index("wide") * 2 + lax.axis_index("pair")


def lockstep(*groups):
    flat = lax.optimization_barrier(sum((list(group) for group in groups), []))
    found = []
    for group in groups:
        found.append(flat[: len(group)])
        flat = flat[len(group) :]
    return found


def reduce_step(parts, wide_count, step):
    return [
        part[0] + exchange(part[1], route[step])
        for part, route in zip(parts, routes(wide_count))
    ]


def tied(value, parts):
    value, *parts = lax.optimization_barrier((value, *parts))
    return value, parts


def static_step(part, left, bit):
    dim = left.index(bit)
    keep = lax.index_in_dim(part, 0, dim, keepdims=False)
    return keep + exchange(lax.index_in_dim(part, 1, dim, keepdims=False), bit)


def route_parts(values, wide_count):
    bits = wide_bits(wide_count)[::-1] + [("pair", 1)]
    return [
        values[..., start:stop].reshape((2,) * len(bits) + (values.shape[1], stop - start))
        for start, stop in cuts(values.shape[-1], lanes)
    ]


def route_step(parts, wide_count, step, static):
    bits = wide_bits(wide_count)[::-1] + [("pair", 1)]
    found = []
    for part, route in zip(parts, routes(wide_count)):
        left = [bit for bit in bits if bit not in route[:step]]
        if static:
            found.append(static_step(part, left, route[step]))
        else:
            found.append(halve(part, route[step], left.index(route[step])))
    return found


def reduce_rows(values, wide_count):
    parts = route_parts(values, wide_count)
    for step in range(len(routes(wide_count)[0])):
        (parts,) = lockstep(route_step(parts, wide_count, step, True))
    return jnp.concatenate(parts, axis=-1)


def gather_start(block, axis, unit):
    return [
        lax.slice_in_dim(block, start, stop, axis=axis)[None]
        for start, stop in cuts(block.shape[axis], unit)
    ]


def gather_step(parts, wide_count, step, with_pair=True):
    return [
        jnp.concatenate([part, exchange(part, route[::-1][step])])
        for part, route in zip(parts, routes(wide_count, with_pair))
    ]


def gather_end(parts, wide_count, axis, with_pair=True):
    ordered = [
        relative_order(part, route[::-1])
        for part, route in zip(parts, routes(wide_count, with_pair))
    ]
    return jnp.concatenate(ordered, axis=1 + axis)


def gather_relative(block, wide_count, axis, unit):
    parts = gather_start(block, axis, unit)
    for step in range(len(routes(wide_count)[0])):
        (parts,) = lockstep(gather_step(parts, wide_count, step))
    return gather_end(parts, wide_count, axis)


def route_shape(route, covered):
    wide = [bit for bit in route if bit not in covered]
    shape = tuple(2 if bit in covered else 1 for bit in route)

    def index(step):
        low = 1 << len(covered) - 1
        return tuple(
            0 if bit in covered else step * low // bit[1] % 2 for bit in route
        )

    assert wide
    return shape, index


def weight_grads(kernel, operands, column_specs, covered, steps, members, wide_count):
    here = jnp.stack([lax.axis_index("wide"), lax.axis_index("pair")]).astype(jnp.int32)
    shapes, specs = [], []
    for route, (start, stop) in zip(routes(wide_count), cuts(D, tile)):
        block, index = route_shape(route, covered)
        tail = (members, stop - start, lanes)
        shapes.append(jax.ShapeDtypeStruct((2,) * len(route) + tail, jnp.float32))
        specs.append(
            pl.BlockSpec(block + tail, lambda step, _, index=index: index(step) + (0, 0, 0))
        )
    return pl.pallas_call(
        kernel,
        grid_spec=pltpu.PrefetchScalarGridSpec(
            num_scalar_prefetch=1, grid=(steps,), in_specs=column_specs, out_specs=specs
        ),
        out_shape=shapes,
    )(here, *operands)


def put(refs, wide_count, covered, where, member, values):
    for ref, route, (start, stop) in zip(refs, routes(wide_count), cuts(D, tile)):
        place = tuple(where[bit] if bit in covered else 0 for bit in route)
        ref[place + (member,)] = values[start:stop]


def ffn_grads_kernel(here, up_rows, down_rows, up_cols, down_cols, *refs, wide_count):
    flip = here[1] == 0
    pair = ("pair", 1)
    for member, (rows, cols) in enumerate(((up_rows, up_cols), (down_rows, down_cols))):
        both = jnp.dot(rows[...], cols[...], preferred_element_type=jnp.float32)
        low, top = both[:, :lanes], both[:, lanes:]
        put(refs, wide_count, [pair], {pair: 0}, member, jnp.where(flip, low, top))
        put(refs, wide_count, [pair], {pair: 1}, member, jnp.where(flip, top, low))


def ffn_weight_grads(up_rows, down_rows, up_cols, down_cols, wide_count):
    whole = pl.BlockSpec(up_rows.shape, lambda step, here: (0, 0))
    cols = pl.BlockSpec((up_cols.shape[0], 2 * lanes), lambda step, here: (0, step ^ here[0]))
    kernel = functools.partial(ffn_grads_kernel, wide_count=wide_count)
    operands = (up_rows, down_rows, up_cols, down_cols)
    specs = [whole, whole, cols, cols]
    return weight_grads(kernel, operands, specs, [("pair", 1)], wide_count, 2, wide_count)


def attn_grads_kernel(here, one_rows, two_rows, one_cols, two_cols, *refs, wide_count):
    swap = here[0] % 2 == 0
    flip = here[1] == 0
    pair, near = ("pair", 1), ("wide", 1)
    blocks = []
    for rows, cols in ((one_rows, one_cols), (two_rows, two_cols)):
        both = jnp.dot(rows[...], cols[...], preferred_element_type=jnp.float32)
        low, top = both[:, :lanes], both[:, lanes:]
        blocks.append((jnp.where(swap, low, top), jnp.where(swap, top, low)))
    for step in range(2):
        one, two = blocks[0][step], blocks[1][step]
        first, second = jnp.where(flip, one, two), jnp.where(flip, two, one)
        put(refs, wide_count, [pair, near], {pair: 0, near: step}, 0, first)
        put(refs, wide_count, [pair, near], {pair: 1, near: step}, 0, second)


def attn_weight_grads(one_rows, two_rows, one_cols, two_cols, wide_count):
    whole = pl.BlockSpec(one_rows.shape, lambda step, here: (0, 0))
    cols = pl.BlockSpec((one_cols.shape[0], 2 * lanes), lambda step, here: (0, step ^ here[0] // 2))
    kernel = functools.partial(attn_grads_kernel, wide_count=wide_count)
    operands = (one_rows, two_rows, one_cols, two_cols)
    specs = [whole, whole, cols, cols]
    covered = [("pair", 1), ("wide", 1)]
    return weight_grads(kernel, operands, specs, covered, wide_count // 2, 1, wide_count)


def in_routes(blocks, wide_count):
    count = wide_count * 2
    order = jnp.arange(count) ^ here16()
    blocks = jnp.take(blocks.reshape((count,) + blocks.shape[2:]), order, axis=0)
    bits = wide_bits(wide_count)[::-1] + [("pair", 1)]
    parts = []
    for route, (start, stop) in zip(routes(wide_count), cuts(D, tile)):
        part = blocks[:, :, start:stop].reshape((2,) * len(bits) + blocks[:, :, start:stop].shape[1:])
        dims = [bits.index(bit) for bit in route]
        parts.append(part.transpose(dims + list(range(len(bits), part.ndim))))
    return parts


def gather_blocks(block, wide_count, axis, unit):
    bits = wide_bits(wide_count)[::-1] + [("pair", 1)]
    parts = []
    for route, (start, stop) in zip(routes(wide_count), cuts(block.shape[axis], unit)):
        part = lax.slice_in_dim(block, start, stop, axis=axis)
        have = []
        for bit in route[::-1]:
            have = sorted(have + [bit], key=bits.index)
            part = double(part, bit, have.index(bit))
        parts.append(part.reshape((wide_count, 2) + part.shape[len(bits) :]))
    return jnp.concatenate(parts, axis=2 + axis)


def select_rows(index, rows, precision=None):
    hits = index[:, None] == jnp.arange(rows.shape[0], dtype=jnp.int32)[None, :]
    return jnp.dot(
        hits.astype(rows.dtype), rows, precision=precision, preferred_element_type=jnp.float32
    )


def logit_grads_kernel(facts, logits_ref, source_ref, rows_ref, grad_ref, loss_ref, dec_ref):
    step = pl.program_id(0)

    @pl.when(step == 0)
    def _():
        loss_ref[...] = jnp.zeros_like(loss_ref)
        dec_ref[...] = jnp.zeros_like(dec_ref)

    columns = lax.broadcasted_iota(jnp.int32, logits_ref.shape, 1) + facts[0]
    is_word = columns < V
    rows = rows_ref[...]
    log_prob = logits_ref[...] - rows[:, 0:1]
    source_log = source_ref[0].astype(jnp.float32) - rows[:, 1:2]
    source_prob = jnp.where(is_word, jnp.exp(source_log), 0.0)
    hits = columns == rows[:, 3:4].astype(jnp.int32)
    keep = is_word & (rows[:, 2:3] > 0.5)
    losses = source_prob * (source_log - log_prob) - jnp.where(hits, log_prob, 0.0)
    loss_ref[...] += jnp.sum(jnp.where(keep, losses, 0.0), axis=0, keepdims=True)
    grads = 2.0 * jnp.exp(log_prob) - jnp.where(hits, 1.0, 0.0) - source_prob
    grads = jnp.where(keep, grads, 0.0).astype(jnp.bfloat16)
    grad_ref[...] = grads
    dec_ref[...] += jnp.sum(grads.astype(jnp.float32), axis=0, keepdims=True)


def logit_grads(facts, logits, source, row_facts, devices):
    owned = logits.shape[1]
    group = devices // 2

    def source_block(step, facts):
        return ((step % group ^ facts[1]) * 2 + (step // group ^ facts[2]), 0, 0)

    line = pl.BlockSpec((1, owned), lambda step, facts: (0, 0))
    grads, losses, dec = pl.pallas_call(
        logit_grads_kernel,
        grid_spec=pltpu.PrefetchScalarGridSpec(
            num_scalar_prefetch=1,
            grid=(devices,),
            in_specs=[
                pl.BlockSpec((MPW, owned), lambda step, facts: (step, 0)),
                pl.BlockSpec((1, MPW, owned), source_block),
                pl.BlockSpec((MPW, 4), lambda step, facts: (step, 0)),
            ],
            out_specs=[pl.BlockSpec((MPW, owned), lambda step, facts: (step, 0)), line, line],
        ),
        out_shape=[
            jax.ShapeDtypeStruct(logits.shape, jnp.bfloat16),
            jax.ShapeDtypeStruct((1, owned), jnp.float32),
            jax.ShapeDtypeStruct((1, owned), jnp.float32),
        ],
    )(facts, logits, source, row_facts)
    return grads, losses, dec[0]


def pick_rows(values, index):
    hits = index[:, None] == jnp.arange(values.shape[0], dtype=jnp.int32)[None, :]
    return jnp.sum(jnp.where(hits[:, :, None], values[None], 0), axis=1)


def add_rows(index, rows, count):
    hits = jnp.arange(count, dtype=jnp.int32)[:, None] == index[None, :]
    return jnp.dot(
        hits.astype(rows.dtype), rows, precision=high, preferred_element_type=jnp.float32
    )


def flat_blocks(size, devices):
    total = size * devices
    starts = [dev * size // (tile * lanes) * tile for dev in range(devices)] + [total // lanes]
    ends = [-(-(dev + 1) * size // (tile * lanes)) * tile for dev in range(devices)]
    rows = max(end - start for start, end in zip(starts, ends))
    return starts, rows


def place_flat(share, device, devices):
    size = share.shape[0]
    _, rows = flat_blocks(size, devices)
    offset = device * size % (tile * lanes)
    block = lax.dynamic_update_slice(jnp.zeros((rows * lanes,), share.dtype), share, (offset,))
    return block.reshape(rows, lanes)


def join_kernel(blocks_ref, out_ref, *, starts):
    rows = blocks_ref.shape[1]
    for dev in range(len(starts) - 1):
        length = starts[dev + 1] - starts[dev]
        out_ref[starts[dev] : starts[dev + 1]] = blocks_ref[dev, :length]
    for dev in range(1, len(starts) - 1):
        length = starts[dev] - starts[dev - 1]
        if length < rows:
            shared = slice(starts[dev], starts[dev] + tile)
            both = blocks_ref[dev, :tile].astype(jnp.float32)
            both += blocks_ref[dev - 1, length : length + tile].astype(jnp.float32)
            out_ref[shared] = both.astype(out_ref.dtype)


def join_flat(blocks, size):
    starts, _ = flat_blocks(size, blocks.shape[0])
    starts[-1] += -starts[-1] % tile
    return pl.pallas_call(
        functools.partial(join_kernel, starts=starts),
        out_shape=jax.ShapeDtypeStruct((starts[-1], lanes), blocks.dtype),
    )(blocks)


def unpack_kernel(*refs):
    half = len(refs) * 2 // 3
    for place, out_ref in enumerate(refs[half:]):
        out_ref[:, :lanes] = refs[2 * place][...].reshape(D, lanes)
        out_ref[:, lanes:] = refs[2 * place + 1][...].reshape(D, lanes)


def unpack_attn(merged, wide_count, narrow_count):
    specs = [
        pl.BlockSpec((1, D, lanes), lambda step, add=step_add, kind=kind: (
            (2 * step + add) * narrow_count + kind, 0, 0
        ))
        for kind in range(narrow_count)
        for step_add in range(2)
    ]
    return pl.pallas_call(
        unpack_kernel,
        grid=(wide_count // 2,),
        in_specs=specs,
        out_specs=[pl.BlockSpec((D, 2 * lanes), lambda step: (0, step))] * narrow_count,
        out_shape=[jax.ShapeDtypeStruct((D, D), merged.dtype)] * narrow_count,
    )(*[merged] * len(specs))


def unpack_ffn(blocks, wide_count):
    specs = [
        pl.BlockSpec((1, 1, D, lanes), lambda step, kind=kind, pair=pair: (
            step % wide_count * 4 + pair * 2 + step // wide_count, kind, 0, 0
        ))
        for kind in range(2)
        for pair in range(2)
    ]
    return pl.pallas_call(
        unpack_kernel,
        grid=(2 * wide_count,),
        in_specs=specs,
        out_specs=[pl.BlockSpec((D, 2 * lanes), lambda step: (0, step))] * 2,
        out_shape=[jax.ShapeDtypeStruct((D, FF), blocks.dtype)] * 2,
    )(*[blocks] * 4)


def split_kernel(front_ref, rest_ref, out_ref, *, starts):
    front, rows = front_ref.shape[0], out_ref.shape[1]
    total = front + rest_ref.shape[0]
    for dev, start in enumerate(starts[:-1]):
        stop = min(start + rows, total)
        middle = min(max(start, front), stop)
        if start < middle:
            out_ref[dev, : middle - start] = front_ref[start:middle]
        if middle < stop:
            out_ref[dev, middle - start : stop - start] = rest_ref[middle - front : stop - front]
        if stop < start + rows:
            left = start + rows - stop
            out_ref[dev, rows - left :] = jnp.zeros((left, lanes), out_ref.dtype)


def scatter_flat(front, rest, size, devices):
    wide_count = lax.axis_size("wide")
    starts, rows = flat_blocks(size, devices)
    blocks = pl.pallas_call(
        functools.partial(split_kernel, starts=starts),
        out_shape=jax.ShapeDtypeStruct((devices, rows, lanes), front.dtype),
    )(front, rest)
    bits = wide_bits(wide_count)[::-1] + [("pair", 1), side_bit]
    part = blocks.reshape((2,) * len(bits) + blocks.shape[1:])
    return halve(part, side_bit, len(bits) - 1)


def other_step(part, wide_count, step):
    bits = wide_bits(wide_count)[::-1] + [("pair", 1)]
    route = routes(wide_count)[0]
    left = [bit for bit in bits if bit not in route[:step]]
    return halve(part, route[step], left.index(route[step]))


def own_share(part, size, device):
    return lax.dynamic_slice(part.reshape(-1), (device * size % (tile * lanes),), (size,))


def shards(
    token_ids,
    live_lengths,
    key_keep,
    buckets,
    mask_pos,
    mask_labels,
    mask_counts,
    source_logits,
    embed_table,
    embed_first,
    embed_second,
    attn_mats,
    attn_moment,
    ffn_mats,
    ffn_moment,
    other_params,
    other_first,
    other_second,
):
    wide_count = lax.axis_size("wide")
    narrow_count = lax.axis_size("pair") * 2
    devices = wide_count * narrow_count
    device = lax.axis_index(everyone).astype(jnp.int32)
    owned = embed_table.shape[0]
    size = other_params.shape[0]
    col_width = attn_mats.shape[2]
    ffn_width = ffn_mats.shape[2]
    kinds = attn_mats.shape[0]
    table_low = embed_table.astype(jnp.bfloat16)

    attn_own = attn_mats.astype(jnp.bfloat16)
    other_own = place_flat(other_params.astype(jnp.bfloat16), device, devices)
    if col_width == lanes:
        merged = jnp.concatenate([attn_own.reshape(-1, lanes), other_own])
        merged = lax.all_gather(merged, everyone)
        other_all = merged[:, kinds * D :]
        attn_low = unpack_attn(merged, wide_count, narrow_count)
    else:
        attn_all = lax.all_gather(attn_own, everyone)
        other_all = lax.all_gather(other_own, everyone)
        attn_all = attn_all.reshape(wide_count, narrow_count * kinds, D, col_width)
        attn_low = attn_all.transpose(1, 2, 0, 3).reshape(narrow_count * kinds, D, D)
    other_flat = join_flat(other_all, size)
    ffn_all = lax.all_gather(ffn_mats.astype(jnp.bfloat16), everyone)
    bias_rows = V // lanes
    up_rows = bias_rows + L * FF // lanes
    vec_rows = up_rows + NV * D // lanes
    dec_bias = lax.dynamic_slice(other_flat.reshape(-1), (device * owned,), (owned,))
    dec_bias = dec_bias.astype(jnp.float32)
    up_biases = other_flat[bias_rows:up_rows].reshape(devices // 2, 2, ffn_width)
    up_biases = up_biases.transpose(1, 0, 2).reshape(L, FF).astype(jnp.float32)
    vectors = other_flat[up_rows:vec_rows].reshape(NV, D).astype(jnp.float32)
    head_weight = other_flat[vec_rows : vec_rows + D * D // lanes].reshape(D, D)

    win_count = token_ids.shape[0]
    assert win_count == 1 and SEQ == 2 * WINDOW
    group = devices // 2
    per_place = WINDOW // group
    tokens = token_ids.reshape(-1)
    token_owner = tokens // owned
    token_local = tokens - token_owner * owned
    order = jnp.arange(WINDOW, dtype=jnp.int32)
    earlier = order[None, :] < order[:, None]
    same = tokens[:, None] == tokens[None, :]
    is_first = ~jnp.any(same & earlier, axis=1)
    same_owner = token_owner[:, None] == token_owner[None, :]
    rank = jnp.sum((same_owner & earlier & is_first[None, :]).astype(jnp.int32), axis=1)
    first_slot = jnp.where(is_first, rank, 0)
    slot = jnp.sum(jnp.where(same & is_first[None, :], first_slot[None, :], 0), axis=1)

    def address(round_idx):
        there = slot - round_idx * slots
        return jnp.where((there >= 0) & (there < slots), token_owner * slots + there, -1)

    def requests(addresses):
        cells = jnp.arange(devices * slots, dtype=jnp.int32)
        hits = (cells[:, None] == addresses[None, :]) & is_first[None, :]
        return jnp.sum(jnp.where(hits, token_local[None, :] + 1, 0), axis=1)

    now = address(0)
    labels_at = slots + 2
    message = jnp.concatenate(
        [
            requests(now).reshape(devices, slots),
            jnp.broadcast_to(jnp.max(slot)[None, None], (devices, 1)),
            jnp.broadcast_to(mask_counts.reshape(1, 1), (devices, 1)),
            jnp.broadcast_to(mask_labels.reshape(1, MPW), (devices, MPW)),
            jnp.zeros((devices, lanes - labels_at - MPW), jnp.int32),
        ],
        axis=1,
    )
    message = swap_all(message)
    rounds = jnp.max(message[:, slots]) // slots + 1
    counts_all = message[:, slots + 1]
    labels_all = message[:, labels_at : labels_at + MPW].reshape(-1)
    masked_total = jnp.sum(counts_all).astype(jnp.float32)
    asked = message[:, :slots].reshape(-1) - 1
    place_rows = V - device * owned + jnp.arange(SEQ, dtype=jnp.int32)
    place_rows = select_rows(place_rows, table_low).astype(jnp.bfloat16)
    place_rows = halve(place_rows.reshape(2, group, per_place, D), side_bit, 0)
    place_parts = route_parts(place_rows, wide_count)
    for step in range(len(routes(wide_count)[0])):
        place_parts = route_step(place_parts, wide_count, step, False)
        if step == 0:
            place_parts, (source_own,) = lockstep(
                place_parts, [source_logits.reshape(MPW, V)]
            )
        else:
            (place_parts,) = lockstep(place_parts)
    place_own = jnp.concatenate(place_parts, axis=-1)
    place_all = gather_blocks(place_own, wide_count, 1, lanes).reshape(WINDOW, D)

    def fetch(asked_rows):
        rows = select_rows(asked_rows, table_low).astype(jnp.bfloat16)
        return swap_all(rows.reshape(devices, slots, D)).reshape(-1, D)

    def ask_again(addresses):
        return swap_all(requests(addresses).reshape(devices, slots)).reshape(-1) - 1

    fetched = fetch(asked)
    source_max = jnp.max(source_own, axis=1).astype(jnp.float32)
    source_sum = jnp.sum(jnp.exp(source_own.astype(jnp.float32) - source_max[:, None]), axis=1)
    source_total = source_max + jnp.log(source_sum)
    source_cut = jnp.pad(source_own, ((0, 0), (0, devices * owned - V)))
    source_cut = source_cut.reshape(MPW, devices, owned).transpose(1, 0, 2)
    fetched, source_cut, source_total, place_all = lax.optimization_barrier(
        (fetched, source_cut, source_total, place_all)
    )
    if ffn_width == lanes:
        ffn_low = unpack_ffn(ffn_all, wide_count)
    else:
        ffn_low = ffn_all.reshape(devices // 2, 2, 2 * L, D, ffn_width)
        ffn_low = ffn_low.transpose(2, 3, 1, 0, 4).reshape(2 * L, D, FF)
    source_here = swap_all(source_cut)
    token_rows = select_rows(now, fetched)

    def more_rows(state):
        round_idx, rows = state
        addresses = address(round_idx)
        return (round_idx + 1, rows + select_rows(addresses, fetch(ask_again(addresses))))

    _, token_rows = lax.while_loop(
        lambda state: state[0] < rounds, more_rows, (jnp.int32(1), token_rows)
    )

    is_valid = (order[None, :] < live_lengths[:, None]) & (key_keep == 1)
    same_bucket = buckets.reshape(WINDOW, 1) == buckets.reshape(1, WINDOW)
    allowed = same_bucket & is_valid.reshape(1, WINDOW) | jnp.eye(WINDOW, dtype=bool)
    allowed = allowed.astype(jnp.float32)
    embedded = (token_rows + place_all.astype(jnp.float32)).reshape(win_count, WINDOW, D)
    hidden, embed_pull = jax.vjp(layer_norm, embedded, vectors[0], vectors[1])
    params = (
        attn_low[0],
        attn_low[1],
        attn_low[2],
        attn_low[3],
        ffn_low[0],
        ffn_low[1],
        up_biases[0],
        vectors[2:10],
    )
    hidden, stored, shared = layer_forward(hidden, params, allowed)
    picks = mask_pos.reshape(-1)
    head_in = select_rows(picks, hidden.reshape(WINDOW, D).astype(jnp.bfloat16))
    head_in = head_in.astype(jnp.bfloat16)
    head_pre = jnp.dot(head_in, head_weight, preferred_element_type=jnp.float32) + vectors[NV - 3]
    head_out, head_pull = jax.vjp(head_tail, head_pre, vectors[NV - 2], vectors[NV - 1])
    head_low = head_out.astype(jnp.bfloat16)

    rows_all = devices * MPW
    side = lax.axis_index("side").astype(jnp.int32)
    here = here16().astype(jnp.int32)
    order_rows = jnp.arange(devices, dtype=jnp.int32)
    rank_of_dev = (order_rows % 2 ^ side) * group + (order_rows // 2 ^ here)
    dev_of_rank = (order_rows % group ^ here) * 2 + (order_rows // group ^ side)
    head_all = gather_relative(head_low, wide_count, 1, lanes)
    head_all, *shared = lax.optimization_barrier((head_all, *shared))
    head_all = jnp.concatenate([head_all, exchange(head_all, side_bit)]).reshape(rows_all, D)
    labels_all = pick_rows(labels_all.reshape(devices, MPW), dev_of_rank).reshape(rows_all, 1)
    is_live = jnp.arange(MPW, dtype=jnp.int32)[None, :] < pick_rows(counts_all[:, None], dev_of_rank)
    word_ids = device * owned + jnp.arange(owned, dtype=jnp.int32)
    is_word = (word_ids < V)[None, :]
    logits = jnp.einsum("rd,vd->rv", head_all, table_low, preferred_element_type=jnp.float32)
    logits = jnp.where(is_word, logits + dec_bias[None, :], masked_fill)
    top_here = jnp.max(logits, axis=1)
    sum_here = jnp.sum(jnp.exp(logits - top_here[:, None]), axis=1)
    stats = jnp.concatenate(
        [
            top_here.reshape(devices, MPW),
            sum_here.reshape(devices, MPW),
            jnp.zeros((devices, 2 * lanes - 2 * MPW), jnp.float32),
        ],
        axis=1,
    )
    stats, source_here = lax.optimization_barrier((stats, source_here))
    stats = swap_all(pick_rows(stats, rank_of_dev))
    tops = stats[:, :MPW]
    top = jnp.max(tops, axis=0)
    total = top + jnp.log(jnp.sum(stats[:, MPW : 2 * MPW] * jnp.exp(tops - top[None]), axis=0))
    totals = spread(jnp.concatenate([total, source_total]), devices)
    totals = pick_rows(totals, dev_of_rank)
    row_facts = jnp.concatenate(
        [
            totals[:, :MPW].reshape(rows_all, 1),
            totals[:, MPW:].reshape(rows_all, 1),
            is_live.reshape(rows_all, 1).astype(jnp.float32),
            labels_all.astype(jnp.float32),
        ],
        axis=1,
    )
    place_facts = jnp.stack([device * owned, here, side]).astype(jnp.int32)
    grad_logits, losses, grad_dec = logit_grads(
        place_facts, logits, source_here, row_facts, devices
    )
    loss_part = jnp.sum(losses)
    give = jnp.dot(grad_logits[rows_all // 2 :], table_low, preferred_element_type=jnp.float32)
    got = exchange(give, side_bit)
    keep = jnp.dot(grad_logits[: rows_all // 2], table_low, preferred_element_type=jnp.float32)
    grad_head_out = reduce_rows((keep + got).reshape(group, MPW, D), wide_count)
    grad_words = jnp.einsum("rv,rd->vd", grad_logits, head_all, preferred_element_type=jnp.float32)
    grad_head_out, grad_words = lax.optimization_barrier((grad_head_out, grad_words))

    grad_pre, grad_head_gain, grad_head_shift = head_pull(grad_head_out)
    pre_low = grad_pre.astype(jnp.bfloat16)
    grad_head_w = jnp.einsum("rd,rf->df", head_in, pre_low, preferred_element_type=jnp.float32)
    grad_head_in = jnp.einsum("rf,df->rd", pre_low, head_weight, preferred_element_type=jnp.float32)
    grad_hidden = add_rows(picks, grad_head_in, WINDOW).reshape(win_count, WINDOW, D)
    grad_hidden, layer_mats, up_grad, vec_grads = layer_backward(
        grad_hidden, stored, shared, params, allowed
    )
    grad_embed, grad_emb_gain, grad_emb_shift = embed_pull(grad_hidden)
    flat_embed = grad_embed.reshape(WINDOW, D)

    ffn_parts, attn_parts = layer_mats[1], layer_mats[0]
    flat_embed, ffn_parts = tied(flat_embed, ffn_parts)
    dec_block = jnp.zeros((devices * owned,), jnp.float32)
    dec_block = lax.dynamic_update_slice(dec_block, grad_dec, (device * owned,))[:V]
    vector_block = jnp.concatenate(
        [jnp.stack([grad_emb_gain, grad_emb_shift])]
        + [vec_grads]
        + [jnp.stack([jnp.sum(pre_low.astype(jnp.float32), 0), grad_head_gain, grad_head_shift])],
        axis=0,
    )
    front = jnp.concatenate(
        [
            dec_block.reshape(-1, lanes),
            up_grad.reshape(2, devices // 2, ffn_width).transpose(1, 0, 2).reshape(-1, lanes),
            vector_block.reshape(-1, lanes),
        ]
    )
    other_part = scatter_flat(front, grad_head_w.reshape(-1, lanes), size, devices)

    place_grad = lax.psum(flat_embed, ("wide", "pair"))
    sent = add_rows(now, flat_embed, devices * slots)
    arrived = swap_all(sent.reshape(devices, slots, D))
    steps = len(routes(wide_count)[0])

    for step in range(steps):
        if step + 3 < steps:
            ffn_parts = reduce_step(ffn_parts, wide_count, step + 3)
        attn_parts, ffn_parts, (other_part,) = lockstep(
            reduce_step(attn_parts, wide_count, step),
            ffn_parts,
            [other_step(other_part, wide_count, step)],
        )
    place_grad, attn_parts = tied(place_grad, attn_parts)
    ffn_grad = jnp.concatenate(ffn_parts, axis=1)
    attn_grad = jnp.concatenate(attn_parts, axis=1)
    other_grad = own_share(other_part, size, device)
    place_grad = jnp.stack([place_grad, exchange(place_grad, side_bit)])
    place_ids = (jnp.arange(2, dtype=jnp.int32)[:, None] ^ side) * WINDOW + order[None, :]
    place_ids = (V - device * owned + place_ids).reshape(-1)
    table_grad = grad_words + add_rows(asked, arrived.reshape(-1, D), owned)
    table_grad = table_grad + add_rows(place_ids, place_grad.reshape(SEQ, D), owned)

    def more_grads(state):
        round_idx, grads = state
        addresses = address(round_idx)
        asked_rows = ask_again(addresses)
        sent = add_rows(addresses, flat_embed, devices * slots)
        arrived = swap_all(sent.reshape(devices, slots, D)).reshape(-1, D)
        return (round_idx + 1, grads + add_rows(asked_rows, arrived, owned))

    _, table_grad = lax.while_loop(
        lambda state: state[0] < rounds, more_grads, (jnp.int32(1), table_grad)
    )

    squares = square_sum((table_grad, attn_grad, ffn_grad, other_grad))
    sums = jnp.sum(spread(jnp.stack([squares, loss_part]), devices), axis=0)
    grad_norm = jnp.sqrt(sums[0]) / masked_total
    loss_value = sums[1] / masked_total
    factor = jnp.minimum(1.0, clip_limit / grad_norm)
    scaling = factor / masked_total

    attn_moment_new = mu_muon * attn_moment + attn_grad * scaling
    ffn_moment_new = mu_muon * ffn_moment + ffn_grad * scaling
    second = lax.axis_index("side") == 1
    keep = jnp.where(second, ffn_moment_new[1], ffn_moment_new[0])
    got = exchange(jnp.where(second, ffn_moment_new[0], ffn_moment_new[1]), side_bit)
    ffn_pair = jnp.concatenate([keep, got], axis=1)[None]
    attn_parts = gather_start(attn_moment_new[0].astype(jnp.bfloat16), 0, tile)
    ffn_parts = gather_start(ffn_pair[0].astype(jnp.bfloat16), 0, tile)
    steps = len(routes(wide_count)[0])
    for step in range(steps - 2):
        attn_parts, ffn_parts = lockstep(
            gather_step(attn_parts, wide_count, step, False),
            gather_step(ffn_parts, wide_count, step),
        )
    (attn_parts,) = lockstep(gather_step(attn_parts, wide_count, steps - 2, False))
    attn_gram = gram_of(gather_end(attn_parts, wide_count, 0, False))
    ffn_parts = gather_step(ffn_parts, wide_count, steps - 2)
    attn_gram, ffn_parts = tied(attn_gram, ffn_parts)
    ffn_found = gather_end(gather_step(ffn_parts, wide_count, steps - 1), wide_count, 0)
    attn_new = muon_cols(attn_mats, attn_moment_new, attn_gram, D)
    ffn_turn = newton_cols(ffn_pair, gram_of(ffn_found))[0]
    keep, give = ffn_turn[:, :ffn_width], ffn_turn[:, ffn_width:]
    got = exchange(give, side_bit)
    ffn_turn = jnp.stack([jnp.where(second, got, keep), jnp.where(second, keep, got)])
    ffn_new = ffn_mats - lr_muon * muon_shape * math.sqrt(max(D, FF)) * ffn_turn
    embed_new, embed_first_new, embed_second_new = adam_step(
        embed_table, embed_first, embed_second, table_grad * scaling
    )
    other_new, other_first_new, other_second_new = adam_step(
        other_params, other_first, other_second, other_grad * scaling
    )
    return (
        loss_value,
        grad_norm,
        embed_new,
        embed_first_new,
        embed_second_new,
        attn_new,
        attn_moment_new,
        ffn_new,
        ffn_moment_new,
        other_new,
        other_first_new,
        other_second_new,
    )


def solution(mesh):
    wide_count, narrow_count = mesh.shape["wide"], mesh.shape["narrow"]
    assert narrow_count % 2 == 0
    split = Mesh(
        np.asarray(mesh.devices).reshape(wide_count, narrow_count // 2, 2), everyone
    )
    rows, narrow = P(everyone), ("pair", "side")
    attn_spec, ffn_spec = P(narrow, None, "wide"), P(None, None, everyone)
    in_specs = (rows,) * 11 + (attn_spec,) * 2 + (ffn_spec,) * 2 + (rows,) * 3
    out_specs = (P(), P()) + (rows,) * 3 + (attn_spec,) * 2 + (ffn_spec,) * 2 + (rows,) * 3

    return jax.shard_map(
        shards, mesh=split, in_specs=in_specs, out_specs=out_specs, check_vma=False
    )
```
